32 devices in a mesh: dp: 4 (over y, core), seq: 8 (over z, x).
Axes of the slice: x: 2, y: 2, z: 4, core: 2. Of those that a mesh axis runs over, the one named last changes fastest.
Arguments:
- tokens: bfloat16 [4, 5120, 1024], P('dp', 'seq'), may hold values from -6 to 6
- cotangent: bfloat16 [4, 5120, 1024], P('dp', 'seq'), may hold values from -6 to 6
- seq_first: int32 [4, 8], P('dp', 'seq'), may hold values from 0 to 6, as said below
- decay_code: int32 [1024], replicated, may hold values from 5 to 17
- mixer_master: float32 [1024, 4096], P('dp'), may hold values from -0.09375 to 0.09375
- mixer_moment: float32 [1024, 4096], P('dp'), may hold values from -0.00018310547 to 0.00018310547
- mixer_square: float32 [1024, 4096], P('dp'), may hold values from 3.973643e-11 to 6.3578287e-10
- mlp_master: float32 [2, 1024, 4096], P(None, 'dp'), may hold values from -0.1875 to 0.1875
- mlp_moment: float32 [2, 1024, 4096], P(None, 'dp'), may hold values from -0.00018310547 to 0.00018310547
- mlp_square: float32 [2, 1024, 4096], P(None, 'dp'), may hold values from 3.973643e-11 to 6.3578287e-10
- channel_master: float32 [3, 4096], replicated, may hold values from 0.25 to 1.75
- channel_moment: float32 [3, 4096], replicated, may hold values from -0.00036621094 to 0.00036621094
- channel_square: float32 [3, 4096], replicated, may hold values from 7.947286e-11 to 1.2715657e-09
- filter_in_master: float32 [33, 64], replicated, may hold values from -3 to 3
- filter_in_moment: float32 [33, 64], replicated, may hold values from -0.00036621094 to 0.00036621094
- filter_in_square: float32 [33, 64], replicated, may hold values from 7.947286e-11 to 1.2715657e-09
- filter_out_master: float32 [64, 1024], replicated, may hold values from -0.75 to 0.75
- filter_out_moment: float32 [64, 1024], replicated, may hold values from -0.00036621094 to 0.00036621094
- filter_out_square: float32 [64, 1024], replicated, may hold values from 7.947286e-11 to 1.2715657e-09
Outputs:
- output: bfloat16 [4, 5120, 1024], P('dp', 'seq')
- tokens_grad: bfloat16 [4, 5120, 1024], P('dp', 'seq')
- grad_norm: float32 [1], replicated
- channel_grad: float32 [3, 4096], replicated
- filter_in_grad: float32 [33, 64], replicated
- filter_out_grad: float32 [64, 1024], replicated
- mixer_new: float32 [1024, 4096], P('dp')
- mixer_moment_new: float32 [1024, 4096], P('dp')
- mixer_square_new: float32 [1024, 4096], P('dp')
- mlp_new: float32 [2, 1024, 4096], P(None, 'dp')
- mlp_moment_new: float32 [2, 1024, 4096], P(None, 'dp')
- mlp_square_new: float32 [2, 1024, 4096], P(None, 'dp')
- channel_new: float32 [3, 4096], replicated
- channel_moment_new: float32 [3, 4096], replicated
- channel_square_new: float32 [3, 4096], replicated
- filter_in_new: float32 [33, 64], replicated
- filter_in_moment_new: float32 [33, 64], replicated
- filter_in_square_new: float32 [33, 64], replicated
- filter_out_new: float32 [64, 1024], replicated
- filter_out_moment_new: float32 [64, 1024], replicated
- filter_out_square_new: float32 [64, 1024], replicated
The draws below stay inside these ranges and needn't reach their ends.
Inputs may be any that keep to these rules, and one draw needn't show every extreme that they name: seq_first[g, b] is the first block of the sequence that holds block b of group g: each group is cut into sequences of consecutive whole blocks, exactly one of 4 blocks and all others of 2 blocks.
All inputs are finite; a program needn't handle non-finite values.
Results may differ from the reference program's by a relative error of at most 0.017.
Values may be sent and summed in bfloat16 or wider, within the bound.
A program may use at most 448 MiB of HBM per device.

```python
import math
import jax
import jax.numpy as jnp
from jax import lax

D = 1024
FF = 4096
FEAT = 33
FHID = 64
TOK_DEV = 640
SHORT_BLOCKS = 2
ADAM_STEP = 10
LONG_BLOCKS = 4
GROUP = 5120
FLEN = 2560
PARAMS = 12582912
N_DP = 4
N_SEQ = 8


def draw_seq_first(key, part):
    seq_count = 1 + (N_SEQ - LONG_BLOCKS) // SHORT_BLOCKS

    def one_group(group_key):
        long_place = jax.random.randint(group_key, (), 0, seq_count - 1)
        lengths = jnp.where(jnp.arange(seq_count) == long_place, LONG_BLOCKS, SHORT_BLOCKS).astype(jnp.int32)
        starts = (jnp.cumsum(lengths) - lengths).astype(jnp.int32)
        blocks = jnp.arange(N_SEQ, dtype=jnp.int32)
        chosen = jnp.where(starts[None, :] <= blocks[:, None], starts[None, :], 0)
        return jnp.max(chosen, axis=1).astype(jnp.int32)
    group_keys = jax.random.split(jax.random.fold_in(key, 7), N_DP)
    return jax.vmap(one_group)(group_keys)


def touch_ends(drawn, stream_key, least, high):
    place = [jax.random.randint(jax.random.fold_in(stream_key, axis), (), 0, length) for axis, length in enumerate(drawn.shape)]
    longest = drawn.shape.index(max(drawn.shape))
    beside = place[:longest] + [(place[longest] + 1) % drawn.shape[longest]] + place[longest + 1:]
    return drawn.at[tuple(place)].set(least).at[tuple(beside)].set(high)


def shard_levels(rng, shape, pieces, smallest, top_value):
    loudness, own = 1.0, jax.random.fold_in(rng, 6)
    for dim, blocks in pieces:
        steps = jnp.exp(jax.random.uniform(jax.random.fold_in(own, dim), (blocks,), jnp.float32, smallest / len(pieces), top_value / len(pieces)))
        loudness = loudness * jnp.repeat(steps, shape[dim] // blocks).reshape([-1 if axis == dim else 1 for axis in range(len(shape))])
    return loudness


def noise(own_key, extent, deviation, reach, cuts=(), kind=jnp.bfloat16):
    drawn = deviation * jax.random.normal(own_key, extent, jnp.float32)
    if cuts:
        drawn = drawn * shard_levels(own_key, extent, cuts, -0.22, 0.18)
    return jnp.clip(drawn, -reach, reach).astype(kind)


def setup_inputs(seed: int = 0) -> dict:
    streams_of = jax.random.split(jax.random.key(seed), 20)
    return {
        "tokens": noise(streams_of[0], (N_DP, GROUP, D), 1.0, 6.0, ((0, 4), (1, 8))),
        "cotangent": noise(streams_of[1], (N_DP, GROUP, D), 1.0, 6.0, ((0, 4), (1, 8))),
        "seq_first": draw_seq_first(jax.random.fold_in(streams_of[19], 71), 0),
        "decay_code": touch_ends(jax.random.randint(streams_of[3], (D,), 5, 18), jax.random.fold_in(streams_of[3], 1), 5, 17).astype(jnp.int32),
        "mixer_master": noise(streams_of[4], (D, 4 * D), (4 * D) ** -0.5, 0.09375, ((0, 4),), jnp.float32),
        "mixer_moment": noise(streams_of[5], (D, 4 * D), (0.11 * PARAMS ** -0.5), 0.00018310547, ((0, 4),), jnp.float32),
        "mixer_square": jnp.clip(jnp.exp(math.log(6.357828707947988e-10) - 2.7725887 * jax.random.uniform(streams_of[6], (D, 4 * D), jnp.float32) ** shard_levels(streams_of[6], (D, 4 * D), ((0, 4),), -0.2, 0.2)), 3.9736429424674924e-11, 6.357828707947988e-10),
        "mlp_master": noise(streams_of[7], (2, D, FF), D ** -0.5, 0.1875, ((1, 4),), jnp.float32),
        "mlp_moment": noise(streams_of[8], (2, D, FF), (0.11 * PARAMS ** -0.5), 0.00018310547, ((1, 4),), jnp.float32),
        "mlp_square": jnp.clip(jnp.exp(math.log(6.357828707947988e-10) - 2.7725887 * jax.random.uniform(streams_of[9], (2, D, FF), jnp.float32) ** shard_levels(streams_of[9], (2, D, FF), ((1, 4),), -0.2, 0.2)), 3.9736429424674924e-11, 6.357828707947988e-10),
        "channel_master": jnp.clip(1.0 + 0.15 * jax.random.normal(streams_of[10], (3, 4 * D), jnp.float32), 0.25, 1.75),
        "channel_moment": noise(streams_of[11], (3, 4 * D), (0.2 * PARAMS ** -0.5), 0.00036621094, (), jnp.float32),
        "channel_square": jnp.clip(jnp.exp(jax.random.uniform(streams_of[12], (3, 4 * D), jnp.float32, math.log(7.947285884934985e-11), math.log(1.2715657415895976e-09))), 7.947285884934985e-11, 1.2715657415895976e-09),
        "filter_in_master": noise(streams_of[13], (FEAT, FHID), (FEAT // 8) ** -0.5, 3.0, (), jnp.float32),
        "filter_in_moment": noise(streams_of[14], (FEAT, FHID), (0.2 * PARAMS ** -0.5), 0.00036621094, (), jnp.float32),
        "filter_in_square": jnp.clip(jnp.exp(jax.random.uniform(streams_of[15], (FEAT, FHID), jnp.float32, math.log(7.947285884934985e-11), math.log(1.2715657415895976e-09))), 7.947285884934985e-11, 1.2715657415895976e-09),
        "filter_out_master": noise(streams_of[16], (FHID, D), FHID ** -0.5, 0.75, (), jnp.float32),
        "filter_out_moment": noise(streams_of[17], (FHID, D), (0.2 * PARAMS ** -0.5), 0.00036621094, (), jnp.float32),
        "filter_out_square": jnp.clip(jnp.exp(jax.random.uniform(streams_of[18], (FHID, D), jnp.float32, math.log(7.947285884934985e-11), math.log(1.2715657415895976e-09))), 7.947285884934985e-11, 1.2715657415895976e-09),
    }


@jax.custom_vjp
def low(v):
    return lax.optimization_barrier(v.astype(jnp.bfloat16)).astype(jnp.float32)

@jax.custom_vjp
def low_back(v):
    return v

def low_keep(v):
    return (low(v), None)

def low_pass(kept, grad):
    return (grad,)

def back_keep(v):
    return (v, None)

def back_low(kept, grad):
    return (low(grad),)
low.defvjp(low_keep, low_pass)
low_back.defvjp(back_keep, back_low)
highest = lax.Precision.HIGHEST
norm_eps = 1e-05
clip_limit = 1.0
beta_one = 0.9
beta_two = 0.999
adam_eps = 1e-08
rate_matrix = 0.03
rate_small = 0.2
weight_decay = 0.1

def layer_norm(values, gain):
    center = lax.optimization_barrier(jnp.mean(values, axis=-1, keepdims=True))
    centred = values - center
    spread = lax.optimization_barrier(jnp.mean(centred * centred, axis=-1, keepdims=True))
    return centred * lax.rsqrt(spread + norm_eps) * gain

def filter_features(length, feature_count):
    places = jnp.arange(length, dtype=jnp.float32)[:, None]
    bands = jnp.arange(1, (feature_count - 1) // 2 + 1, dtype=jnp.float32)[None, :]
    angles = 2.0 * math.pi / length * places * bands
    return jnp.concatenate([places / length, jnp.cos(angles), jnp.sin(angles)], axis=1)

def make_filter(first_weight, last_weight, decay_code, length):
    features = filter_features(length, first_weight.shape[0])
    hidden = jnp.sin(jnp.dot(features, first_weight, precision=highest))
    raw_filter = jnp.dot(hidden, last_weight, precision=highest)
    rates = jnp.exp2(-decay_code.astype(jnp.float32))
    places = jnp.arange(length, dtype=jnp.float32)[:, None]
    shaped = raw_filter * jnp.exp(-places * rates[None, :])
    return shaped * lax.rsqrt(lax.optimization_barrier(jnp.sum(shaped * shaped, axis=0, keepdims=True)) + norm_eps)

def long_conv(conv_input, filt, firsts):
    total = conv_input.shape[0]
    window_len = 2 * total
    padded = jnp.concatenate([filt, jnp.zeros((total - filt.shape[0], filt.shape[1]), filt.dtype)], axis=0)
    filt_spec = jnp.fft.rfft(padded, n=window_len, axis=0)
    token_first = jnp.repeat(firsts, TOK_DEV)

    def one_start(totals, start_block):
        member = (token_first == start_block).astype(conv_input.dtype)[:, None]
        spectrum = jnp.fft.rfft(conv_input * member, n=window_len, axis=0)
        result = jnp.fft.irfft(spectrum * filt_spec, n=window_len, axis=0)[:total]
        return (totals + result * member, None)
    summed, _ = lax.scan(jax.checkpoint(one_start), jnp.zeros_like(conv_input), jnp.arange(N_SEQ, dtype=jnp.int32))
    return summed

def forward(inputs, mixer, mlp, channel, first_weight, last_weight, decay_code, seq_first):
    lane_count = 3 * D
    w_in = low(mixer[:, :lane_count])
    w_out = low(mixer[:, lane_count:])
    w_up = low(mlp[0])
    w_down = low(mlp[1])
    conv_taps = channel[:, :lane_count]
    gain_one = channel[0, lane_count:]
    gain_two = channel[1, lane_count:]
    skip_gain = channel[2, lane_count:]
    filt = make_filter(first_weight, last_weight, decay_code, FLEN)
    normed = low(layer_norm(inputs, gain_one))
    proj = low_back(low(jnp.einsum('gtd,de->gte', normed, w_in, precision=highest)))
    places = jnp.arange(GROUP, dtype=jnp.int32)[None, :] - TOK_DEV * jnp.repeat(seq_first, TOK_DEV, axis=1)
    one_back = jnp.pad(proj, ((0, 0), (1, 0), (0, 0)))[:, :GROUP] * (places >= 1).astype(proj.dtype)[:, :, None]
    two_back = jnp.pad(proj, ((0, 0), (2, 0), (0, 0)))[:, :GROUP] * (places >= 2).astype(proj.dtype)[:, :, None]
    short = low_back(conv_taps[0] * proj + conv_taps[1] * one_back + conv_taps[2] * two_back)
    v_part = short[..., :D]
    x_one = short[..., D:2 * D]
    x_zero = short[..., 2 * D:]
    conv_in = low(v_part * x_one)
    conv = low_back(jnp.stack([long_conv(conv_in[group], filt, seq_first[group]) for group in range(N_DP)]))
    mixed = conv + skip_gain * conv_in
    gated = low(x_zero * mixed)
    branch = low_back(jnp.einsum('gti,oi->gto', gated, w_out, precision=highest))
    resid = inputs + branch
    normed_two = low(layer_norm(resid, gain_two))
    up_proj = low_back(jnp.einsum('gtd,df->gtf', normed_two, w_up, precision=highest))
    act = low(jax.nn.gelu(up_proj))
    down = low_back(jnp.einsum('gtf,df->gtd', act, w_down, precision=highest))
    return resid + down

def adam_update(master, moment, square, grad, factor, rate, decay):
    clipped = grad * factor
    moment_new = beta_one * moment + (1.0 - beta_one) * clipped
    square_new = beta_two * square + (1.0 - beta_two) * clipped * clipped
    moment_hat = moment_new / (1.0 - beta_one ** ADAM_STEP)
    square_hat = square_new / (1.0 - beta_two ** ADAM_STEP)
    master_new = master - rate * (moment_hat / (jnp.sqrt(square_hat) + adam_eps) + decay * master)
    return (master_new, moment_new, square_new)

def reference(tokens, cotangent, seq_first, decay_code, mixer_master, mixer_moment, mixer_square, mlp_master, mlp_moment, mlp_square, channel_master, channel_moment, channel_square, filter_in_master, filter_in_moment, filter_in_square, filter_out_master, filter_out_moment, filter_out_square):

    def layer(inputs, mixer, mlp, channel, first_weight, last_weight):
        return forward(inputs, mixer, mlp, channel, first_weight, last_weight, decay_code, seq_first)
    output, pull = jax.vjp(layer, tokens.astype(jnp.float32), mixer_master, mlp_master, channel_master, filter_in_master, filter_out_master)
    tokens_grad, mixer_grad, mlp_grad, channel_grad, first_grad, last_grad = pull(cotangent.astype(jnp.float32))
    total = jnp.sum(mixer_grad * mixer_grad) + jnp.sum(mlp_grad * mlp_grad) + jnp.sum(channel_grad * channel_grad) + jnp.sum(first_grad * first_grad) + jnp.sum(last_grad * last_grad)
    grad_norm = jnp.sqrt(total)
    factor = jnp.minimum(1.0, clip_limit / (grad_norm + 1e-06))
    mixer_new, mixer_moment_new, mixer_square_new = adam_update(mixer_master, mixer_moment, mixer_square, mixer_grad, factor, rate_matrix, weight_decay)
    mlp_new, mlp_moment_new, mlp_square_new = adam_update(mlp_master, mlp_moment, mlp_square, mlp_grad, factor, rate_matrix, weight_decay)
    channel_new, channel_moment_new, channel_square_new = adam_update(channel_master, channel_moment, channel_square, channel_grad, factor, rate_small, 0.0)
    filter_in_new, filter_in_moment_new, filter_in_square_new = adam_update(filter_in_master, filter_in_moment, filter_in_square, first_grad, factor, rate_small, weight_decay)
    filter_out_new, filter_out_moment_new, filter_out_square_new = adam_update(filter_out_master, filter_out_moment, filter_out_square, last_grad, factor, rate_small, weight_decay)
    return (output.astype(jnp.bfloat16), tokens_grad.astype(jnp.bfloat16), grad_norm.reshape(1), channel_grad, first_grad, last_grad, mixer_new, mixer_moment_new, mixer_square_new, mlp_new, mlp_moment_new, mlp_square_new, channel_new, channel_moment_new, channel_square_new, filter_in_new, filter_in_moment_new, filter_in_square_new, filter_out_new, filter_out_moment_new, filter_out_square_new)
```

```python
import functools
import math

import jax
import jax.numpy as jnp
import numpy as np
from jax import lax
from jax.experimental import pallas as pl
from jax.experimental.pallas import tpu as pltpu
from jax.sharding import PartitionSpec as P

ADAM_STEP = 10


highest = lax.Precision.HIGHEST
norm_eps = 1e-05
clip_limit = 1.0
beta_one = 0.9
beta_two = 0.999
adam_eps = 1e-08
rate_matrix = 0.03
rate_small = 0.2
weight_decay = 0.1
PIECE = 128


def passed_along(value, axis, steps):
    count = lax.axis_size(axis)
    first, last = (max(0, -steps), min(count, count - steps))
    return lax.ppermute(value, axis, [(source, source + steps) for source in range(first, last)])


def layer_norm(values, gain):
    center = jnp.mean(values, axis=-1, keepdims=True)
    centred = values - center
    spread = jnp.mean(centred * centred, axis=-1, keepdims=True)
    return centred * lax.rsqrt(spread + norm_eps) * gain


def filter_features(length, feature_count):
    places = jnp.arange(length, dtype=jnp.float32)[:, None]
    bands = jnp.arange(1, (feature_count - 1) // 2 + 1, dtype=jnp.float32)[None, :]
    angles = 2.0 * math.pi / length * places * bands
    return jnp.concatenate([places / length, jnp.cos(angles), jnp.sin(angles)], axis=1)


def make_filter(first_weight, last_weight, decay_code, length):
    features = filter_features(length, first_weight.shape[0])
    hidden = jnp.sin(jnp.dot(features, first_weight, precision=highest))
    raw_filter = jnp.dot(hidden, last_weight, precision=highest)
    rates = jnp.exp2(-decay_code.astype(jnp.float32))
    places = jnp.arange(length, dtype=jnp.float32)[:, None]
    shaped = raw_filter * jnp.exp(-places * rates[None, :])
    return shaped * lax.rsqrt(jnp.sum(shaped * shaped, axis=0, keepdims=True) + norm_eps)


def odd_tables(parts):
    freq = np.arange(PIECE)[:, None] * 2 + 1
    sample = np.arange(PIECE)[None, :]
    angles = (freq * sample % (4 * PIECE)) * (2.0 * math.pi / (4 * PIECE))
    pair = np.stack([np.cos(angles), -np.sin(angles)]).reshape(2, parts, PIECE // parts, PIECE)
    table = pair.transpose(1, 0, 2, 3).reshape(parts, 2 * PIECE // parts, PIECE).astype(np.float32)
    upper = table.astype(jnp.bfloat16)
    lower = (table - upper.astype(np.float32)).astype(jnp.bfloat16)
    swap = (0, 2, 1)
    return tuple(jnp.asarray(v) for v in (upper, lower, upper.transpose(swap), lower.transpose(swap)))


def dot32(left, right):
    return jnp.dot(left, right, preferred_element_type=jnp.float32)


def split_two(value):
    upper = value.astype(jnp.bfloat16)
    return upper, (value - upper.astype(jnp.float32)).astype(jnp.bfloat16)


def dot_three(table_upper, table_lower, value):
    upper, lower = split_two(value)
    return dot32(table_upper, upper) + (dot32(table_lower, upper) + dot32(table_upper, lower))


def freq_signs(rows, width):
    places = lax.broadcasted_iota(jnp.int32, (rows, width), 0)
    return 1.0 - 2.0 * (places % 2).astype(jnp.float32)


def filter_spectrum(filt_ref, fwd_u, fwd_l, h_ref):
    half = fwd_u.shape[0] // 2
    signs = freq_signs(half, filt_ref.shape[1])
    prev = None
    for k in range(filt_ref.shape[0] // PIECE):
        spec = dot_three(fwd_u, fwd_l, filt_ref[k * PIECE : (k + 1) * PIECE, :])
        if prev is None:
            h_ref[k] = spec
        else:
            h_ref[k, :half] = spec[:half] - signs * prev[half:]
            h_ref[k, half:] = spec[half:] + signs * prev[:half]
        prev = spec


def emit(part, parts, out_ref, acc_ref, p, value):
    if parts == 1:
        out_ref[p] = value.astype(out_ref.dtype)
        return
    total = value if part == 0 else acc_ref[p] + value
    if part == parts - 1:
        out_ref[p] = total.astype(out_ref.dtype)
    else:
        acc_ref[p] = total


def conv_forward_kernel(per, first_ref, x_ref, filt_ref, fu_ref, fl_ref, iu_ref, il_ref, o_ref, xs, hs, *rest):
    count, _, lanes = x_ref.shape
    blocks = count // per
    parts = fu_ref.shape[0]
    half = PIECE // parts
    tiles = half // 8
    for part in range(parts):
        filter_spectrum(filt_ref, fu_ref[part], fl_ref[part], hs)

        def to_freq(p, carry):
            xs[p] = dot32(fu_ref[part], x_ref[p]) + dot32(fl_ref[part], x_ref[p])
            return carry

        lax.fori_loop(0, count, to_freq, 0)

        def one_tile(step, carry):
            b = blocks - 1 - step // tiles
            row = pl.multiple_of((step % tiles) * 8, 8)
            re = pl.ds(row, 8)
            im = pl.ds(row + half, 8)

            def add_pairs(acc, a, lag, diagonal):
                acc = list(acc)
                for j in range(per):
                    sr, si = xs[a * per + j, re], xs[a * per + j, im]
                    for i in range(j if diagonal else 0, per):
                        hr, hi = hs[lag + i - j, re], hs[lag + i - j, im]
                        acc[2 * i] = acc[2 * i] + (sr * hr - si * hi)
                        acc[2 * i + 1] = acc[2 * i + 1] + (sr * hi + si * hr)
                return tuple(acc)

            acc = tuple(jnp.zeros((8, lanes), jnp.float32) for _ in range(2 * per))
            acc = add_pairs(acc, b, 0, True)
            acc = lax.fori_loop(first_ref[b], b, lambda a, c: add_pairs(c, a, (b - a) * per, False), acc)
            for i in range(per):
                xs[b * per + i, re] = acc[2 * i]
                xs[b * per + i, im] = acc[2 * i + 1]
            return carry

        lax.fori_loop(0, blocks * tiles, one_tile, 0)

        def to_time(p, carry):
            value = dot_three(iu_ref[part], il_ref[part], xs[p] * (1.0 / PIECE))
            emit(part, parts, o_ref, rest[0] if rest else None, p, value)
            return carry

        lax.fori_loop(0, count, to_time, 0)


def conv_backward_kernel(
    per, first_ref, last_ref, x_ref, g_ref, filt_ref, fu_ref, fl_ref, iu_ref, il_ref, dx_ref, df_ref, xs, gs, hs, dh, *rest
):
    count, _, lanes = x_ref.shape
    blocks = count // per
    taps = filt_ref.shape[0] // PIECE
    parts = fu_ref.shape[0]
    half = PIECE // parts
    tiles = half // 8
    for part in range(parts):
        filter_spectrum(filt_ref, fu_ref[part], fl_ref[part], hs)

        def to_freq(p, carry):
            xs[p] = dot32(fu_ref[part], x_ref[p]) + dot32(fl_ref[part], x_ref[p])
            gs[p] = (dot32(fu_ref[part], g_ref[p]) + dot32(fl_ref[part], g_ref[p])) * (1.0 / PIECE)
            return carry

        lax.fori_loop(0, count, to_freq, 0)
        dh[...] = jnp.zeros_like(dh)

        def one_tile(step, carry):
            a = step // tiles
            row = pl.multiple_of((step % tiles) * 8, 8)
            re = pl.ds(row, 8)
            im = pl.ds(row + half, 8)

            def add_pairs(acc, b, lag, diagonal):
                acc = list(acc)
                for delta in range(0 if diagonal else 1 - per, per):
                    hr, hi = hs[lag + delta, re], hs[lag + delta, im]
                    tr, ti = dh[lag + delta, re], dh[lag + delta, im]
                    for j in range(max(0, -delta), per - max(0, delta)):
                        sr, si = xs[a * per + j, re], xs[a * per + j, im]
                        gr, gi = gs[b * per + j + delta, re], gs[b * per + j + delta, im]
                        acc[2 * j] = acc[2 * j] + (hr * gr + hi * gi)
                        acc[2 * j + 1] = acc[2 * j + 1] + (hr * gi - hi * gr)
                        tr = tr + (sr * gr + si * gi)
                        ti = ti + (sr * gi - si * gr)
                    dh[lag + delta, re] = tr
                    dh[lag + delta, im] = ti
                return tuple(acc)

            acc = tuple(jnp.zeros((8, lanes), jnp.float32) for _ in range(2 * per))
            acc = add_pairs(acc, a, 0, True)
            acc = lax.fori_loop(a + 1, last_ref[a] + 1, lambda b, c: add_pairs(c, b, (b - a) * per, False), acc)
            for j in range(per):
                xs[a * per + j, re] = acc[2 * j]
                xs[a * per + j, im] = acc[2 * j + 1]
            return carry

        lax.fori_loop(0, blocks * tiles, one_tile, 0)

        def to_time(p, carry):
            value = dot_three(iu_ref[part], il_ref[part], xs[p])
            emit(part, parts, dx_ref, rest[0] if rest else None, p, value)
            return carry

        lax.fori_loop(0, count, to_time, 0)
        signs = freq_signs(half, lanes)
        for k in range(taps):
            grad = dh[k]
            if k + 1 < taps:
                grad = grad + jnp.concatenate([signs * dh[k + 1, half:], -signs * dh[k + 1, :half]], axis=0)
            value = dot_three(iu_ref[part], il_ref[part], grad)
            rows = slice(k * PIECE, (k + 1) * PIECE)
            df_ref[rows, :] = value if part == 0 else df_ref[rows, :] + value


VMEM_SPEC = pl.BlockSpec(memory_space=pltpu.VMEM)
SMEM_SPEC = pl.BlockSpec(memory_space=pltpu.SMEM)


def conv_parts(count):
    return 1 if count <= 64 else 4


def conv_forward(firsts, pieces, filt, per):
    count, _, lanes = pieces.shape
    taps = filt.shape[0] // PIECE
    parts = conv_parts(count)
    spec = (2 * PIECE // parts, lanes)
    scratch = [pltpu.VMEM((count,) + spec, jnp.float32), pltpu.VMEM((taps,) + spec, jnp.float32)]
    if parts > 1:
        scratch.append(pltpu.VMEM(pieces.shape, jnp.float32))
    return pl.pallas_call(
        functools.partial(conv_forward_kernel, per),
        out_shape=jax.ShapeDtypeStruct(pieces.shape, jnp.bfloat16),
        in_specs=[SMEM_SPEC] + [VMEM_SPEC] * 6,
        out_specs=VMEM_SPEC,
        scratch_shapes=scratch,
        compiler_params=pltpu.CompilerParams(vmem_limit_bytes=56 * 2**20),
        cost_estimate=pl.CostEstimate(flops=2 * 10**9, bytes_accessed=8 * 10**6, transcendentals=0),
        name="long_conv",
    )(firsts, pieces, filt, *odd_tables(parts))


def conv_backward(firsts, lasts, pieces, grads, filt, per):
    count, _, lanes = pieces.shape
    taps = filt.shape[0] // PIECE
    parts = conv_parts(count)
    spec = (2 * PIECE // parts, lanes)
    scratch = [pltpu.VMEM((n,) + spec, jnp.float32) for n in (count, count, taps, taps)]
    if parts > 1:
        scratch.append(pltpu.VMEM(pieces.shape, jnp.float32))
    return pl.pallas_call(
        functools.partial(conv_backward_kernel, per),
        out_shape=(
            jax.ShapeDtypeStruct(pieces.shape, jnp.bfloat16),
            jax.ShapeDtypeStruct(filt.shape, jnp.float32),
        ),
        in_specs=[SMEM_SPEC] * 2 + [VMEM_SPEC] * 7,
        out_specs=(VMEM_SPEC, VMEM_SPEC),
        scratch_shapes=scratch,
        compiler_params=pltpu.CompilerParams(vmem_limit_bytes=56 * 2**20),
        cost_estimate=pl.CostEstimate(flops=4 * 10**9, bytes_accessed=10**7, transcendentals=0),
        name="long_conv_back",
    )(firsts, lasts, pieces, grads, filt, *odd_tables(parts))


def to_channels(value, count):
    rows, width = value.shape
    tiles = value.reshape(rows, count, width // count).transpose(1, 0, 2)
    return lax.all_to_all(tiles, "seq", 0, 0, tiled=True)


def to_tokens(value):
    count, rows, width = value.shape
    tiles = lax.all_to_all(value, "seq", 0, 0, tiled=True)
    return tiles.transpose(1, 0, 2).reshape(rows, count * width)


def short_conv(extended, conv_taps):
    token_count = extended.shape[0] - 2
    return (
        conv_taps[0] * extended[2:]
        + conv_taps[1] * extended[1 : token_count + 1]
        + conv_taps[2] * extended[:token_count]
    )


def contract_rows(left, right):
    return lax.dot_general(
        left, right, (((0,), (0,)), ((), ())), preferred_element_type=jnp.float32
    )


def contract_cols(left, right):
    return lax.dot_general(
        left, right, (((1,), (1,)), ((), ())), preferred_element_type=jnp.float32
    )


def adam_update(master, moment, square, grad, factor, rate, decay):
    clipped = grad * factor
    moment_new = beta_one * moment + (1.0 - beta_one) * clipped
    square_new = beta_two * square + (1.0 - beta_two) * clipped * clipped
    moment_hat = moment_new / (1.0 - beta_one**ADAM_STEP)
    square_hat = square_new / (1.0 - beta_two**ADAM_STEP)
    master_new = master - rate * (moment_hat / (jnp.sqrt(square_hat) + adam_eps) + decay * master)
    return (master_new, moment_new, square_new)


def summed_rows(grad_b, axis):
    own = lax.psum_scatter(grad_b, "dp", scatter_dimension=axis, tiled=True)
    part = lax.psum_scatter(own, "seq", scatter_dimension=axis, tiled=True)
    return lax.all_gather(part, "seq", axis=axis, tiled=True)


def on_device(
    tokens,
    cotangent,
    seq_first,
    decay_code,
    mixer_master,
    mixer_moment,
    mixer_square,
    mlp_master,
    mlp_moment,
    mlp_square,
    channel_master,
    channel_moment,
    channel_square,
    filter_in_master,
    filter_in_moment,
    filter_in_square,
    filter_out_master,
    filter_out_moment,
    filter_out_square,
):
    block_rows = tokens.shape[1]
    model_width = tokens.shape[2]
    lane_count = 3 * model_width
    per = block_rows // PIECE
    seq_count = lax.axis_size("seq")
    long_blocks = max(seq_count // 4, 4)
    length = long_blocks * block_rows
    own_width = model_width // seq_count
    seq_index = lax.axis_index("seq")
    own_first = seq_first[0, 0]
    has_prev = seq_index - own_first >= 1
    w_in = lax.all_gather(mixer_master[:, :lane_count].astype(jnp.bfloat16), "dp", axis=0, tiled=True)
    firsts = lax.all_gather(seq_first[0], "seq", axis=0, tiled=True)
    w_out = lax.all_gather(mixer_master[:, lane_count:].astype(jnp.bfloat16), "dp", axis=0, tiled=True)
    mlp_full = lax.all_gather(mlp_master.astype(jnp.bfloat16), "dp", axis=1, tiled=True)
    w_up = mlp_full[0]
    w_down = mlp_full[1]
    blocks = jnp.arange(seq_count, dtype=jnp.int32)
    lasts = jnp.max(
        jnp.where(firsts[None, :] == firsts[:, None], blocks[None, :], 0), axis=1
    ).astype(jnp.int32)
    conv_taps = channel_master[:, :lane_count]
    gain_one = channel_master[0, lane_count:]
    gain_two = channel_master[1, lane_count:]
    skip_gain = channel_master[2, lane_count:]
    own_codes = lax.dynamic_slice_in_dim(decay_code, seq_index * own_width, own_width, 0)
    own_last = lax.dynamic_slice_in_dim(filter_out_master, seq_index * own_width, own_width, 1)
    filt, filter_pull = jax.vjp(
        lambda first, last: make_filter(first, last, own_codes, length), filter_in_master, own_last
    )
    inputs = tokens[0].astype(jnp.float32)
    normed_b = layer_norm(inputs, gain_one).astype(jnp.bfloat16)
    proj_b = jnp.dot(normed_b, w_in, preferred_element_type=jnp.float32).astype(jnp.bfloat16)
    previous = passed_along(proj_b[block_rows - 2 :], "seq", 1)
    previous = jnp.where(has_prev, previous, jnp.zeros_like(previous))
    extended = jnp.concatenate([previous, proj_b], axis=0).astype(jnp.float32)
    short, short_pull = jax.vjp(short_conv, extended, conv_taps)
    v_part = short[:, :model_width]
    x_one = short[:, model_width : 2 * model_width]
    x_zero = short[:, 2 * model_width :]
    conv_input = (v_part * x_one).astype(jnp.bfloat16)
    conv_in_f = conv_input.astype(jnp.float32)
    pieces = to_channels(conv_input, seq_count).reshape(seq_count * per, PIECE, own_width)
    conv_out = conv_forward(firsts, pieces, filt, per)
    conv = to_tokens(conv_out.reshape(seq_count, block_rows, own_width)).astype(jnp.float32)
    mixed = conv + skip_gain * conv_in_f
    gated_b = (x_zero * mixed).astype(jnp.bfloat16)
    branch = contract_cols(gated_b, w_out)
    resid = inputs + branch
    normed_two, norm_two_pull = jax.vjp(layer_norm, resid, gain_two)
    normed_two_b = normed_two.astype(jnp.bfloat16)
    up_proj = jnp.dot(normed_two_b, w_up, preferred_element_type=jnp.float32)
    act_f, gelu_pull = jax.vjp(jax.nn.gelu, up_proj)
    act_b = act_f.astype(jnp.bfloat16)
    down = contract_cols(act_b, w_down)
    output = resid + down
    grad_down_b = cotangent[0]
    grad_out = grad_down_b.astype(jnp.float32)
    d_act = jnp.dot(grad_down_b, w_down, preferred_element_type=jnp.float32)
    grad_up_b = gelu_pull(d_act)[0].astype(jnp.bfloat16)
    d_normed_two = contract_cols(grad_up_b, w_up)
    resid_part, d_gain_two = norm_two_pull(d_normed_two)
    d_resid = grad_out + resid_part
    grad_branch_b = d_resid.astype(jnp.bfloat16)
    d_gated = jnp.dot(grad_branch_b, w_out, preferred_element_type=jnp.float32)
    d_x_zero = d_gated * mixed
    d_mixed = d_gated * x_zero
    conv_grad = d_mixed.astype(jnp.bfloat16)
    d_skip = jnp.sum(d_mixed * conv_in_f, axis=0)
    up_grad_b = contract_rows(normed_two_b, grad_up_b).astype(jnp.bfloat16)
    down_grad_b = contract_rows(grad_down_b, act_b).astype(jnp.bfloat16)
    out_grad_b = contract_rows(grad_branch_b, gated_b).astype(jnp.bfloat16)
    up_grad = summed_rows(up_grad_b, 0).astype(jnp.float32)
    down_grad = summed_rows(down_grad_b, 0).astype(jnp.float32)
    grad_pieces = to_channels(conv_grad, seq_count).reshape(seq_count * per, PIECE, own_width)
    conv_in_grad, filt_grad = conv_backward(firsts, lasts, pieces, grad_pieces, filt, per)
    back = to_tokens(conv_in_grad.reshape(seq_count, block_rows, own_width)).astype(jnp.float32)
    d_conv_in = skip_gain * d_mixed + back
    first_grad, own_last_grad = filter_pull(filt_grad)
    last_grad = lax.dynamic_update_slice_in_dim(
        jnp.zeros_like(filter_out_master), own_last_grad, seq_index * own_width, 1
    )
    grad_short_b = jnp.concatenate(
        [d_conv_in * x_one, d_conv_in * v_part, d_x_zero], axis=1
    ).astype(jnp.bfloat16)
    d_extended, d_taps = short_pull(grad_short_b.astype(jnp.float32))
    sent_rows = jnp.where(has_prev, grad_short_b[:2], jnp.zeros_like(grad_short_b[:2]))
    later_rows = passed_along(sent_rows, "seq", -1).astype(jnp.float32)
    tail_rows = jnp.stack(
        [conv_taps[2] * later_rows[0], conv_taps[1] * later_rows[0] + conv_taps[2] * later_rows[1]]
    )
    d_proj = d_extended[2:].at[block_rows - 2 :].add(tail_rows)
    grad_proj_b = d_proj.astype(jnp.bfloat16)
    d_normed = contract_cols(grad_proj_b, w_in)
    _, norm_one_pull = jax.vjp(layer_norm, inputs, gain_one)
    input_part, d_gain_one = norm_one_pull(d_normed)
    tokens_grad = d_resid + input_part
    in_grad_b = contract_rows(normed_b, grad_proj_b).astype(jnp.bfloat16)
    mixer_grad = summed_rows(jnp.concatenate([in_grad_b, out_grad_b], axis=1), 0).astype(jnp.float32)
    mlp_grad = jnp.stack([up_grad, down_grad])
    vectors = jnp.stack([d_gain_one, d_gain_two, d_skip])
    channel_grad = jnp.concatenate([d_taps, vectors], axis=1)
    squares = (jnp.sum(mixer_grad * mixer_grad) + jnp.sum(mlp_grad * mlp_grad)) * (1.0 / seq_count)
    channel_grad, first_grad, last_grad, squares = lax.psum(
        (channel_grad, first_grad, last_grad, squares), ("dp", "seq")
    )
    total = (
        squares
        + jnp.sum(channel_grad * channel_grad)
        + jnp.sum(first_grad * first_grad)
        + jnp.sum(last_grad * last_grad)
    )
    grad_norm = jnp.sqrt(total)
    factor = jnp.minimum(1.0, clip_limit / (grad_norm + 1e-06))
    mixer_new, mixer_moment_new, mixer_square_new = adam_update(
        mixer_master, mixer_moment, mixer_square, mixer_grad, factor, rate_matrix, weight_decay
    )
    mlp_new, mlp_moment_new, mlp_square_new = adam_update(
        mlp_master, mlp_moment, mlp_square, mlp_grad, factor, rate_matrix, weight_decay
    )
    channel_new, channel_moment_new, channel_square_new = adam_update(
        channel_master, channel_moment, channel_square, channel_grad, factor, rate_small, 0.0
    )
    filter_in_new, filter_in_moment_new, filter_in_square_new = adam_update(
        filter_in_master,
        filter_in_moment,
        filter_in_square,
        first_grad,
        factor,
        rate_small,
        weight_decay,
    )
    filter_out_new, filter_out_moment_new, filter_out_square_new = adam_update(
        filter_out_master,
        filter_out_moment,
        filter_out_square,
        last_grad,
        factor,
        rate_small,
        weight_decay,
    )
    return (
        output.astype(jnp.bfloat16)[None],
        tokens_grad.astype(jnp.bfloat16)[None],
        grad_norm.reshape(1),
        channel_grad,
        first_grad,
        last_grad,
        mixer_new,
        mixer_moment_new,
        mixer_square_new,
        mlp_new,
        mlp_moment_new,
        mlp_square_new,
        channel_new,
        channel_moment_new,
        channel_square_new,
        filter_in_new,
        filter_in_moment_new,
        filter_in_square_new,
        filter_out_new,
        filter_out_moment_new,
        filter_out_square_new,
    )


def solution(mesh):
    in_specs = (
        P("dp", "seq", None),
        P("dp", "seq", None),
        P("dp", "seq"),
        P(),
        P("dp", None),
        P("dp", None),
        P("dp", None),
        P(None, "dp", None),
        P(None, "dp", None),
        P(None, "dp", None),
        P(),
        P(),
        P(),
        P(),
        P(),
        P(),
        P(),
        P(),
        P(),
    )
    out_specs = (
        P("dp", "seq", None),
        P("dp", "seq", None),
        P(),
        P(),
        P(),
        P(),
        P("dp", None),
        P("dp", None),
        P("dp", None),
        P(None, "dp", None),
        P(None, "dp", None),
        P(None, "dp", None),
        P(),
        P(),
        P(),
        P(),
        P(),
        P(),
        P(),
        P(),
        P(),
    )
    return jax.shard_map(
        on_device, mesh=mesh, in_specs=in_specs, out_specs=out_specs, check_vma=False
    )
```

```python
import functools
import math

import jax
import jax.numpy as jnp
import numpy as np
from jax import lax
from jax.experimental import pallas as pl
from jax.experimental.pallas import tpu as pltpu
from jax.sharding import PartitionSpec as P

ADAM_STEP = 10


highest = lax.Precision.HIGHEST
norm_eps = 1e-05
clip_limit = 1.0
beta_one = 0.9
beta_two = 0.999
adam_eps = 1e-08
rate_matrix = 0.03
rate_small = 0.2
weight_decay = 0.1
PIECE = 128


def passed_along(value, axis, steps):
    count = lax.axis_size(axis)
    first, last = (max(0, -steps), min(count, count - steps))
    return lax.ppermute(value, axis, [(source, source + steps) for source in range(first, last)])


def layer_norm(values, gain):
    center = jnp.mean(values, axis=-1, keepdims=True)
    centred = values - center
    spread = jnp.mean(centred * centred, axis=-1, keepdims=True)
    return centred * lax.rsqrt(spread + norm_eps) * gain


def filter_features(length, feature_count):
    places = jnp.arange(length, dtype=jnp.float32)[:, None]
    bands = jnp.arange(1, (feature_count - 1) // 2 + 1, dtype=jnp.float32)[None, :]
    angles = 2.0 * math.pi / length * places * bands
    return jnp.concatenate([places / length, jnp.cos(angles), jnp.sin(angles)], axis=1)


def make_filter(first_weight, last_weight, decay_code, length):
    features = filter_features(length, first_weight.shape[0])
    hidden = jnp.sin(jnp.dot(features, first_weight, precision=highest))
    raw_filter = jnp.dot(hidden, last_weight, precision=highest)
    rates = jnp.exp2(-decay_code.astype(jnp.float32))
    places = jnp.arange(length, dtype=jnp.float32)[:, None]
    shaped = raw_filter * jnp.exp(-places * rates[None, :])
    return shaped * lax.rsqrt(jnp.sum(shaped * shaped, axis=0, keepdims=True) + norm_eps)


def odd_tables(parts):
    freq = np.arange(PIECE)[:, None] * 2 + 1
    sample = np.arange(PIECE)[None, :]
    angles = (freq * sample % (4 * PIECE)) * (2.0 * math.pi / (4 * PIECE))
    pair = np.stack([np.cos(angles), -np.sin(angles)]).reshape(2, parts, PIECE // parts, PIECE)
    table = pair.transpose(1, 0, 2, 3).reshape(parts, 2 * PIECE // parts, PIECE).astype(np.float32)
    upper = table.astype(jnp.bfloat16)
    lower = (table - upper.astype(np.float32)).astype(jnp.bfloat16)
    swap = (0, 2, 1)
    return tuple(jnp.asarray(v) for v in (upper, lower, upper.transpose(swap), lower.transpose(swap)))


def dot32(left, right):
    return jnp.dot(left, right, preferred_element_type=jnp.float32)


def split_two(value):
    upper = value.astype(jnp.bfloat16)
    return upper, (value - upper.astype(jnp.float32)).astype(jnp.bfloat16)


def dot_three(table_upper, table_lower, value):
    upper, lower = split_two(value)
    return dot32(table_upper, upper) + (dot32(table_lower, upper) + dot32(table_upper, lower))


def freq_signs(rows, width):
    places = lax.broadcasted_iota(jnp.int32, (rows, width), 0)
    return 1.0 - 2.0 * (places % 2).astype(jnp.float32)


def filter_spectrum(filt_ref, fwd_u, fwd_l, h_ref):
    half = fwd_u.shape[0] // 2
    signs = freq_signs(half, filt_ref.shape[1])
    prev = None
    for k in range(filt_ref.shape[0] // PIECE):
        spec = dot_three(fwd_u, fwd_l, filt_ref[k * PIECE : (k + 1) * PIECE, :])
        if prev is None:
            h_ref[k] = spec
        else:
            h_ref[k, :half] = spec[:half] - signs * prev[half:]
            h_ref[k, half:] = spec[half:] + signs * prev[:half]
        prev = spec


def emit(part, parts, out_ref, acc_ref, p, value):
    if parts == 1:
        out_ref[p] = value.astype(out_ref.dtype)
        return
    total = value if part == 0 else acc_ref[p] + value
    if part == parts - 1:
        out_ref[p] = total.astype(out_ref.dtype)
    else:
        acc_ref[p] = total


def conv_forward_kernel(per, first_ref, x_ref, filt_ref, fu_ref, fl_ref, iu_ref, il_ref, o_ref, xs, hs, *rest):
    count, _, lanes = x_ref.shape
    blocks = count // per
    parts = fu_ref.shape[0]
    half = PIECE // parts
    tiles = half // 8
    for part in range(parts):
        filter_spectrum(filt_ref, fu_ref[part], fl_ref[part], hs)

        def to_freq(p, carry):
            xs[p] = dot32(fu_ref[part], x_ref[p]) + dot32(fl_ref[part], x_ref[p])
            return carry

        lax.fori_loop(0, count, to_freq, 0)

        def one_tile(step, carry):
            b = blocks - 1 - step // tiles
            row = pl.multiple_of((step % tiles) * 8, 8)
            re = pl.ds(row, 8)
            im = pl.ds(row + half, 8)

            def add_pairs(acc, a, lag, diagonal):
                acc = list(acc)
                for j in range(per):
                    sr, si = xs[a * per + j, re], xs[a * per + j, im]
                    for i in range(j if diagonal else 0, per):
                        hr, hi = hs[lag + i - j, re], hs[lag + i - j, im]
                        acc[2 * i] = acc[2 * i] + (sr * hr - si * hi)
                        acc[2 * i + 1] = acc[2 * i + 1] + (sr * hi + si * hr)
                return tuple(acc)

            acc = tuple(jnp.zeros((8, lanes), jnp.float32) for _ in range(2 * per))
            acc = add_pairs(acc, b, 0, True)
            acc = lax.fori_loop(first_ref[b], b, lambda a, c: add_pairs(c, a, (b - a) * per, False), acc)
            for i in range(per):
                xs[b * per + i, re] = acc[2 * i]
                xs[b * per + i, im] = acc[2 * i + 1]
            return carry

        lax.fori_loop(0, blocks * tiles, one_tile, 0)

        def to_time(p, carry):
            value = dot_three(iu_ref[part], il_ref[part], xs[p] * (1.0 / PIECE))
            emit(part, parts, o_ref, rest[0] if rest else None, p, value)
            return carry

        lax.fori_loop(0, count, to_time, 0)


def conv_backward_kernel(
    per, first_ref, last_ref, x_ref, g_ref, filt_ref, fu_ref, fl_ref, iu_ref, il_ref, dx_ref, df_ref, xs, gs, hs, dh, *rest
):
    count, _, lanes = x_ref.shape
    blocks = count // per
    taps = filt_ref.shape[0] // PIECE
    parts = fu_ref.shape[0]
    half = PIECE // parts
    tiles = half // 8
    for part in range(parts):
        filter_spectrum(filt_ref, fu_ref[part], fl_ref[part], hs)

        def to_freq(p, carry):
            xs[p] = dot32(fu_ref[part], x_ref[p]) + dot32(fl_ref[part], x_ref[p])
            gs[p] = (dot32(fu_ref[part], g_ref[p]) + dot32(fl_ref[part], g_ref[p])) * (1.0 / PIECE)
            return carry

        lax.fori_loop(0, count, to_freq, 0)
        dh[...] = jnp.zeros_like(dh)

        def one_tile(step, carry):
            a = step // tiles
            row = pl.multiple_of((step % tiles) * 8, 8)
            re = pl.ds(row, 8)
            im = pl.ds(row + half, 8)

            def add_pairs(acc, b, lag, diagonal):
                acc = list(acc)
                for delta in range(0 if diagonal else 1 - per, per):
                    hr, hi = hs[lag + delta, re], hs[lag + delta, im]
                    tr, ti = dh[lag + delta, re], dh[lag + delta, im]
                    for j in range(max(0, -delta), per - max(0, delta)):
                        sr, si = xs[a * per + j, re], xs[a * per + j, im]
                        gr, gi = gs[b * per + j + delta, re], gs[b * per + j + delta, im]
                        acc[2 * j] = acc[2 * j] + (hr * gr + hi * gi)
                        acc[2 * j + 1] = acc[2 * j + 1] + (hr * gi - hi * gr)
                        tr = tr + (sr * gr + si * gi)
                        ti = ti + (sr * gi - si * gr)
                    dh[lag + delta, re] = tr
                    dh[lag + delta, im] = ti
                return tuple(acc)

            acc = tuple(jnp.zeros((8, lanes), jnp.float32) for _ in range(2 * per))
            acc = add_pairs(acc, a, 0, True)
            acc = lax.fori_loop(a + 1, last_ref[a] + 1, lambda b, c: add_pairs(c, b, (b - a) * per, False), acc)
            for j in range(per):
                xs[a * per + j, re] = acc[2 * j]
                xs[a * per + j, im] = acc[2 * j + 1]
            return carry

        lax.fori_loop(0, blocks * tiles, one_tile, 0)

        def to_time(p, carry):
            value = dot_three(iu_ref[part], il_ref[part], xs[p])
            emit(part, parts, dx_ref, rest[0] if rest else None, p, value)
            return carry

        lax.fori_loop(0, count, to_time, 0)
        signs = freq_signs(half, lanes)
        for k in range(taps):
            grad = dh[k]
            if k + 1 < taps:
                grad = grad + jnp.concatenate([signs * dh[k + 1, half:], -signs * dh[k + 1, :half]], axis=0)
            value = dot_three(iu_ref[part], il_ref[part], grad)
            rows = slice(k * PIECE, (k + 1) * PIECE)
            df_ref[rows, :] = value if part == 0 else df_ref[rows, :] + value


VMEM_SPEC = pl.BlockSpec(memory_space=pltpu.VMEM)
SMEM_SPEC = pl.BlockSpec(memory_space=pltpu.SMEM)


def conv_parts(count):
    return 1 if count <= 64 else 4


def conv_forward(firsts, pieces, filt, per):
    count, _, lanes = pieces.shape
    taps = filt.shape[0] // PIECE
    parts = conv_parts(count)
    spec = (2 * PIECE // parts, lanes)
    scratch = [pltpu.VMEM((count,) + spec, jnp.float32), pltpu.VMEM((taps,) + spec, jnp.float32)]
    if parts > 1:
        scratch.append(pltpu.VMEM(pieces.shape, jnp.float32))
    return pl.pallas_call(
        functools.partial(conv_forward_kernel, per),
        out_shape=jax.ShapeDtypeStruct(pieces.shape, jnp.bfloat16),
        in_specs=[SMEM_SPEC] + [VMEM_SPEC] * 6,
        out_specs=VMEM_SPEC,
        scratch_shapes=scratch,
        compiler_params=pltpu.CompilerParams(vmem_limit_bytes=56 * 2**20),
        cost_estimate=pl.CostEstimate(flops=2 * 10**9, bytes_accessed=8 * 10**6, transcendentals=0),
        name="long_conv",
    )(firsts, pieces, filt, *odd_tables(parts))


def conv_backward(firsts, lasts, pieces, grads, filt, per):
    count, _, lanes = pieces.shape
    taps = filt.shape[0] // PIECE
    parts = conv_parts(count)
    spec = (2 * PIECE // parts, lanes)
    scratch = [pltpu.VMEM((n,) + spec, jnp.float32) for n in (count, count, taps, taps)]
    if parts > 1:
        scratch.append(pltpu.VMEM(pieces.shape, jnp.float32))
    return pl.pallas_call(
        functools.partial(conv_backward_kernel, per),
        out_shape=(
            jax.ShapeDtypeStruct(pieces.shape, jnp.bfloat16),
            jax.ShapeDtypeStruct(filt.shape, jnp.float32),
        ),
        in_specs=[SMEM_SPEC] * 2 + [VMEM_SPEC] * 7,
        out_specs=(VMEM_SPEC, VMEM_SPEC),
        scratch_shapes=scratch,
        compiler_params=pltpu.CompilerParams(vmem_limit_bytes=56 * 2**20),
        cost_estimate=pl.CostEstimate(flops=4 * 10**9, bytes_accessed=10**7, transcendentals=0),
        name="long_conv_back",
    )(firsts, lasts, pieces, grads, filt, *odd_tables(parts))


def to_channels(value, count):
    rows, width = value.shape
    tiles = value.reshape(rows, count, width // count).transpose(1, 0, 2)
    return lax.all_to_all(tiles, "seq", 0, 0, tiled=True)


def to_tokens(value):
    count, rows, width = value.shape
    tiles = lax.all_to_all(value, "seq", 0, 0, tiled=True)
    return tiles.transpose(1, 0, 2).reshape(rows, count * width)


MESH_ID = pl.DeviceIdType.MESH
STRIP = 32


def grad_sum_kernel(
    sizes, g0, g1, g2, small, out, small_out, norm, own, r0, r1, r2, r3, b0, b1, b2, b3, sq, norms,
    load_sem, s0, t0, s1, t1, s2, t2, s3, t3, s4, t4, s5, t5, small_send, small_recv, norm_send, norm_recv,
):
    ny, nx, nz = sizes
    strips = out.shape[1] // STRIP
    width = out.shape[2]
    half, quarter = width // nx, width // nx // nz
    total = 3 * strips
    dp, sq_idx = lax.axis_index("dp"), lax.axis_index("seq")
    y, c = dp // 2, dp % 2
    z, x = sq_idx // nx, sq_idx % nx
    sibling = (y * 2 + 1 - c, sq_idx)

    def at_y(step):
        other = lax.rem(y + step, ny)
        return other, (other * 2 + c, sq_idx)

    def at_x(step):
        other = lax.rem(x + step, nx)
        return other, (dp, z * nx + other)

    def at_z(step):
        other = lax.rem(z + step, nz)
        return other, (dp, other * nx + x)

    barrier = pltpu.get_barrier_semaphore()
    partners = [sibling] + [at_y(i)[1] for i in range(1, ny)] + [at_x(i)[1] for i in range(1, nx)]
    partners += [at_z(i)[1] for i in range(1, nz)]
    for partner in partners:
        pl.semaphore_signal(barrier, inc=1, device_id=partner, device_id_type=MESH_ID)
    pl.semaphore_wait(barrier, len(partners))

    def remote(src, dst, send, recv, device):
        return pltpu.make_async_remote_copy(src, dst, send, recv, device_id=device, device_id_type=MESH_ID)

    def rows_of(k):
        return pl.ds(pl.multiple_of(lax.rem(k, strips) * STRIP, STRIP), STRIP)

    def cols(start, size):
        return pl.ds(pl.multiple_of(start * size, size), size)

    def core_copy(k, g):
        return remote(g.at[:, 1 - c, rows_of(k)], r0.at[k], s0.at[k], t0.at[k], sibling)

    def own_copy(k, g):
        slot = lax.rem(k, 4)
        return pltpu.make_async_copy(g.at[:, c, rows_of(k)], own.at[slot], load_sem.at[slot])

    def start_first(k):
        for i, g in enumerate((g0, g1, g2)):

            @pl.when(k // strips == i)
            def _():
                core_copy(k, g).start()
                own_copy(k, g).start()

    def y_copy(k, i):
        other, device = at_y(i)
        return remote(r0.at[k, other], r1.at[k, ny - 1 - i], s1.at[k, i - 1], t1.at[k, ny - 1 - i], device)

    def x_copy(k, i):
        other, device = at_x(i)
        return remote(r1.at[k, 0, :, cols(other, half)], r2.at[k, nx - 1 - i], s2.at[k, i - 1], t2.at[k, nx - 1 - i], device)

    def z_copy(k, i):
        other, device = at_z(i)
        return remote(r2.at[k, 0, :, cols(other, quarter)], r3.at[k, nz - 1 - i], s3.at[k, i - 1], t3.at[k, nz - 1 - i], device)

    def z_back(k, i):
        other, device = at_z(i)
        part = out.at[k // strips, rows_of(k), cols(x * nz + z, quarter)]
        return remote(part, part, s4.at[k, i - 1], t4.at[k, nz - 1 - i], device)

    def x_back(k, i):
        other, device = at_x(i)
        part = out.at[k // strips, rows_of(k), cols(x, half)]
        return remote(part, part, s5.at[k, i - 1], t5.at[k, nx - 1 - i], device)

    axes = ((2, c, None), (ny, y, at_y), (nx, x, at_x), (nz, z, at_z))
    base = (0, 1, ny, ny + nx - 1, ny + nx + nz - 2)

    def small_copies(stage):
        def numbered(first, pairs):
            return [
                remote(src, dst, small_send.at[first + i], small_recv.at[first + back], device)
                for i, back, src, dst, device in pairs
            ]

        def spread(axis, pick):
            count, _, at = axes[axis]
            return [(i - 1, count - 1 - i) + pick(i, *at(i)) for i in range(1, count)]

        if stage == 0:
            return numbered(0, [(0, 0, small.at[:, 1 - c], b0, sibling)])
        if stage == 1:
            return numbered(base[1], spread(1, lambda i, o, d: (b0.at[o], b1.at[ny - 1 - i], d)))
        if stage == 2:
            return numbered(base[2], spread(2, lambda i, o, d: (b1.at[0, o], b2.at[nx - 1 - i], d)))
        if stage == 3:
            return numbered(base[3], spread(3, lambda i, o, d: (b2.at[0, o], b3.at[nz - 1 - i], d)))
        again = base[4]
        if stage == 4:
            part = small_out.at[y, c, x, z]
            return numbered(again + base[3], spread(3, lambda i, o, d: (part, part, d)))
        if stage == 5:
            part = small_out.at[y, c, x]
            return numbered(again + base[2], spread(2, lambda i, o, d: (part, part, d)))
        if stage == 6:
            part = small_out.at[y, c]
            return numbered(again + base[1], spread(1, lambda i, o, d: (part, part, d)))
        part = small_out.at[:, c]
        return numbered(again, [(0, 0, part, part, sibling)])

    def small_step(stage):
        if stage > 0:
            for copy in small_copies(stage - 1):
                copy.wait_recv()
        if stage == 1:
            b0[...] += small[:, c]
        if stage == 2:
            value = b0[y]
            for i in range(ny - 1):
                value = value + b1[i]
            b1[0] = value
        if stage == 3:
            value = b1[0, x]
            for i in range(nx - 1):
                value = value + b2[i]
            b2[0] = value
        if stage == 4:
            value = b2[0, z]
            for i in range(nz - 1):
                value = value + b3[i]
            small_out[y, c, x, z] = value
            sq[:, :128] += jnp.concatenate(
                [value * value, jnp.zeros((STRIP - value.shape[0], 128), jnp.float32)], axis=0
            )
        if stage < 8:
            for copy in small_copies(stage):
                copy.start()

    def norm_copies(stage):
        count, place, at = axes[stage]
        devices = [sibling] if at is None else [at(i)[1] for i in range(1, count)]
        return [
            remote(norms.at[stage, place], norms.at[stage, place], norm_send.at[stage, i], norm_recv.at[stage, len(devices) - 1 - i], device)
            for i, device in enumerate(devices)
        ]

    def wide(ref):
        return ref[...].astype(jnp.float32)

    def tiles(size, body):
        step = min(size, 512)

        def one(i, carry):
            body(pl.ds(pl.multiple_of(i * step, step), step))
            return carry

        lax.fori_loop(0, size // step, one, 0)

    sq[...] = jnp.zeros_like(sq)
    start_first(jnp.int32(0))
    start_first(jnp.int32(1))

    def step(t, carry):
        @pl.when(t + 2 < total)
        def _():
            start_first(t + 2)

        @pl.when(t < total)
        def _():
            k, slot = t, lax.rem(t, 4)
            core_copy(k, g0).wait_recv()
            own_copy(k, g0).wait()
            for other in range(ny):

                def add(at):
                    r0[k, other, :, at] = (wide(r0.at[k, other, :, at]) + wide(own.at[slot, other, :, at])).astype(r0.dtype)

                tiles(width, add)
            for i in range(1, ny):
                y_copy(k, i).start()

        @pl.when((t >= 1) & (t < total + 1))
        def _():
            k = t - 1
            for i in range(1, ny):
                y_copy(k, i).wait_recv()

            def add(at):
                value = wide(r0.at[k, y, :, at])
                for i in range(ny - 1):
                    value = value + wide(r1.at[k, i, :, at])
                r1[k, 0, :, at] = value.astype(r1.dtype)

            tiles(width, add)
            for i in range(1, nx):
                x_copy(k, i).start()

        @pl.when((t >= 2) & (t < total + 2))
        def _():
            k = t - 2
            for i in range(1, nx):
                x_copy(k, i).wait_recv()

            def add(at):
                mine = pl.ds(pl.multiple_of(x * half + at.start, 128), at.size)
                value = wide(r1.at[k, 0, :, mine])
                for i in range(nx - 1):
                    value = value + wide(r2.at[k, i, :, at])
                r2[k, 0, :, at] = value.astype(r2.dtype)

            tiles(half, add)
            for i in range(1, nz):
                z_copy(k, i).start()

        @pl.when((t >= 3) & (t < total + 3))
        def _():
            k = t - 3
            for i in range(1, nz):
                z_copy(k, i).wait_recv()
            value = wide(r2.at[k, 0, :, cols(z, quarter)])
            for i in range(nz - 1):
                value = value + wide(r3.at[k, i])
            sq[...] += value * value
            out[k // strips, rows_of(k), cols(x * nz + z, quarter)] = value.astype(out.dtype)
            for i in range(1, nz):
                z_back(k, i).start()

        for stage in range(9):

            @pl.when(t == stage)
            def _():
                small_step(stage)

        @pl.when(t >= 4)
        def _():
            k = t - 4
            for i in range(1, nz):
                z_back(k, i).wait_recv()
            for i in range(1, nx):
                x_back(k, i).start()

        return carry

    lax.fori_loop(0, total + 4, step, 0)
    tile = jnp.zeros((8, 128), jnp.float32)
    for row in range(STRIP // 8):
        for col in range(quarter // 128):
            tile = tile + sq[row * 8 : (row + 1) * 8, col * 128 : (col + 1) * 128]
    for stage in range(4):
        count, place, _ = axes[stage]
        norms[stage, place] = tile
        for copy in norm_copies(stage):
            copy.start()
        for copy in norm_copies(stage):
            copy.wait_recv()
        tile = norms[stage, 0]
        for i in range(1, count):
            tile = tile + norms[stage, i]
    norm[...] = tile
    for stage in range(4):
        for copy in norm_copies(stage):
            copy.wait_send()
    for stage in range(8):
        for copy in small_copies(stage):
            copy.wait_send()

    def finish(k, carry):
        for i in range(1, nx):
            x_back(k, i).wait()
            x_copy(k, i).wait_send()
        for i in range(1, nz):
            z_copy(k, i).wait_send()
            z_back(k, i).wait_send()
        for i in range(1, ny):
            y_copy(k, i).wait_send()
        core_copy(k, g0).wait_send()
        return carry

    lax.fori_loop(0, total, finish, 0)


def grad_sum(up, down, mixer, small):
    rows_all, width = up.shape
    ny = lax.axis_size("dp") // 2
    seq = lax.axis_size("seq")
    nz = 4
    nx = seq // nz
    rows = rows_all // (2 * ny)
    total = 3 * rows // STRIP
    half = jnp.bfloat16
    dma = pltpu.SemaphoreType.DMA
    hbm = pl.BlockSpec(memory_space=pl.ANY)
    shape = (ny, 2, rows, width)
    parts = 2 * ny * seq
    piece = -(-small.shape[0] // (parts * 1024)) * 8
    small = jnp.pad(small, (0, parts * piece * 128 - small.shape[0])).reshape(ny, 2, nx, nz, piece, 128)
    pairs = [(total,), (total, ny - 1), (total, nx - 1), (total, nz - 1), (total, nz - 1), (total, nx - 1)]
    most = max(2, ny, nx, nz)
    smalls = 2 * (ny + nx + nz - 2)
    large, summed, norm = pl.pallas_call(
        functools.partial(grad_sum_kernel, (ny, nx, nz)),
        out_shape=(
            jax.ShapeDtypeStruct((3, rows, width), half),
            jax.ShapeDtypeStruct(small.shape, jnp.float32),
            jax.ShapeDtypeStruct((8, 128), jnp.float32),
        ),
        in_specs=[hbm] * 3 + [VMEM_SPEC],
        out_specs=(VMEM_SPEC,) * 3,
        scratch_shapes=[
            pltpu.VMEM((4, ny, STRIP, width), half),
            pltpu.VMEM((total, ny, STRIP, width), half),
            pltpu.VMEM((total, ny - 1, STRIP, width), half),
            pltpu.VMEM((total, nx - 1, STRIP, width // nx), half),
            pltpu.VMEM((total, nz - 1, STRIP, width // seq), half),
            pltpu.VMEM((ny, nx, nz, piece, 128), jnp.float32),
            pltpu.VMEM((ny - 1, nx, nz, piece, 128), jnp.float32),
            pltpu.VMEM((nx - 1, nz, piece, 128), jnp.float32),
            pltpu.VMEM((nz - 1, piece, 128), jnp.float32),
            pltpu.VMEM((STRIP, width // seq), jnp.float32),
            pltpu.VMEM((4, most, 8, 128), jnp.float32),
            dma((4,)),
        ]
        + [dma(p) for p in pairs for _ in range(2)]
        + [dma((smalls,)), dma((smalls,)), dma((4, most - 1)), dma((4, most - 1))],
        compiler_params=pltpu.CompilerParams(vmem_limit_bytes=56 * 2**20, collective_id=1, has_side_effects=True),
        cost_estimate=pl.CostEstimate(flops=10**8, bytes_accessed=50 * 10**6, transcendentals=0),
        name="grad_sum",
    )(up.reshape(shape), down.reshape(shape), mixer.reshape(shape), small)
    return large, summed.reshape(-1), jnp.sum(norm)


def short_conv(extended, conv_taps):
    token_count = extended.shape[0] - 2
    return (
        conv_taps[0] * extended[2:]
        + conv_taps[1] * extended[1 : token_count + 1]
        + conv_taps[2] * extended[:token_count]
    )


def contract_rows(left, right):
    return lax.dot_general(
        left, right, (((0,), (0,)), ((), ())), preferred_element_type=jnp.float32
    )


def contract_cols(left, right):
    return lax.dot_general(
        left, right, (((1,), (1,)), ((), ())), preferred_element_type=jnp.float32
    )


def adam_update(master, moment, square, grad, factor, rate, decay):
    clipped = grad * factor
    moment_new = beta_one * moment + (1.0 - beta_one) * clipped
    square_new = beta_two * square + (1.0 - beta_two) * clipped * clipped
    moment_hat = moment_new / (1.0 - beta_one**ADAM_STEP)
    square_hat = square_new / (1.0 - beta_two**ADAM_STEP)
    master_new = master - rate * (moment_hat / (jnp.sqrt(square_hat) + adam_eps) + decay * master)
    return (master_new, moment_new, square_new)


def on_device(
    tokens,
    cotangent,
    seq_first,
    decay_code,
    mixer_master,
    mixer_moment,
    mixer_square,
    mlp_master,
    mlp_moment,
    mlp_square,
    channel_master,
    channel_moment,
    channel_square,
    filter_in_master,
    filter_in_moment,
    filter_in_square,
    filter_out_master,
    filter_out_moment,
    filter_out_square,
):
    block_rows = tokens.shape[1]
    model_width = tokens.shape[2]
    lane_count = 3 * model_width
    per = block_rows // PIECE
    seq_count = lax.axis_size("seq")
    long_blocks = max(seq_count // 4, 4)
    length = long_blocks * block_rows
    own_width = model_width // seq_count
    seq_index = lax.axis_index("seq")
    own_first = seq_first[0, 0]
    has_prev = seq_index - own_first >= 1
    w_in = lax.all_gather(mixer_master[:, :lane_count].astype(jnp.bfloat16), "dp", axis=0, tiled=True)
    firsts = lax.all_gather(seq_first[0], "seq", axis=0, tiled=True)
    w_out = lax.all_gather(mixer_master[:, lane_count:].astype(jnp.bfloat16), "dp", axis=0, tiled=True)
    mlp_full = lax.all_gather(mlp_master.astype(jnp.bfloat16), "dp", axis=1, tiled=True)
    w_up = mlp_full[0]
    w_down = mlp_full[1]
    blocks = jnp.arange(seq_count, dtype=jnp.int32)
    lasts = jnp.max(
        jnp.where(firsts[None, :] == firsts[:, None], blocks[None, :], 0), axis=1
    ).astype(jnp.int32)
    conv_taps = channel_master[:, :lane_count]
    gain_one = channel_master[0, lane_count:]
    gain_two = channel_master[1, lane_count:]
    skip_gain = channel_master[2, lane_count:]
    own_codes = lax.dynamic_slice_in_dim(decay_code, seq_index * own_width, own_width, 0)
    own_last = lax.dynamic_slice_in_dim(filter_out_master, seq_index * own_width, own_width, 1)
    filt, filter_pull = jax.vjp(
        lambda first, last: make_filter(first, last, own_codes, length), filter_in_master, own_last
    )
    inputs = tokens[0].astype(jnp.float32)
    normed_b = layer_norm(inputs, gain_one).astype(jnp.bfloat16)
    proj_b = jnp.dot(normed_b, w_in, preferred_element_type=jnp.float32).astype(jnp.bfloat16)
    previous = passed_along(proj_b[block_rows - 2 :], "seq", 1)
    previous = jnp.where(has_prev, previous, jnp.zeros_like(previous))
    extended = jnp.concatenate([previous, proj_b], axis=0).astype(jnp.float32)
    short, short_pull = jax.vjp(short_conv, extended, conv_taps)
    v_part = short[:, :model_width]
    x_one = short[:, model_width : 2 * model_width]
    x_zero = short[:, 2 * model_width :]
    conv_input = (v_part * x_one).astype(jnp.bfloat16)
    conv_in_f = conv_input.astype(jnp.float32)
    pieces = to_channels(conv_input, seq_count).reshape(seq_count * per, PIECE, own_width)
    conv_out = conv_forward(firsts, pieces, filt, per)
    conv = to_tokens(conv_out.reshape(seq_count, block_rows, own_width)).astype(jnp.float32)
    mixed = conv + skip_gain * conv_in_f
    gated_b = (x_zero * mixed).astype(jnp.bfloat16)
    branch = contract_cols(gated_b, w_out)
    resid = inputs + branch
    normed_two, norm_two_pull = jax.vjp(layer_norm, resid, gain_two)
    normed_two_b = normed_two.astype(jnp.bfloat16)
    up_proj = jnp.dot(normed_two_b, w_up, preferred_element_type=jnp.float32)
    act_f, gelu_pull = jax.vjp(jax.nn.gelu, up_proj)
    act_b = act_f.astype(jnp.bfloat16)
    down = contract_cols(act_b, w_down)
    output = resid + down
    grad_down_b = cotangent[0]
    grad_out = grad_down_b.astype(jnp.float32)
    d_act = jnp.dot(grad_down_b, w_down, preferred_element_type=jnp.float32)
    grad_up_b = gelu_pull(d_act)[0].astype(jnp.bfloat16)
    d_normed_two = contract_cols(grad_up_b, w_up)
    resid_part, d_gain_two = norm_two_pull(d_normed_two)
    d_resid = grad_out + resid_part
    grad_branch_b = d_resid.astype(jnp.bfloat16)
    d_gated = jnp.dot(grad_branch_b, w_out, preferred_element_type=jnp.float32)
    d_x_zero = d_gated * mixed
    d_mixed = d_gated * x_zero
    conv_grad = d_mixed.astype(jnp.bfloat16)
    d_skip = jnp.sum(d_mixed * conv_in_f, axis=0)
    up_grad_b = contract_rows(normed_two_b, grad_up_b).astype(jnp.bfloat16)
    down_grad_b = contract_rows(grad_down_b, act_b).astype(jnp.bfloat16)
    out_grad_b = contract_rows(grad_branch_b, gated_b).astype(jnp.bfloat16)
    grad_pieces = to_channels(conv_grad, seq_count).reshape(seq_count * per, PIECE, own_width)
    conv_in_grad, filt_grad = conv_backward(firsts, lasts, pieces, grad_pieces, filt, per)
    back = to_tokens(conv_in_grad.reshape(seq_count, block_rows, own_width)).astype(jnp.float32)
    d_conv_in = skip_gain * d_mixed + back
    first_grad, own_last_grad = filter_pull(filt_grad)
    last_grad = lax.dynamic_update_slice_in_dim(
        jnp.zeros_like(filter_out_master), own_last_grad, seq_index * own_width, 1
    )
    grad_short_b = jnp.concatenate(
        [d_conv_in * x_one, d_conv_in * v_part, d_x_zero], axis=1
    ).astype(jnp.bfloat16)
    d_extended, d_taps = short_pull(grad_short_b.astype(jnp.float32))
    sent_rows = jnp.where(has_prev, grad_short_b[:2], jnp.zeros_like(grad_short_b[:2]))
    later_rows = passed_along(sent_rows, "seq", -1).astype(jnp.float32)
    tail_rows = jnp.stack(
        [conv_taps[2] * later_rows[0], conv_taps[1] * later_rows[0] + conv_taps[2] * later_rows[1]]
    )
    d_proj = d_extended[2:].at[block_rows - 2 :].add(tail_rows)
    grad_proj_b = d_proj.astype(jnp.bfloat16)
    d_normed = contract_cols(grad_proj_b, w_in)
    _, norm_one_pull = jax.vjp(layer_norm, inputs, gain_one)
    input_part, d_gain_one = norm_one_pull(d_normed)
    tokens_grad = d_resid + input_part
    in_grad_b = contract_rows(normed_b, grad_proj_b).astype(jnp.bfloat16)
    mixer_grad_b = jnp.concatenate([in_grad_b, out_grad_b], axis=1)
    vectors = jnp.stack([d_gain_one, d_gain_two, d_skip])
    channel_grad = jnp.concatenate([d_taps, vectors], axis=1)
    small_parts = (channel_grad, first_grad, last_grad)
    large_grads, small_sum, total = grad_sum(
        up_grad_b, down_grad_b, mixer_grad_b, jnp.concatenate([part.reshape(-1) for part in small_parts])
    )
    mlp_grad = large_grads[:2].astype(jnp.float32)
    mixer_grad = large_grads[2].astype(jnp.float32)
    ends = np.cumsum([part.size for part in small_parts])
    channel_grad, first_grad, last_grad = (
        small_sum[end - part.size : end].reshape(part.shape) for part, end in zip(small_parts, ends)
    )
    grad_norm = jnp.sqrt(total)
    factor = jnp.minimum(1.0, clip_limit / (grad_norm + 1e-06))
    mixer_new, mixer_moment_new, mixer_square_new = adam_update(
        mixer_master, mixer_moment, mixer_square, mixer_grad, factor, rate_matrix, weight_decay
    )
    mlp_new, mlp_moment_new, mlp_square_new = adam_update(
        mlp_master, mlp_moment, mlp_square, mlp_grad, factor, rate_matrix, weight_decay
    )
    channel_new, channel_moment_new, channel_square_new = adam_update(
        channel_master, channel_moment, channel_square, channel_grad, factor, rate_small, 0.0
    )
    filter_in_new, filter_in_moment_new, filter_in_square_new = adam_update(
        filter_in_master,
        filter_in_moment,
        filter_in_square,
        first_grad,
        factor,
        rate_small,
        weight_decay,
    )
    filter_out_new, filter_out_moment_new, filter_out_square_new = adam_update(
        filter_out_master,
        filter_out_moment,
        filter_out_square,
        last_grad,
        factor,
        rate_small,
        weight_decay,
    )
    return (
        output.astype(jnp.bfloat16)[None],
        tokens_grad.astype(jnp.bfloat16)[None],
        grad_norm.reshape(1),
        channel_grad,
        first_grad,
        last_grad,
        mixer_new,
        mixer_moment_new,
        mixer_square_new,
        mlp_new,
        mlp_moment_new,
        mlp_square_new,
        channel_new,
        channel_moment_new,
        channel_square_new,
        filter_in_new,
        filter_in_moment_new,
        filter_in_square_new,
        filter_out_new,
        filter_out_moment_new,
        filter_out_square_new,
    )


def solution(mesh):
    in_specs = (
        P("dp", "seq", None),
        P("dp", "seq", None),
        P("dp", "seq"),
        P(),
        P("dp", None),
        P("dp", None),
        P("dp", None),
        P(None, "dp", None),
        P(None, "dp", None),
        P(None, "dp", None),
        P(),
        P(),
        P(),
        P(),
        P(),
        P(),
        P(),
        P(),
        P(),
    )
    out_specs = (
        P("dp", "seq", None),
        P("dp", "seq", None),
        P(),
        P(),
        P(),
        P(),
        P("dp", None),
        P("dp", None),
        P("dp", None),
        P(None, "dp", None),
        P(None, "dp", None),
        P(None, "dp", None),
        P(),
        P(),
        P(),
        P(),
        P(),
        P(),
        P(),
        P(),
        P(),
    )
    return jax.shard_map(
        on_device, mesh=mesh, in_specs=in_specs, out_specs=out_specs, check_vma=False
    )
```

```python
import functools
import math

import jax
import jax.numpy as jnp
import numpy as np
from jax import lax
from jax.experimental import pallas as pl
from jax.experimental.pallas import tpu as pltpu
from jax.sharding import PartitionSpec as P

ADAM_STEP = 10


highest = lax.Precision.HIGHEST
norm_eps = 1e-05
clip_limit = 1.0
beta_one = 0.9
beta_two = 0.999
adam_eps = 1e-08
rate_matrix = 0.03
rate_small = 0.2
weight_decay = 0.1
PIECE = 128


def passed_along(value, axis, steps):
    count = lax.axis_size(axis)
    first, last = (max(0, -steps), min(count, count - steps))
    return lax.ppermute(value, axis, [(source, source + steps) for source in range(first, last)])


def filter_features(length, feature_count):
    places = jnp.arange(length, dtype=jnp.float32)[:, None]
    bands = jnp.arange(1, (feature_count - 1) // 2 + 1, dtype=jnp.float32)[None, :]
    angles = 2.0 * math.pi / length * places * bands
    return jnp.concatenate([places / length, jnp.cos(angles), jnp.sin(angles)], axis=1)


def make_filter(first_weight, last_weight, decay_code, length):
    features = filter_features(length, first_weight.shape[0])
    hidden = jnp.sin(jnp.dot(features, first_weight, precision=highest))
    raw_filter = jnp.dot(hidden, last_weight, precision=highest)
    rates = jnp.exp2(-decay_code.astype(jnp.float32))
    places = jnp.arange(length, dtype=jnp.float32)[:, None]
    shaped = raw_filter * jnp.exp(-places * rates[None, :])
    return shaped * lax.rsqrt(jnp.sum(shaped * shaped, axis=0, keepdims=True) + norm_eps)


def odd_tables(parts):
    freq = np.arange(PIECE)[:, None] * 2 + 1
    sample = np.arange(PIECE)[None, :]
    angles = (freq * sample % (4 * PIECE)) * (2.0 * math.pi / (4 * PIECE))
    pair = np.stack([np.cos(angles), -np.sin(angles)]).reshape(2, parts, PIECE // parts, PIECE)
    table = pair.transpose(1, 0, 2, 3).reshape(parts, 2 * PIECE // parts, PIECE).astype(np.float32)
    upper = table.astype(jnp.bfloat16)
    lower = (table - upper.astype(np.float32)).astype(jnp.bfloat16)
    swap = (0, 2, 1)
    forward = np.concatenate([upper, lower, upper], axis=2)
    backward = np.concatenate([upper.transpose(swap), lower.transpose(swap)], axis=1)
    return jnp.asarray(forward), jnp.asarray(backward)


def dot32(left, right):
    return jnp.dot(left, right, preferred_element_type=jnp.float32)


def split_two(value):
    upper = value.astype(jnp.bfloat16)
    return upper, (value - upper.astype(jnp.float32)).astype(jnp.bfloat16)


def freq_signs(rows, width):
    places = lax.broadcasted_iota(jnp.int32, (rows, width), 0)
    return 1.0 - 2.0 * (places % 2).astype(jnp.float32)


def side_by_side(ref, p, count):
    return jnp.concatenate([ref[p + i] for i in range(count)], axis=1)


def in_groups(count, body):
    size = 8

    def one(i, carry):
        for j in range(0, size, 2):
            body(i * size + j)
        return carry

    lax.fori_loop(0, count // size, one, 0)


def to_freq(table, ref, out, count, factor):
    lanes = ref.shape[2]

    def body(p):
        data = side_by_side(ref, p, 2)
        spec = dot32(table[:, : 2 * PIECE], jnp.concatenate([data, data], axis=0))
        if factor != 1.0:
            spec = spec * factor
        out[p] = spec[:, :lanes]
        out[p + 1] = spec[:, lanes:]

    in_groups(count, body)


def filter_spectrum(filt_ref, table, h_ref):
    half = table.shape[0] // 2
    lanes = filt_ref.shape[1]
    signs = freq_signs(half, lanes)
    prev = None
    for k in range(0, filt_ref.shape[0] // PIECE, 2):
        data = jnp.concatenate([filt_ref[i * PIECE : (i + 1) * PIECE, :] for i in (k, k + 1)], axis=1)
        upper, lower = split_two(data)
        both = dot32(table, jnp.concatenate([upper, upper, lower], axis=0))
        for i in range(2):
            spec = both[:, i * lanes : (i + 1) * lanes]
            if prev is None:
                h_ref[0] = spec
            else:
                h_ref[k + i, :half] = spec[:half] - signs * prev[half:]
                h_ref[k + i, half:] = spec[half:] + signs * prev[:half]
            prev = spec


def to_time(table, ref, count, factor, store):
    lanes = ref.shape[2]

    def body(p):
        value = dot32(table[:PIECE], side_by_side(ref, p, 2).astype(jnp.bfloat16))
        if factor != 1.0:
            value = value * factor
        store(p, value[:, :lanes])
        store(p + 1, value[:, lanes:])

    in_groups(count, body)


def emitter(part, parts, out_ref, acc_ref):
    def store(p, value):
        if parts == 1:
            out_ref[p] = value.astype(out_ref.dtype)
            return
        total = value if part == 0 else acc_ref[p] + value
        if part == parts - 1:
            out_ref[p] = total.astype(out_ref.dtype)
        else:
            acc_ref[p] = total

    return store


def conv_forward_kernel(per, first_ref, x_ref, filt_ref, f_ref, i_ref, o_ref, xs, hs, *rest):
    count, _, lanes = x_ref.shape
    blocks = count // per
    parts = f_ref.shape[0]
    half = PIECE // parts
    tiles = half // 8
    for part in range(parts):
        filter_spectrum(filt_ref, f_ref[part], hs)
        to_freq(f_ref[part], x_ref, xs, count, 1.0)

        def one_tile(step, carry):
            b = blocks - 1 - step // tiles
            row = pl.multiple_of((step % tiles) * 8, 8)
            re = pl.ds(row, 8)
            im = pl.ds(row + half, 8)

            def add_pairs(acc, a, lag, diagonal):
                acc = list(acc)
                for j in range(per):
                    sr, si = xs[a * per + j, re], xs[a * per + j, im]
                    for i in range(j if diagonal else 0, per):
                        hr, hi = hs[lag + i - j, re], hs[lag + i - j, im]
                        acc[2 * i] = acc[2 * i] + (sr * hr - si * hi)
                        acc[2 * i + 1] = acc[2 * i + 1] + (sr * hi + si * hr)
                return tuple(acc)

            acc = tuple(jnp.zeros((8, lanes), jnp.float32) for _ in range(2 * per))
            acc = add_pairs(acc, b, 0, True)
            acc = lax.fori_loop(first_ref[b], b, lambda a, c: add_pairs(c, a, (b - a) * per, False), acc)
            for i in range(per):
                xs[b * per + i, re] = acc[2 * i]
                xs[b * per + i, im] = acc[2 * i + 1]
            return carry

        lax.fori_loop(0, blocks * tiles, one_tile, 0)
        to_time(i_ref[part], xs, count, 1.0 / PIECE, emitter(part, parts, o_ref, rest[0] if rest else None))


def conv_backward_kernel(
    per, first_ref, last_ref, x_ref, g_ref, filt_ref, f_ref, i_ref, dx_ref, df_ref, xs, gs, hs, dh, *rest
):
    count, _, lanes = x_ref.shape
    blocks = count // per
    taps = filt_ref.shape[0] // PIECE
    parts = f_ref.shape[0]
    half = PIECE // parts
    tiles = half // 8
    for part in range(parts):
        filter_spectrum(filt_ref, f_ref[part], hs)
        to_freq(f_ref[part], x_ref, xs, count, 1.0)
        to_freq(f_ref[part], g_ref, gs, count, 1.0 / PIECE)
        dh[...] = jnp.zeros_like(dh)

        def one_tile(step, carry):
            a = step // tiles
            row = pl.multiple_of((step % tiles) * 8, 8)
            re = pl.ds(row, 8)
            im = pl.ds(row + half, 8)

            def add_pairs(acc, b, lag, diagonal):
                acc = list(acc)
                for delta in range(0 if diagonal else 1 - per, per):
                    hr, hi = hs[lag + delta, re], hs[lag + delta, im]
                    tr, ti = dh[lag + delta, re], dh[lag + delta, im]
                    for j in range(max(0, -delta), per - max(0, delta)):
                        sr, si = xs[a * per + j, re], xs[a * per + j, im]
                        gr, gi = gs[b * per + j + delta, re], gs[b * per + j + delta, im]
                        acc[2 * j] = acc[2 * j] + (hr * gr + hi * gi)
                        acc[2 * j + 1] = acc[2 * j + 1] + (hr * gi - hi * gr)
                        tr = tr + (sr * gr + si * gi)
                        ti = ti + (sr * gi - si * gr)
                    dh[lag + delta, re] = tr
                    dh[lag + delta, im] = ti
                return tuple(acc)

            acc = tuple(jnp.zeros((8, lanes), jnp.float32) for _ in range(2 * per))
            acc = add_pairs(acc, a, 0, True)
            acc = lax.fori_loop(a + 1, last_ref[a] + 1, lambda b, c: add_pairs(c, b, (b - a) * per, False), acc)
            for j in range(per):
                xs[a * per + j, re] = acc[2 * j]
                xs[a * per + j, im] = acc[2 * j + 1]
            return carry

        lax.fori_loop(0, blocks * tiles, one_tile, 0)
        to_time(i_ref[part], xs, count, 1.0, emitter(part, parts, dx_ref, rest[0] if rest else None))
        signs = freq_signs(half, lanes)
        back_u, back_l = i_ref[part, :PIECE], i_ref[part, PIECE:]
        for k in range(taps):
            grad = dh[k]
            if k + 1 < taps:
                grad = grad + jnp.concatenate([signs * dh[k + 1, half:], -signs * dh[k + 1, :half]], axis=0)
            upper, lower = split_two(grad)
            value = dot32(back_u, upper) + (dot32(back_l, upper) + dot32(back_u, lower))
            rows = slice(k * PIECE, (k + 1) * PIECE)
            df_ref[rows, :] = value if part == 0 else df_ref[rows, :] + value


VMEM_SPEC = pl.BlockSpec(memory_space=pltpu.VMEM)
SMEM_SPEC = pl.BlockSpec(memory_space=pltpu.SMEM)


def conv_parts(count):
    return 1 if count <= 64 else 4


def conv_forward(firsts, pieces, filt, per):
    count, _, lanes = pieces.shape
    taps = filt.shape[0] // PIECE
    parts = conv_parts(count)
    spec = (2 * PIECE // parts, lanes)
    scratch = [pltpu.VMEM((count,) + spec, jnp.float32), pltpu.VMEM((taps,) + spec, jnp.float32)]
    if parts > 1:
        scratch.append(pltpu.VMEM(pieces.shape, jnp.float32))
    return pl.pallas_call(
        functools.partial(conv_forward_kernel, per),
        out_shape=jax.ShapeDtypeStruct(pieces.shape, jnp.bfloat16),
        in_specs=[SMEM_SPEC] + [VMEM_SPEC] * 4,
        out_specs=VMEM_SPEC,
        scratch_shapes=scratch,
        compiler_params=pltpu.CompilerParams(vmem_limit_bytes=56 * 2**20),
        cost_estimate=pl.CostEstimate(flops=2 * 10**9, bytes_accessed=8 * 10**6, transcendentals=0),
        name="long_conv",
    )(firsts, pieces, filt, *odd_tables(parts))


def conv_backward(firsts, lasts, pieces, grads, filt, per):
    count, _, lanes = pieces.shape
    taps = filt.shape[0] // PIECE
    parts = conv_parts(count)
    spec = (2 * PIECE // parts, lanes)
    scratch = [pltpu.VMEM((n,) + spec, jnp.float32) for n in (count, count, taps, taps)]
    if parts > 1:
        scratch.append(pltpu.VMEM(pieces.shape, jnp.float32))
    return pl.pallas_call(
        functools.partial(conv_backward_kernel, per),
        out_shape=(
            jax.ShapeDtypeStruct(pieces.shape, jnp.bfloat16),
            jax.ShapeDtypeStruct(filt.shape, jnp.float32),
        ),
        in_specs=[SMEM_SPEC] * 2 + [VMEM_SPEC] * 5,
        out_specs=(VMEM_SPEC, VMEM_SPEC),
        scratch_shapes=scratch,
        compiler_params=pltpu.CompilerParams(vmem_limit_bytes=56 * 2**20),
        cost_estimate=pl.CostEstimate(flops=4 * 10**9, bytes_accessed=10**7, transcendentals=0),
        name="long_conv_back",
    )(firsts, lasts, pieces, grads, filt, *odd_tables(parts))


def to_channels(value, count):
    groups, rows, lanes = value.shape
    if groups != count:
        own = groups * lanes // count
        value = value.reshape(groups, rows, lanes // own, own).transpose(0, 2, 1, 3).reshape(count, rows, own)
    return lax.all_to_all(value, "seq", 0, 0, tiled=True)


def to_tokens(value):
    count, rows, own = value.shape
    value = lax.all_to_all(value, "seq", 0, 0, tiled=True)
    if own != LANES:
        value = value.reshape(-1, LANES // own, rows, own).transpose(0, 2, 1, 3).reshape(-1, rows, LANES)
    return value


MESH_ID = pl.DeviceIdType.MESH
STRIP = 32


def grad_sum_kernel(
    sizes, g0, g1, g2, small, out, small_out, norm, own, r0, r1, r2, r3, b0, b1, b2, b3, sq, norms,
    load_sem, s0, t0, s1, t1, s2, t2, s3, t3, s4, t4, s5, t5, small_send, small_recv, norm_send, norm_recv,
):
    ny, nx, nz = sizes
    strips = out.shape[1] // STRIP
    width = out.shape[2]
    half, quarter = width // nx, width // nx // nz
    total = 3 * strips
    dp, sq_idx = lax.axis_index("dp"), lax.axis_index("seq")
    y, c = dp // 2, dp % 2
    z, x = sq_idx // nx, sq_idx % nx
    sibling = (y * 2 + 1 - c, sq_idx)

    def at_y(step):
        other = lax.rem(y + step, ny)
        return other, (other * 2 + c, sq_idx)

    def at_x(step):
        other = lax.rem(x + step, nx)
        return other, (dp, z * nx + other)

    def at_z(step):
        other = lax.rem(z + step, nz)
        return other, (dp, other * nx + x)

    barrier = pltpu.get_barrier_semaphore()
    partners = [sibling] + [at_y(i)[1] for i in range(1, ny)] + [at_x(i)[1] for i in range(1, nx)]
    partners += [at_z(i)[1] for i in range(1, nz)]
    for partner in partners:
        pl.semaphore_signal(barrier, inc=1, device_id=partner, device_id_type=MESH_ID)
    pl.semaphore_wait(barrier, len(partners))

    def remote(src, dst, send, recv, device):
        return pltpu.make_async_remote_copy(src, dst, send, recv, device_id=device, device_id_type=MESH_ID)

    def rows_of(k):
        return pl.ds(pl.multiple_of(lax.rem(k, strips) * STRIP, STRIP), STRIP)

    def cols(start, size):
        return pl.ds(pl.multiple_of(start * size, size), size)

    def core_copy(k, g):
        return remote(g.at[:, 1 - c, rows_of(k)], r0.at[k], s0.at[k], t0.at[k], sibling)

    def own_copy(k, g):
        slot = lax.rem(k, 4)
        return pltpu.make_async_copy(g.at[:, c, rows_of(k)], own.at[slot], load_sem.at[slot])

    def start_first(k):
        for i, g in enumerate((g0, g1, g2)):

            @pl.when(k // strips == i)
            def _():
                core_copy(k, g).start()
                own_copy(k, g).start()

    def y_copy(k, i):
        other, device = at_y(i)
        return remote(r0.at[k, other], r1.at[k, ny - 1 - i], s1.at[k, i - 1], t1.at[k, ny - 1 - i], device)

    def x_copy(k, i):
        other, device = at_x(i)
        return remote(r1.at[k, 0, :, cols(other, half)], r2.at[k, nx - 1 - i], s2.at[k, i - 1], t2.at[k, nx - 1 - i], device)

    def z_copy(k, i):
        other, device = at_z(i)
        return remote(r2.at[k, 0, :, cols(other, quarter)], r3.at[k, nz - 1 - i], s3.at[k, i - 1], t3.at[k, nz - 1 - i], device)

    def z_back(k, i):
        other, device = at_z(i)
        part = out.at[k // strips, rows_of(k), cols(x * nz + z, quarter)]
        return remote(part, part, s4.at[k, i - 1], t4.at[k, nz - 1 - i], device)

    def x_back(k, i):
        other, device = at_x(i)
        part = out.at[k // strips, rows_of(k), cols(x, half)]
        return remote(part, part, s5.at[k, i - 1], t5.at[k, nx - 1 - i], device)

    axes = ((2, c, None), (ny, y, at_y), (nx, x, at_x), (nz, z, at_z))
    base = (0, 1, ny, ny + nx - 1, ny + nx + nz - 2)

    def small_copies(stage):
        def numbered(first, pairs):
            return [
                remote(src, dst, small_send.at[first + i], small_recv.at[first + back], device)
                for i, back, src, dst, device in pairs
            ]

        def spread(axis, pick):
            count, _, at = axes[axis]
            return [(i - 1, count - 1 - i) + pick(i, *at(i)) for i in range(1, count)]

        if stage == 0:
            return numbered(0, [(0, 0, small.at[:, 1 - c], b0, sibling)])
        if stage == 1:
            return numbered(base[1], spread(1, lambda i, o, d: (b0.at[o], b1.at[ny - 1 - i], d)))
        if stage == 2:
            return numbered(base[2], spread(2, lambda i, o, d: (b1.at[0, o], b2.at[nx - 1 - i], d)))
        if stage == 3:
            return numbered(base[3], spread(3, lambda i, o, d: (b2.at[0, o], b3.at[nz - 1 - i], d)))
        again = base[4]
        if stage == 4:
            part = small_out.at[y, c, x, z]
            return numbered(again + base[3], spread(3, lambda i, o, d: (part, part, d)))
        if stage == 5:
            part = small_out.at[y, c, x]
            return numbered(again + base[2], spread(2, lambda i, o, d: (part, part, d)))
        if stage == 6:
            part = small_out.at[y, c]
            return numbered(again + base[1], spread(1, lambda i, o, d: (part, part, d)))
        part = small_out.at[:, c]
        return numbered(again, [(0, 0, part, part, sibling)])

    def small_step(stage):
        if stage > 0:
            for copy in small_copies(stage - 1):
                copy.wait_recv()
        if stage == 1:
            b0[...] += small[:, c]
        if stage == 2:
            value = b0[y]
            for i in range(ny - 1):
                value = value + b1[i]
            b1[0] = value
        if stage == 3:
            value = b1[0, x]
            for i in range(nx - 1):
                value = value + b2[i]
            b2[0] = value
        if stage == 4:
            value = b2[0, z]
            for i in range(nz - 1):
                value = value + b3[i]
            small_out[y, c, x, z] = value
            sq[:, :128] += jnp.concatenate(
                [value * value, jnp.zeros((STRIP - value.shape[0], 128), jnp.float32)], axis=0
            )
        if stage < 8:
            for copy in small_copies(stage):
                copy.start()

    def norm_copies(stage):
        count, place, at = axes[stage]
        devices = [sibling] if at is None else [at(i)[1] for i in range(1, count)]
        return [
            remote(norms.at[stage, place], norms.at[stage, place], norm_send.at[stage, i], norm_recv.at[stage, len(devices) - 1 - i], device)
            for i, device in enumerate(devices)
        ]

    def wide(ref):
        return ref[...].astype(jnp.float32)

    def tiles(size, body):
        step = min(size, 512)

        def one(i, carry):
            body(pl.ds(pl.multiple_of(i * step, step), step))
            return carry

        lax.fori_loop(0, size // step, one, 0)

    sq[...] = jnp.zeros_like(sq)
    start_first(jnp.int32(0))
    start_first(jnp.int32(1))

    def step(t, carry):
        @pl.when(t + 2 < total)
        def _():
            start_first(t + 2)

        @pl.when(t < total)
        def _():
            k, slot = t, lax.rem(t, 4)
            core_copy(k, g0).wait_recv()
            own_copy(k, g0).wait()
            for other in range(ny):

                def add(at):
                    r0[k, other, :, at] = (wide(r0.at[k, other, :, at]) + wide(own.at[slot, other, :, at])).astype(r0.dtype)

                tiles(width, add)
            for i in range(1, ny):
                y_copy(k, i).start()

        @pl.when((t >= 1) & (t < total + 1))
        def _():
            k = t - 1
            for i in range(1, ny):
                y_copy(k, i).wait_recv()

            def add(at):
                value = wide(r0.at[k, y, :, at])
                for i in range(ny - 1):
                    value = value + wide(r1.at[k, i, :, at])
                r1[k, 0, :, at] = value.astype(r1.dtype)

            tiles(width, add)
            for i in range(1, nx):
                x_copy(k, i).start()

        @pl.when((t >= 2) & (t < total + 2))
        def _():
            k = t - 2
            for i in range(1, nx):
                x_copy(k, i).wait_recv()

            def add(at):
                mine = pl.ds(pl.multiple_of(x * half + at.start, 128), at.size)
                value = wide(r1.at[k, 0, :, mine])
                for i in range(nx - 1):
                    value = value + wide(r2.at[k, i, :, at])
                r2[k, 0, :, at] = value.astype(r2.dtype)

            tiles(half, add)
            for i in range(1, nz):
                z_copy(k, i).start()

        @pl.when((t >= 3) & (t < total + 3))
        def _():
            k = t - 3
            for i in range(1, nz):
                z_copy(k, i).wait_recv()
            value = wide(r2.at[k, 0, :, cols(z, quarter)])
            for i in range(nz - 1):
                value = value + wide(r3.at[k, i])
            sq[...] += value * value
            out[k // strips, rows_of(k), cols(x * nz + z, quarter)] = value.astype(out.dtype)
            for i in range(1, nz):
                z_back(k, i).start()

        for stage in range(9):

            @pl.when(t == stage)
            def _():
                small_step(stage)

        @pl.when(t >= 4)
        def _():
            k = t - 4
            for i in range(1, nz):
                z_back(k, i).wait_recv()
            for i in range(1, nx):
                x_back(k, i).start()

        return carry

    lax.fori_loop(0, total + 4, step, 0)
    tile = jnp.zeros((8, 128), jnp.float32)
    for row in range(STRIP // 8):
        for col in range(quarter // 128):
            tile = tile + sq[row * 8 : (row + 1) * 8, col * 128 : (col + 1) * 128]
    for stage in range(4):
        count, place, _ = axes[stage]
        norms[stage, place] = tile
        for copy in norm_copies(stage):
            copy.start()
        for copy in norm_copies(stage):
            copy.wait_recv()
        tile = norms[stage, 0]
        for i in range(1, count):
            tile = tile + norms[stage, i]
    norm[...] = tile
    for stage in range(4):
        for copy in norm_copies(stage):
            copy.wait_send()
    for stage in range(8):
        for copy in small_copies(stage):
            copy.wait_send()

    def finish(k, carry):
        for i in range(1, nx):
            x_back(k, i).wait()
            x_copy(k, i).wait_send()
        for i in range(1, nz):
            z_copy(k, i).wait_send()
            z_back(k, i).wait_send()
        for i in range(1, ny):
            y_copy(k, i).wait_send()
        core_copy(k, g0).wait_send()
        return carry

    lax.fori_loop(0, total, finish, 0)


def grad_sum(up, down, mixer, small):
    rows_all, width = up.shape
    ny = lax.axis_size("dp") // 2
    seq = lax.axis_size("seq")
    nz = 4
    nx = seq // nz
    rows = rows_all // (2 * ny)
    total = 3 * rows // STRIP
    half = jnp.bfloat16
    dma = pltpu.SemaphoreType.DMA
    hbm = pl.BlockSpec(memory_space=pl.ANY)
    shape = (ny, 2, rows, width)
    parts = 2 * ny * seq
    piece = -(-small.shape[0] // (parts * 1024)) * 8
    small = jnp.pad(small, (0, parts * piece * 128 - small.shape[0])).reshape(ny, 2, nx, nz, piece, 128)
    pairs = [(total,), (total, ny - 1), (total, nx - 1), (total, nz - 1), (total, nz - 1), (total, nx - 1)]
    most = max(2, ny, nx, nz)
    smalls = 2 * (ny + nx + nz - 2)
    large, summed, norm = pl.pallas_call(
        functools.partial(grad_sum_kernel, (ny, nx, nz)),
        out_shape=(
            jax.ShapeDtypeStruct((3, rows, width), half),
            jax.ShapeDtypeStruct(small.shape, jnp.float32),
            jax.ShapeDtypeStruct((8, 128), jnp.float32),
        ),
        in_specs=[hbm] * 3 + [VMEM_SPEC],
        out_specs=(VMEM_SPEC,) * 3,
        scratch_shapes=[
            pltpu.VMEM((4, ny, STRIP, width), half),
            pltpu.VMEM((total, ny, STRIP, width), half),
            pltpu.VMEM((total, ny - 1, STRIP, width), half),
            pltpu.VMEM((total, nx - 1, STRIP, width // nx), half),
            pltpu.VMEM((total, nz - 1, STRIP, width // seq), half),
            pltpu.VMEM((ny, nx, nz, piece, 128), jnp.float32),
            pltpu.VMEM((ny - 1, nx, nz, piece, 128), jnp.float32),
            pltpu.VMEM((nx - 1, nz, piece, 128), jnp.float32),
            pltpu.VMEM((nz - 1, piece, 128), jnp.float32),
            pltpu.VMEM((STRIP, width // seq), jnp.float32),
            pltpu.VMEM((4, most, 8, 128), jnp.float32),
            dma((4,)),
        ]
        + [dma(p) for p in pairs for _ in range(2)]
        + [dma((smalls,)), dma((smalls,)), dma((4, most - 1)), dma((4, most - 1))],
        compiler_params=pltpu.CompilerParams(vmem_limit_bytes=56 * 2**20, collective_id=1, has_side_effects=True),
        cost_estimate=pl.CostEstimate(flops=10**8, bytes_accessed=50 * 10**6, transcendentals=0),
        name="grad_sum",
    )(up.reshape(shape), down.reshape(shape), mixer.reshape(shape), small)
    return large, summed.reshape(-1), jnp.sum(norm)


def contract_rows(left, right):
    return lax.dot_general(
        left, right, (((0,), (0,)), ((), ())), preferred_element_type=jnp.float32
    )


def block_specs(shapes):
    return [pl.BlockSpec(shape, lambda j, n=len(shape): (0,) * n, pipeline_mode=pl.Buffered(1)) for shape in shapes]


def normalized(values):
    center = jnp.mean(values, axis=-1, keepdims=True)
    centred = values - center
    scale = lax.rsqrt(jnp.mean(centred * centred, axis=-1, keepdims=True) + norm_eps)
    return centred * scale, scale


def norm_back(grad, gain, scaled, scale):
    inner = grad * gain
    mean_inner = jnp.mean(inner, axis=-1, keepdims=True)
    mean_scaled = jnp.mean(inner * scaled, axis=-1, keepdims=True)
    return scale * (inner - mean_inner - scaled * mean_scaled)


def dot_cols(left, right):
    return lax.dot_general(left, right, (((1,), (1,)), ((), ())), preferred_element_type=jnp.float32)


LANES = 128
HALO = 8


def project_kernel(tok, before, prev, gain, w_v, w_one, w_zero, t_v, t_one, t_zero,
                   conv_in, factors, zero_out, projs, normed_out, normed, held):
    rows = tok.shape[0]
    keep = prev[0].astype(jnp.float32)

    @pl.when(pl.program_id(0) == 0)
    def _():
        scaled, _ = normalized(before[...].astype(jnp.float32))
        normed[:HALO] = (scaled * gain[...]).astype(jnp.bfloat16)
        for start in range(0, rows, PIECE):
            at = slice(start, start + PIECE)
            scaled, _ = normalized(tok[at].astype(jnp.float32))
            value = (scaled * gain[...]).astype(jnp.bfloat16)
            normed[start + HALO : start + PIECE + HALO] = value
            normed_out[at] = value

    shorts = []
    for i, (w, taps) in enumerate(((w_v, t_v), (w_one, t_one), (w_zero, t_zero))):
        proj = dot32(normed[...], w[...]).astype(jnp.bfloat16)
        projs[i] = proj
        held[...] = proj.astype(jnp.float32)
        held[:HALO] = held[:HALO] * keep
        shorts.append(
            taps[0:1] * held[HALO : HALO + rows]
            + taps[1:2] * held[HALO - 1 : HALO - 1 + rows]
            + taps[2:3] * held[HALO - 2 : HALO - 2 + rows]
        )
    factors[0] = shorts[1]
    factors[1] = shorts[0]
    zero_out[...] = shorts[2]
    product = (shorts[0] * shorts[1]).astype(jnp.bfloat16)
    for i in range(conv_in.shape[0]):
        conv_in[i] = product[:, i * LANES : (i + 1) * LANES]


def project(tok, before, has_prev, gain, w_in, taps):
    rows, width = tok.shape
    size = 256
    steps = width // size
    col = lambda part: (lambda j: (0, part * steps + j))
    parts = [pl.BlockSpec((width, size), col(i)) for i in range(3)]
    tap_parts = [pl.BlockSpec((3, size), col(i)) for i in range(3)]
    wide = lambda n, dtype: jax.ShapeDtypeStruct((n, width), dtype)
    stack = lambda m, n: pl.BlockSpec((m, n, size), lambda j: (0, 0, j))
    return pl.pallas_call(
        project_kernel,
        grid=(steps,),
        out_shape=[jax.ShapeDtypeStruct((width // LANES, rows, LANES), jnp.bfloat16)]
        + [jax.ShapeDtypeStruct((2, rows, width), jnp.float32), wide(rows, jnp.float32)]
        + [jax.ShapeDtypeStruct((3, rows + HALO, width), jnp.bfloat16), wide(rows, jnp.bfloat16)],
        in_specs=block_specs([(rows, width), (HALO, width)]) + [SMEM_SPEC] + block_specs([(1, width)]) + parts + tap_parts,
        out_specs=[pl.BlockSpec((size // LANES, rows, LANES), lambda j: (j, 0, 0))]
        + [stack(2, rows), pl.BlockSpec((rows, size), lambda j: (0, j)), stack(3, rows + HALO)]
        + block_specs([(rows, width)]),
        scratch_shapes=[pltpu.VMEM((rows + HALO, width), jnp.bfloat16), pltpu.VMEM((rows + HALO, size), jnp.float32)],
        compiler_params=pltpu.CompilerParams(vmem_limit_bytes=48 * 2**20),
        cost_estimate=pl.CostEstimate(flops=6 * rows * width * width, bytes_accessed=20 * 10**6, transcendentals=0),
        name="project",
    )(tok, before, has_prev, gain, w_in, w_in, w_in, taps, taps, taps)


def mlp_kernel(conv, conv_in, zero, tok, cot, skip, gain, w_out, w_up, w_down,
               output, act_out, up_out, gated, normed, d_resid, branch_out, conv_grad, d_mixed, d_zero, d_gain, d_skip,
               resid, down, d_normed):
    rows, width = tok.shape
    groups = width // LANES
    step = pl.program_id(0)

    @pl.when(step == 0)
    def _():
        for g in range(groups):
            at = slice(g * LANES, (g + 1) * LANES)
            mixed = conv[g].astype(jnp.float32) + skip[:, at] * conv_in[g].astype(jnp.float32)
            gated[:, at] = (zero[:, at] * mixed).astype(jnp.bfloat16)
        resid[...] = tok[...].astype(jnp.float32) + dot_cols(gated[...], w_out[...])
        for start in range(0, rows, PIECE):
            at = slice(start, start + PIECE)
            scaled, _ = normalized(resid[at])
            normed[at] = (scaled * gain[...]).astype(jnp.bfloat16)

    up = dot32(normed[...], w_up[...])
    d_act = dot32(cot[...], w_down[...])
    root = math.sqrt(2.0 / math.pi)
    square = up * up
    bent = jnp.tanh(root * up * (1.0 + 0.044715 * square))
    act = (0.5 * up * (1.0 + bent)).astype(jnp.bfloat16)
    slope = 0.5 * (1.0 + bent) + (0.5 * root) * up * (1.0 - bent * bent) * (1.0 + (3.0 * 0.044715) * square)
    g_up = (slope * d_act).astype(jnp.bfloat16)
    act_out[...] = act
    up_out[...] = g_up
    down_part = dot_cols(act, w_down[...])
    normed_part = dot_cols(g_up, w_up[...])

    @pl.when(step == 0)
    def _():
        down[...] = down_part
        d_normed[...] = normed_part

    @pl.when(step > 0)
    def _():
        down[...] += down_part
        d_normed[...] += normed_part

    @pl.when(step == pl.num_programs(0) - 1)
    def _():
        gain_sum = jnp.zeros((1, width), jnp.float32)
        for start in range(0, rows, PIECE):
            at = slice(start, start + PIECE)
            output[at] = (resid[at] + down[at]).astype(jnp.bfloat16)
            scaled, scale = normalized(resid[at])
            grad = d_normed[at]
            gain_sum = gain_sum + jnp.sum(grad * scaled, axis=0, keepdims=True)
            total = cot[at].astype(jnp.float32) + norm_back(grad, gain[...], scaled, scale)
            d_resid[at] = total
            branch_out[at] = total.astype(jnp.bfloat16)
        d_gain[...] = gain_sum
        down[...] = dot32(branch_out[...], w_out[...])
        for g in range(groups):
            at = slice(g * LANES, (g + 1) * LANES)
            source = conv_in[g].astype(jnp.float32)
            mixed = conv[g].astype(jnp.float32) + skip[:, at] * source
            d_gated = down[:, at]
            d_zero[:, at] = (d_gated * mixed).astype(jnp.bfloat16)
            grad = d_gated * zero[:, at]
            d_mixed[g] = grad
            conv_grad[g] = grad.astype(jnp.bfloat16)
            d_skip[:, at] = jnp.sum(grad * source, axis=0, keepdims=True)


def mlp_block(conv, conv_in, zero, tok, cot, skip, gain, w_out, weights):
    rows, width = tok.shape
    hidden = weights.shape[2]
    size = 512
    steps = hidden // size
    groups = width // LANES
    flat = lambda dtype: jax.ShapeDtypeStruct((rows, width), dtype)
    cut = lambda dtype: jax.ShapeDtypeStruct((groups, rows, LANES), dtype)
    row = jax.ShapeDtypeStruct((1, width), jnp.float32)
    big = jax.ShapeDtypeStruct((rows, hidden), jnp.bfloat16)
    half, full = jnp.bfloat16, jnp.float32
    ends = [flat(half), flat(half), flat(full), flat(half), cut(half), cut(full), flat(half), row, row]
    tile = pl.BlockSpec((rows, size), lambda j: (0, j))
    one = block_specs([(rows, width)])
    return pl.pallas_call(
        mlp_kernel,
        grid=(steps,),
        out_shape=[flat(half), big, big] + ends,
        in_specs=block_specs([conv.shape, conv.shape, zero.shape, tok.shape, cot.shape, (1, width), (1, width), w_out.shape])
        + [pl.BlockSpec((None, width, size), lambda j, i=i: (i, 0, j)) for i in range(2)],
        out_specs=one + [tile, tile] + block_specs([e.shape for e in ends]),
        scratch_shapes=[pltpu.VMEM((rows, width), full)] * 3,
        compiler_params=pltpu.CompilerParams(vmem_limit_bytes=60 * 2**20),
        cost_estimate=pl.CostEstimate(flops=8 * rows * width * hidden + 4 * rows * width * width, bytes_accessed=50 * 10**6, transcendentals=rows * hidden),
        name="mlp_block",
    )(conv, conv_in, zero, tok, cot, skip, gain, w_out, weights, weights)


def project_back_kernel(back, d_mixed, other, d_zero, proj, after, prev, nxt, skip, taps, w_in, normed, branch, gated, tok, d_resid, gain,
                        d_mixer, d_taps, tokens_grad, d_gain, normed_t, branch_t, d_normed, held, wide_proj):
    rows = tok.shape[0]
    size = held.shape[1]
    step = pl.program_id(0)
    steps = pl.num_programs(0)
    part = step // (steps // 4)

    @pl.when(step == 0)
    def _():
        d_normed[...] = jnp.zeros_like(d_normed)
        normed_t[...] = normed[...].T
        branch_t[...] = branch[...].T

    def spread(ref):
        return jnp.concatenate([ref[i].astype(jnp.float32) for i in range(ref.shape[0])], axis=1)

    @pl.when(part < 2)
    def _():
        d_conv_in = skip[...] * spread(d_mixed) + spread(back)
        held[:rows] = (d_conv_in * other[...]).astype(jnp.bfloat16).astype(jnp.float32)

    @pl.when(part == 2)
    def _():
        held[:rows] = d_zero[...].astype(jnp.float32)

    @pl.when(part < 3)
    def _():
        held[rows:] = after[...].astype(jnp.float32) * nxt[0].astype(jnp.float32)
        g_proj = (
            taps[0:1] * held[:rows] + taps[1:2] * held[1 : rows + 1] + taps[2:3] * held[2 : rows + 2]
        ).astype(jnp.bfloat16)
        wide_proj[...] = proj[...].astype(jnp.float32)
        wide_proj[:HALO] = wide_proj[:HALO] * prev[0].astype(jnp.float32)
        d_taps[...] = jnp.concatenate(
            [jnp.sum(held[:rows] * wide_proj[HALO - i : HALO - i + rows], axis=0, keepdims=True) for i in range(3)], axis=0
        )
        d_normed[...] += dot_cols(g_proj, w_in[...])
        d_mixer[...] = dot32(normed_t[...], g_proj).astype(jnp.bfloat16)

    @pl.when(part == 3)
    def _():
        d_mixer[...] = dot32(branch_t[...], gated[...]).astype(jnp.bfloat16)

    @pl.when(step == steps - 1)
    def _():
        gain_sum = jnp.zeros((1, tok.shape[1]), jnp.float32)
        for start in range(0, rows, PIECE):
            at = slice(start, start + PIECE)
            scaled, scale = normalized(tok[at].astype(jnp.float32))
            grad = d_normed[at]
            gain_sum = gain_sum + jnp.sum(grad * scaled, axis=0, keepdims=True)
            tokens_grad[at] = (d_resid[at] + norm_back(grad, gain[...], scaled, scale)).astype(jnp.bfloat16)
        d_gain[...] = gain_sum


def project_back(back, d_mixed, shorts, d_zero, projs, after, has_prev, has_next, skip, taps, w_in, normed, branch, gated, tok, d_resid, gain):
    rows, width = tok.shape
    size = 512
    per = width // size
    steps = 4 * per
    half = jnp.bfloat16
    lane = lambda j: lax.rem(j, per)
    inner = lambda j: jnp.minimum(j, 3 * per - 1)
    group = pl.BlockSpec((size // LANES, rows, LANES), lambda j: (lane(j), 0, 0))
    third = lambda n: pl.BlockSpec((n, size), lambda j: (0, inner(j)))
    tile = pl.BlockSpec((rows, size), lambda j: (0, lane(j)))
    return pl.pallas_call(
        project_back_kernel,
        grid=(steps,),
        out_shape=[
            jax.ShapeDtypeStruct((width, 4 * width), half),
            jax.ShapeDtypeStruct((3, 3 * width), jnp.float32),
            jax.ShapeDtypeStruct((rows, width), half),
            jax.ShapeDtypeStruct((1, width), jnp.float32),
        ],
        in_specs=[group, group, pl.BlockSpec((None, rows, size), lambda j: (jnp.minimum(j // per, 1), 0, lane(j))), tile]
        + [pl.BlockSpec((None, rows + HALO, size), lambda j: (jnp.minimum(j // per, 2), 0, lane(j)))]
        + [third(HALO), SMEM_SPEC, SMEM_SPEC, pl.BlockSpec((1, size), lambda j: (0, lane(j))), third(3), third(width)]
        + block_specs([(rows, width)] * 2)
        + [tile]
        + block_specs([(rows, width)] * 2 + [(1, width)]),
        out_specs=[pl.BlockSpec((width, size), lambda j: (0, j)), third(3)] + block_specs([(rows, width), (1, width)]),
        scratch_shapes=[
            pltpu.VMEM((width, rows), half),
            pltpu.VMEM((width, rows), half),
            pltpu.VMEM((rows, width), jnp.float32),
            pltpu.VMEM((rows + HALO, size), jnp.float32),
            pltpu.VMEM((rows + HALO, size), jnp.float32),
        ],
        compiler_params=pltpu.CompilerParams(vmem_limit_bytes=60 * 2**20),
        cost_estimate=pl.CostEstimate(flops=14 * rows * width * width, bytes_accessed=50 * 10**6, transcendentals=0),
        name="project_back",
    )(back, d_mixed, shorts, d_zero, projs, after, has_prev, has_next, skip, taps, w_in, normed, branch, gated, tok, d_resid, gain)


def adam_update(master, moment, square, grad, factor, rate, decay):
    clipped = grad * factor
    moment_new = beta_one * moment + (1.0 - beta_one) * clipped
    square_new = beta_two * square + (1.0 - beta_two) * clipped * clipped
    moment_hat = moment_new / (1.0 - beta_one**ADAM_STEP)
    square_hat = square_new / (1.0 - beta_two**ADAM_STEP)
    master_new = master - rate * (moment_hat / (jnp.sqrt(square_hat) + adam_eps) + decay * master)
    return (master_new, moment_new, square_new)


def on_device(
    tokens,
    cotangent,
    seq_first,
    decay_code,
    mixer_master,
    mixer_moment,
    mixer_square,
    mlp_master,
    mlp_moment,
    mlp_square,
    channel_master,
    channel_moment,
    channel_square,
    filter_in_master,
    filter_in_moment,
    filter_in_square,
    filter_out_master,
    filter_out_moment,
    filter_out_square,
):
    block_rows = tokens.shape[1]
    model_width = tokens.shape[2]
    lane_count = 3 * model_width
    per = block_rows // PIECE
    seq_count = lax.axis_size("seq")
    long_blocks = max(seq_count // 4, 4)
    length = long_blocks * block_rows
    own_width = model_width // seq_count
    seq_index = lax.axis_index("seq")
    w_in = lax.all_gather(mixer_master[:, :lane_count].astype(jnp.bfloat16), "dp", axis=0, tiled=True)
    before = passed_along(tokens[0, block_rows - HALO :], "seq", 1)
    firsts = lax.all_gather(seq_first[0], "seq", axis=0, tiled=True)
    w_out = lax.all_gather(mixer_master[:, lane_count:].astype(jnp.bfloat16), "dp", axis=0, tiled=True)
    mlp_full = lax.all_gather(mlp_master.astype(jnp.bfloat16), "dp", axis=1, tiled=True)
    blocks = jnp.arange(seq_count, dtype=jnp.int32)
    same = firsts[None, :] == firsts[:, None]
    lasts = jnp.max(jnp.where(same, blocks[None, :], 0), axis=1).astype(jnp.int32)
    own_first = firsts[seq_index]
    has_prev = (seq_index - own_first >= 1).astype(jnp.int32).reshape(1)
    has_next = (lasts[seq_index] > seq_index).astype(jnp.int32).reshape(1)
    conv_taps = channel_master[:, :lane_count]
    gain_one = channel_master[0:1, lane_count:]
    gain_two = channel_master[1:2, lane_count:]
    skip_gain = channel_master[2:3, lane_count:]
    own_codes = lax.dynamic_slice_in_dim(decay_code, seq_index * own_width, own_width, 0)
    own_last = lax.dynamic_slice_in_dim(filter_out_master, seq_index * own_width, own_width, 1)
    filt, filter_pull = jax.vjp(
        lambda first, last: make_filter(first, last, own_codes, length), filter_in_master, own_last
    )
    conv_input, factors, x_zero, projs, normed_b = project(tokens[0], before, has_prev, gain_one, w_in, conv_taps)
    pieces = to_channels(conv_input, seq_count).reshape(seq_count * per, PIECE, own_width)
    conv_out = conv_forward(firsts, pieces, filt, per)
    conv = to_tokens(conv_out.reshape(seq_count, block_rows, own_width))
    (
        output, act_b, grad_up_b, gated_b, normed_two_b, d_resid, grad_branch_b, conv_grad, d_mixed, d_x_zero, d_gain_two, d_skip,
    ) = mlp_block(conv, conv_input, x_zero, tokens[0], cotangent[0], skip_gain, gain_two, w_out, mlp_full)
    grad_pieces = to_channels(conv_grad, seq_count).reshape(seq_count * per, PIECE, own_width)
    up_grad_b = contract_rows(normed_two_b, grad_up_b).astype(jnp.bfloat16)
    down_grad_b = contract_rows(cotangent[0], act_b).astype(jnp.bfloat16)
    conv_in_grad, filt_grad = conv_backward(firsts, lasts, pieces, grad_pieces, filt, per)
    back = to_tokens(conv_in_grad.reshape(seq_count, block_rows, own_width))
    head_grad = skip_gain.reshape(-1, 1, LANES) * d_mixed[:, :HALO] + back[:, :HALO].astype(jnp.float32)
    head_grad = head_grad.transpose(1, 0, 2).reshape(HALO, model_width)
    head = [head_grad * factors[0, :HALO], head_grad * factors[1, :HALO], d_x_zero[:HALO].astype(jnp.float32)]
    after = passed_along(jnp.concatenate(head, axis=1).astype(jnp.bfloat16), "seq", -1)
    first_grad, own_last_grad = filter_pull(filt_grad)
    last_grad = lax.dynamic_update_slice_in_dim(
        jnp.zeros_like(filter_out_master), own_last_grad, seq_index * own_width, 1
    )
    mixer_grad_b, d_taps, tokens_grad, d_gain_one = project_back(
        back, d_mixed, factors, d_x_zero, projs, after, has_prev, has_next, skip_gain, conv_taps, w_in,
        normed_b, grad_branch_b, gated_b, tokens[0], d_resid, gain_one,
    )
    vectors = jnp.concatenate([d_gain_one, d_gain_two, d_skip], axis=0)
    channel_grad = jnp.concatenate([d_taps, vectors], axis=1)
    small_parts = (channel_grad, first_grad, last_grad)
    large_grads, small_sum, total = grad_sum(
        up_grad_b, down_grad_b, mixer_grad_b, jnp.concatenate([part.reshape(-1) for part in small_parts])
    )
    mlp_grad = large_grads[:2].astype(jnp.float32)
    mixer_grad = large_grads[2].astype(jnp.float32)
    ends = np.cumsum([part.size for part in small_parts])
    channel_grad, first_grad, last_grad = (
        small_sum[end - part.size : end].reshape(part.shape) for part, end in zip(small_parts, ends)
    )
    grad_norm = jnp.sqrt(total)
    factor = jnp.minimum(1.0, clip_limit / (grad_norm + 1e-06))
    mixer_new, mixer_moment_new, mixer_square_new = adam_update(
        mixer_master, mixer_moment, mixer_square, mixer_grad, factor, rate_matrix, weight_decay
    )
    mlp_new, mlp_moment_new, mlp_square_new = adam_update(
        mlp_master, mlp_moment, mlp_square, mlp_grad, factor, rate_matrix, weight_decay
    )
    channel_new, channel_moment_new, channel_square_new = adam_update(
        channel_master, channel_moment, channel_square, channel_grad, factor, rate_small, 0.0
    )
    filter_in_new, filter_in_moment_new, filter_in_square_new = adam_update(
        filter_in_master,
        filter_in_moment,
        filter_in_square,
        first_grad,
        factor,
        rate_small,
        weight_decay,
    )
    filter_out_new, filter_out_moment_new, filter_out_square_new = adam_update(
        filter_out_master,
        filter_out_moment,
        filter_out_square,
        last_grad,
        factor,
        rate_small,
        weight_decay,
    )
    return (
        output[None],
        tokens_grad[None],
        grad_norm.reshape(1),
        channel_grad,
        first_grad,
        last_grad,
        mixer_new,
        mixer_moment_new,
        mixer_square_new,
        mlp_new,
        mlp_moment_new,
        mlp_square_new,
        channel_new,
        channel_moment_new,
        channel_square_new,
        filter_in_new,
        filter_in_moment_new,
        filter_in_square_new,
        filter_out_new,
        filter_out_moment_new,
        filter_out_square_new,
    )


def solution(mesh):
    in_specs = (
        P("dp", "seq", None),
        P("dp", "seq", None),
        P("dp", "seq"),
        P(),
        P("dp", None),
        P("dp", None),
        P("dp", None),
        P(None, "dp", None),
        P(None, "dp", None),
        P(None, "dp", None),
        P(),
        P(),
        P(),
        P(),
        P(),
        P(),
        P(),
        P(),
        P(),
    )
    out_specs = (
        P("dp", "seq", None),
        P("dp", "seq", None),
        P(),
        P(),
        P(),
        P(),
        P("dp", None),
        P("dp", None),
        P("dp", None),
        P(None, "dp", None),
        P(None, "dp", None),
        P(None, "dp", None),
        P(),
        P(),
        P(),
        P(),
        P(),
        P(),
        P(),
        P(),
        P(),
    )
    return jax.shard_map(
        on_device, mesh=mesh, in_specs=in_specs, out_specs=out_specs, check_vma=False
    )
```

```python
import functools
import math

import jax
import jax.numpy as jnp
import numpy as np
from jax import lax
from jax.experimental import pallas as pl
from jax.experimental.pallas import tpu as pltpu
from jax.sharding import PartitionSpec as P

ADAM_STEP = 10


highest = lax.Precision.HIGHEST
norm_eps = 1e-05
clip_limit = 1.0
beta_one = 0.9
beta_two = 0.999
adam_eps = 1e-08
rate_matrix = 0.03
rate_small = 0.2
weight_decay = 0.1
PIECE = 128


def passed_along(value, axis, steps):
    count = lax.axis_size(axis)
    first, last = (max(0, -steps), min(count, count - steps))
    return lax.ppermute(value, axis, [(source, source + steps) for source in range(first, last)])


def filter_features(length, feature_count):
    places = jnp.arange(length, dtype=jnp.float32)[:, None]
    bands = jnp.arange(1, (feature_count - 1) // 2 + 1, dtype=jnp.float32)[None, :]
    angles = 2.0 * math.pi / length * places * bands
    return jnp.concatenate([places / length, jnp.cos(angles), jnp.sin(angles)], axis=1)


def make_filter(first_weight, last_weight, decay_code, length):
    features = filter_features(length, first_weight.shape[0])
    hidden = jnp.sin(jnp.dot(features, first_weight, precision=highest))
    raw_filter = jnp.dot(hidden, last_weight, precision=highest)
    rates = jnp.exp2(-decay_code.astype(jnp.float32))
    places = jnp.arange(length, dtype=jnp.float32)[:, None]
    shaped = raw_filter * jnp.exp(-places * rates[None, :])
    return shaped * lax.rsqrt(jnp.sum(shaped * shaped, axis=0, keepdims=True) + norm_eps)


def odd_tables(parts):
    freq = np.arange(PIECE)[:, None] * 2 + 1
    sample = np.arange(PIECE)[None, :]
    angles = (freq * sample % (4 * PIECE)) * (2.0 * math.pi / (4 * PIECE))
    pair = np.stack([np.cos(angles), -np.sin(angles)]).reshape(2, parts, PIECE // parts, PIECE)
    table = pair.transpose(1, 0, 2, 3).reshape(parts, 2 * PIECE // parts, PIECE).astype(np.float32)
    upper = table.astype(jnp.bfloat16)
    lower = (table - upper.astype(np.float32)).astype(jnp.bfloat16)
    swap = (0, 2, 1)
    forward = np.concatenate([upper, lower, upper], axis=2)
    backward = np.concatenate([upper.transpose(swap), lower.transpose(swap)], axis=1)
    return jnp.asarray(forward), jnp.asarray(backward)


def dot32(left, right):
    return jnp.dot(left, right, preferred_element_type=jnp.float32)


def split_two(value):
    upper = value.astype(jnp.bfloat16)
    return upper, (value - upper.astype(jnp.float32)).astype(jnp.bfloat16)


def freq_signs(rows, width):
    places = lax.broadcasted_iota(jnp.int32, (rows, width), 0)
    return 1.0 - 2.0 * (places % 2).astype(jnp.float32)


def side_by_side(ref, p, count):
    return jnp.concatenate([ref[p + i] for i in range(count)], axis=1)


def in_groups(count, body):
    size = 8

    def one(i, carry):
        for j in range(0, size, 2):
            body(i * size + j)
        return carry

    lax.fori_loop(0, count // size, one, 0)


def to_freq(table, ref, out, count, factor):
    lanes = ref.shape[2]

    def body(p):
        data = side_by_side(ref, p, 2)
        spec = dot32(table[:, : 2 * PIECE], jnp.concatenate([data, data], axis=0))
        if factor != 1.0:
            spec = spec * factor
        out[p] = spec[:, :lanes]
        out[p + 1] = spec[:, lanes:]

    in_groups(count, body)


def filter_spectrum(filt_ref, table, h_ref):
    half = table.shape[0] // 2
    lanes = filt_ref.shape[1]
    signs = freq_signs(half, lanes)
    prev = None
    for k in range(0, filt_ref.shape[0] // PIECE, 2):
        data = jnp.concatenate([filt_ref[i * PIECE : (i + 1) * PIECE, :] for i in (k, k + 1)], axis=1)
        upper, lower = split_two(data)
        both = dot32(table, jnp.concatenate([upper, upper, lower], axis=0))
        for i in range(2):
            spec = both[:, i * lanes : (i + 1) * lanes]
            if prev is None:
                h_ref[0] = spec
            else:
                h_ref[k + i, :half] = spec[:half] - signs * prev[half:]
                h_ref[k + i, half:] = spec[half:] + signs * prev[:half]
            prev = spec


def to_time(table, ref, count, factor, store):
    lanes = ref.shape[2]

    def body(p):
        value = dot32(table[:PIECE], side_by_side(ref, p, 2).astype(jnp.bfloat16))
        if factor != 1.0:
            value = value * factor
        store(p, value[:, :lanes])
        store(p + 1, value[:, lanes:])

    in_groups(count, body)


def emitter(part, parts, out_ref, acc_ref):
    def store(p, value):
        if parts == 1:
            out_ref[p] = value.astype(out_ref.dtype)
            return
        total = value if part == 0 else acc_ref[p] + value
        if part == parts - 1:
            out_ref[p] = total.astype(out_ref.dtype)
        else:
            acc_ref[p] = total

    return store


def conv_forward_kernel(per, first_ref, x_ref, filt_ref, f_ref, i_ref, o_ref, xs, hs, *rest):
    count, _, lanes = x_ref.shape
    blocks = count // per
    parts = f_ref.shape[0]
    half = PIECE // parts
    tiles = half // 8
    for part in range(parts):
        filter_spectrum(filt_ref, f_ref[part], hs)
        to_freq(f_ref[part], x_ref, xs, count, 1.0)

        def one_tile(step, carry):
            b = blocks - 1 - step // tiles
            row = pl.multiple_of((step % tiles) * 8, 8)
            re = pl.ds(row, 8)
            im = pl.ds(row + half, 8)

            def add_pairs(acc, a, lag, diagonal):
                acc = list(acc)
                for j in range(per):
                    sr, si = xs[a * per + j, re], xs[a * per + j, im]
                    for i in range(j if diagonal else 0, per):
                        hr, hi = hs[lag + i - j, re], hs[lag + i - j, im]
                        acc[2 * i] = acc[2 * i] + (sr * hr - si * hi)
                        acc[2 * i + 1] = acc[2 * i + 1] + (sr * hi + si * hr)
                return tuple(acc)

            acc = tuple(jnp.zeros((8, lanes), jnp.float32) for _ in range(2 * per))
            acc = add_pairs(acc, b, 0, True)
            acc = lax.fori_loop(first_ref[b], b, lambda a, c: add_pairs(c, a, (b - a) * per, False), acc)
            for i in range(per):
                xs[b * per + i, re] = acc[2 * i]
                xs[b * per + i, im] = acc[2 * i + 1]
            return carry

        lax.fori_loop(0, blocks * tiles, one_tile, 0)
        to_time(i_ref[part], xs, count, 1.0 / PIECE, emitter(part, parts, o_ref, rest[0] if rest else None))


def conv_backward_kernel(
    per, first_ref, last_ref, x_ref, g_ref, filt_ref, f_ref, i_ref, dx_ref, df_ref, xs, gs, hs, dh, *rest
):
    count, _, lanes = x_ref.shape
    blocks = count // per
    taps = filt_ref.shape[0] // PIECE
    parts = f_ref.shape[0]
    half = PIECE // parts
    tiles = half // 8
    for part in range(parts):
        filter_spectrum(filt_ref, f_ref[part], hs)
        to_freq(f_ref[part], x_ref, xs, count, 1.0)
        to_freq(f_ref[part], g_ref, gs, count, 1.0 / PIECE)
        dh[...] = jnp.zeros_like(dh)

        def one_tile(step, carry):
            a = step // tiles
            row = pl.multiple_of((step % tiles) * 8, 8)
            re = pl.ds(row, 8)
            im = pl.ds(row + half, 8)

            def add_pairs(acc, b, lag, diagonal):
                acc = list(acc)
                for delta in range(0 if diagonal else 1 - per, per):
                    hr, hi = hs[lag + delta, re], hs[lag + delta, im]
                    tr, ti = dh[lag + delta, re], dh[lag + delta, im]
                    for j in range(max(0, -delta), per - max(0, delta)):
                        sr, si = xs[a * per + j, re], xs[a * per + j, im]
                        gr, gi = gs[b * per + j + delta, re], gs[b * per + j + delta, im]
                        acc[2 * j] = acc[2 * j] + (hr * gr + hi * gi)
                        acc[2 * j + 1] = acc[2 * j + 1] + (hr * gi - hi * gr)
                        tr = tr + (sr * gr + si * gi)
                        ti = ti + (sr * gi - si * gr)
                    dh[lag + delta, re] = tr
                    dh[lag + delta, im] = ti
                return tuple(acc)

            acc = tuple(jnp.zeros((8, lanes), jnp.float32) for _ in range(2 * per))
            acc = add_pairs(acc, a, 0, True)
            acc = lax.fori_loop(a + 1, last_ref[a] + 1, lambda b, c: add_pairs(c, b, (b - a) * per, False), acc)
            for j in range(per):
                xs[a * per + j, re] = acc[2 * j]
                xs[a * per + j, im] = acc[2 * j + 1]
            return carry

        lax.fori_loop(0, blocks * tiles, one_tile, 0)
        to_time(i_ref[part], xs, count, 1.0, emitter(part, parts, dx_ref, rest[0] if rest else None))
        signs = freq_signs(half, lanes)
        back_u, back_l = i_ref[part, :PIECE], i_ref[part, PIECE:]
        for k in range(taps):
            grad = dh[k]
            if k + 1 < taps:
                grad = grad + jnp.concatenate([signs * dh[k + 1, half:], -signs * dh[k + 1, :half]], axis=0)
            upper, lower = split_two(grad)
            value = dot32(back_u, upper) + (dot32(back_l, upper) + dot32(back_u, lower))
            rows = slice(k * PIECE, (k + 1) * PIECE)
            df_ref[rows, :] = value if part == 0 else df_ref[rows, :] + value


VMEM_SPEC = pl.BlockSpec(memory_space=pltpu.VMEM)
SMEM_SPEC = pl.BlockSpec(memory_space=pltpu.SMEM)


def conv_parts(count):
    return 1 if count <= 64 else 4


def conv_forward(firsts, pieces, filt, per):
    count, _, lanes = pieces.shape
    taps = filt.shape[0] // PIECE
    parts = conv_parts(count)
    spec = (2 * PIECE // parts, lanes)
    scratch = [pltpu.VMEM((count,) + spec, jnp.float32), pltpu.VMEM((taps,) + spec, jnp.float32)]
    if parts > 1:
        scratch.append(pltpu.VMEM(pieces.shape, jnp.float32))
    return pl.pallas_call(
        functools.partial(conv_forward_kernel, per),
        out_shape=jax.ShapeDtypeStruct(pieces.shape, jnp.bfloat16),
        in_specs=[SMEM_SPEC] + [VMEM_SPEC] * 4,
        out_specs=VMEM_SPEC,
        scratch_shapes=scratch,
        compiler_params=pltpu.CompilerParams(vmem_limit_bytes=56 * 2**20),
        cost_estimate=pl.CostEstimate(flops=2 * 10**9, bytes_accessed=8 * 10**6, transcendentals=0),
        name="long_conv",
    )(firsts, pieces, filt, *odd_tables(parts))


def conv_backward(firsts, lasts, pieces, grads, filt, per):
    count, _, lanes = pieces.shape
    taps = filt.shape[0] // PIECE
    parts = conv_parts(count)
    spec = (2 * PIECE // parts, lanes)
    scratch = [pltpu.VMEM((n,) + spec, jnp.float32) for n in (count, count, taps, taps)]
    if parts > 1:
        scratch.append(pltpu.VMEM(pieces.shape, jnp.float32))
    return pl.pallas_call(
        functools.partial(conv_backward_kernel, per),
        out_shape=(
            jax.ShapeDtypeStruct(pieces.shape, jnp.bfloat16),
            jax.ShapeDtypeStruct(filt.shape, jnp.float32),
        ),
        in_specs=[SMEM_SPEC] * 2 + [VMEM_SPEC] * 5,
        out_specs=(VMEM_SPEC, VMEM_SPEC),
        scratch_shapes=scratch,
        compiler_params=pltpu.CompilerParams(vmem_limit_bytes=56 * 2**20),
        cost_estimate=pl.CostEstimate(flops=4 * 10**9, bytes_accessed=10**7, transcendentals=0),
        name="long_conv_back",
    )(firsts, lasts, pieces, grads, filt, *odd_tables(parts))


def channel_order(value, count):
    groups, rows, lanes = value.shape
    if groups != count:
        own = groups * lanes // count
        value = value.reshape(groups, rows, lanes // own, own).transpose(0, 2, 1, 3).reshape(count, rows, own)
    return value


def lane_order(value):
    _, rows, own = value.shape
    if own != LANES:
        value = value.reshape(-1, LANES // own, rows, own).transpose(0, 2, 1, 3).reshape(-1, rows, LANES)
    return value


def to_channels(value, count):
    return lax.all_to_all(channel_order(value, count), "seq", 0, 0, tiled=True)


def to_tokens(value):
    return lane_order(lax.all_to_all(value, "seq", 0, 0, tiled=True))


MESH_ID = pl.DeviceIdType.MESH
def remote(src, dst, send, recv, device):
    return pltpu.make_async_remote_copy(src, dst, send, recv, device_id=device, device_id_type=MESH_ID)


def greet(partners):
    barrier = pltpu.get_barrier_semaphore()
    for partner in partners:
        pl.semaphore_signal(barrier, inc=1, device_id=partner, device_id_type=MESH_ID)
    pl.semaphore_wait(barrier, len(partners))


def place_of(sizes):
    ny, nx, nz = sizes
    dp, seq = lax.axis_index("dp"), lax.axis_index("seq")
    y, c = dp // 2, dp % 2
    z, x = seq // nx, seq % nx

    def at_y(step):
        other = lax.rem(y + step, ny)
        return other, (other * 2 + c, seq)

    def at_x(step):
        other = lax.rem(x + step, nx)
        return other, (dp, z * nx + other)

    def at_z(step):
        other = lax.rem(z + step, nz)
        return other, (dp, other * nx + x)

    return (y, c, z, x), (y * 2 + 1 - c, seq), at_y, at_x, at_z


def axis_sizes():
    seq = lax.axis_size("seq")
    return lax.axis_size("dp") // 2, seq // 4, 4


def wide(ref):
    return ref[...].astype(jnp.float32)


def staged_sum(sizes, grads, out, sq, scratch):
    own, r0, r1, r2, r3, load_sem, s0, t0, s1, t1, s2, t2, s3, t3, s4, t4, s5, t5 = scratch
    ny, nx, nz = sizes
    strip = r0.shape[2]
    strips = out.shape[1] // strip
    width = out.shape[2]
    half, quarter = width // nx, width // nx // nz
    total = len(grads) * strips
    (y, c, z, x), sibling, at_y, at_x, at_z = place_of(sizes)

    def rows_of(k):
        return pl.ds(pl.multiple_of(lax.rem(k, strips) * strip, strip), strip)

    def cols(start, size):
        return pl.ds(pl.multiple_of(start * size, size), size)

    def core_copy(k, g):
        return remote(g.at[:, 1 - c, rows_of(k)], r0.at[k], s0.at[k], t0.at[k], sibling)

    def own_copy(k, g):
        slot = lax.rem(k, 4)
        return pltpu.make_async_copy(g.at[:, c, rows_of(k)], own.at[slot], load_sem.at[slot])

    def start_first(k):
        for i, g in enumerate(grads):

            @pl.when(k // strips == i)
            def _():
                core_copy(k, g).start()
                own_copy(k, g).start()

    def y_copy(k, i):
        other, device = at_y(i)
        return remote(r0.at[k, other], r1.at[k, ny - 1 - i], s1.at[k, i - 1], t1.at[k, ny - 1 - i], device)

    def x_copy(k, i):
        other, device = at_x(i)
        return remote(r1.at[k, 0, :, cols(other, half)], r2.at[k, nx - 1 - i], s2.at[k, i - 1], t2.at[k, nx - 1 - i], device)

    def z_copy(k, i):
        other, device = at_z(i)
        return remote(r2.at[k, 0, :, cols(other, quarter)], r3.at[k, nz - 1 - i], s3.at[k, i - 1], t3.at[k, nz - 1 - i], device)

    def z_back(k, i):
        other, device = at_z(i)
        part = out.at[k // strips, rows_of(k), cols(x * nz + z, quarter)]
        return remote(part, part, s4.at[k, i - 1], t4.at[k, nz - 1 - i], device)

    def x_back(k, i):
        other, device = at_x(i)
        part = out.at[k // strips, rows_of(k), cols(x, half)]
        return remote(part, part, s5.at[k, i - 1], t5.at[k, nx - 1 - i], device)

    def tiles(size, body):
        piece = min(size, TILE // strip)

        def one(i, carry):
            body(pl.ds(pl.multiple_of(i * piece, piece), piece))
            return carry

        lax.fori_loop(0, size // piece, one, 0)

    def begin():
        start_first(jnp.int32(0))
        start_first(jnp.int32(1))

    def step(t):
        @pl.when(t + 2 < total)
        def _():
            start_first(t + 2)

        @pl.when(t < total)
        def _():
            k, slot = t, lax.rem(t, 4)
            core_copy(k, grads[0]).wait_recv()
            own_copy(k, grads[0]).wait()
            for other in range(ny):

                def add(at):
                    r0[k, other, :, at] = (wide(r0.at[k, other, :, at]) + wide(own.at[slot, other, :, at])).astype(r0.dtype)

                tiles(width, add)
            for i in range(1, ny):
                y_copy(k, i).start()

        @pl.when((t >= OFFSETS[0]) & (t < total + OFFSETS[0]))
        def _():
            k = t - OFFSETS[0]
            for i in range(1, ny):
                y_copy(k, i).wait_recv()

            def add(at):
                value = wide(r0.at[k, y, :, at])
                for i in range(ny - 1):
                    value = value + wide(r1.at[k, i, :, at])
                r1[k, 0, :, at] = value.astype(r1.dtype)

            tiles(width, add)
            for i in range(1, nx):
                x_copy(k, i).start()

        @pl.when((t >= OFFSETS[1]) & (t < total + OFFSETS[1]))
        def _():
            k = t - OFFSETS[1]
            for i in range(1, nx):
                x_copy(k, i).wait_recv()

            def add(at):
                mine = pl.ds(pl.multiple_of(x * half + at.start, 128), at.size)
                value = wide(r1.at[k, 0, :, mine])
                for i in range(nx - 1):
                    value = value + wide(r2.at[k, i, :, at])
                r2[k, 0, :, at] = value.astype(r2.dtype)

            tiles(half, add)
            for i in range(1, nz):
                z_copy(k, i).start()

        @pl.when((t >= OFFSETS[2]) & (t < total + OFFSETS[2]))
        def _():
            k = t - OFFSETS[2]
            for i in range(1, nz):
                z_copy(k, i).wait_recv()
            value = wide(r2.at[k, 0, :, cols(z, quarter)])
            for i in range(nz - 1):
                value = value + wide(r3.at[k, i])
            sq[...] += value * value
            out[k // strips, rows_of(k), cols(x * nz + z, quarter)] = value.astype(out.dtype)
            for i in range(1, nz):
                z_back(k, i).start()

        @pl.when((t >= OFFSETS[3]) & (t < total + OFFSETS[3]))
        def _():
            k = t - OFFSETS[3]
            for i in range(1, nz):
                z_back(k, i).wait_recv()
            for i in range(1, nx):
                x_back(k, i).start()

    def finish():
        def one(k, carry):
            for i in range(1, nx):
                x_back(k, i).wait()
                x_copy(k, i).wait_send()
            for i in range(1, nz):
                z_copy(k, i).wait_send()
                z_back(k, i).wait_send()
            for i in range(1, ny):
                y_copy(k, i).wait_send()
            core_copy(k, grads[0]).wait_send()
            return carry

        lax.fori_loop(0, total, one, 0)

    return begin, step, finish, total + OFFSETS[3]


def staged_scratch(sizes, count, rows, strip, width):
    ny, nx, nz = sizes
    total = count * rows // strip
    half = jnp.bfloat16
    dma = pltpu.SemaphoreType.DMA
    pairs = [(total,), (total, ny - 1), (total, nx - 1), (total, nz - 1), (total, nz - 1), (total, nx - 1)]
    return [
        pltpu.VMEM((4, ny, strip, width), half),
        pltpu.VMEM((total, ny, strip, width), half),
        pltpu.VMEM((total, ny - 1, strip, width), half),
        pltpu.VMEM((total, nx - 1, strip, width // nx), half),
        pltpu.VMEM((total, nz - 1, strip, width // nx // nz), half),
        dma((4,)),
    ] + [dma(p) for p in pairs for _ in range(2)]


STAGED = 18
TILE = 65536
OFFSETS = (1, 2, 3, 4)


def grad_sum_kernel(sizes, g0, g1, g2, small, out, small_out, norm, *scratch):
    staged, (b0, b1, b2, b3, sq, norms, small_send, small_recv, norm_send, norm_recv) = scratch[:STAGED], scratch[STAGED:]
    ny, nx, nz = sizes
    (y, c, z, x), sibling, at_y, at_x, at_z = place_of(sizes)
    partners = [sibling] + [at_y(i)[1] for i in range(1, ny)] + [at_x(i)[1] for i in range(1, nx)]
    greet(partners + [at_z(i)[1] for i in range(1, nz)])
    axes = ((2, c, None), (ny, y, at_y), (nx, x, at_x), (nz, z, at_z))
    base = (0, 1, ny, ny + nx - 1, ny + nx + nz - 2)

    def small_copies(stage):
        def numbered(first, pairs):
            return [
                remote(src, dst, small_send.at[first + i], small_recv.at[first + back], device)
                for i, back, src, dst, device in pairs
            ]

        def spread(axis, pick):
            count, _, at = axes[axis]
            return [(i - 1, count - 1 - i) + pick(i, *at(i)) for i in range(1, count)]

        if stage == 0:
            return numbered(0, [(0, 0, small.at[:, 1 - c], b0, sibling)])
        if stage == 1:
            return numbered(base[1], spread(1, lambda i, o, d: (b0.at[o], b1.at[ny - 1 - i], d)))
        if stage == 2:
            return numbered(base[2], spread(2, lambda i, o, d: (b1.at[0, o], b2.at[nx - 1 - i], d)))
        if stage == 3:
            return numbered(base[3], spread(3, lambda i, o, d: (b2.at[0, o], b3.at[nz - 1 - i], d)))
        again = base[4]
        if stage == 4:
            part = small_out.at[y, c, x, z]
            return numbered(again + base[3], spread(3, lambda i, o, d: (part, part, d)))
        if stage == 5:
            part = small_out.at[y, c, x]
            return numbered(again + base[2], spread(2, lambda i, o, d: (part, part, d)))
        if stage == 6:
            part = small_out.at[y, c]
            return numbered(again + base[1], spread(1, lambda i, o, d: (part, part, d)))
        part = small_out.at[:, c]
        return numbered(again, [(0, 0, part, part, sibling)])

    def small_step(stage):
        if stage > 0:
            for copy in small_copies(stage - 1):
                copy.wait_recv()
        if stage == 1:
            b0[...] += small[:, c]
        if stage == 2:
            value = b0[y]
            for i in range(ny - 1):
                value = value + b1[i]
            b1[0] = value
        if stage == 3:
            value = b1[0, x]
            for i in range(nx - 1):
                value = value + b2[i]
            b2[0] = value
        if stage == 4:
            value = b2[0, z]
            for i in range(nz - 1):
                value = value + b3[i]
            small_out[y, c, x, z] = value
            for row in range(0, value.shape[0], 8):
                sq[:8, :128] += value[row : row + 8] * value[row : row + 8]
        if stage < 8:
            for copy in small_copies(stage):
                copy.start()

    def norm_copies(stage):
        count, place, at = axes[stage]
        devices = [sibling] if at is None else [at(i)[1] for i in range(1, count)]
        return [
            remote(norms.at[stage, place], norms.at[stage, place], norm_send.at[stage, i], norm_recv.at[stage, len(devices) - 1 - i], device)
            for i, device in enumerate(devices)
        ]

    begin, step, finish, count = staged_sum(sizes, (g0, g1, g2), out, sq, staged)
    sq[...] = jnp.zeros_like(sq)
    begin()

    def one_step(t, carry):
        step(t)
        for stage in range(9):

            @pl.when(t == stage)
            def _():
                small_step(stage)

        return carry

    lax.fori_loop(0, max(count, 9), one_step, 0)
    tile = jnp.zeros((8, 128), jnp.float32)
    for row in range(0, sq.shape[0], 8):
        for col in range(0, sq.shape[1], 128):
            tile = tile + sq[row : row + 8, col : col + 128]
    for stage in range(4):
        count, place, _ = axes[stage]
        norms[stage, place] = tile
        for copy in norm_copies(stage):
            copy.start()
        for copy in norm_copies(stage):
            copy.wait_recv()
        tile = norms[stage, 0]
        for i in range(1, count):
            tile = tile + norms[stage, i]
    norm[...] = tile
    for stage in range(4):
        for copy in norm_copies(stage):
            copy.wait_send()
    for stage in range(8):
        for copy in small_copies(stage):
            copy.wait_send()
    finish()


def grad_sum(up, down, mixer, small):
    sizes = ny, nx, nz = axis_sizes()
    rows_all, width = mixer.shape
    seq = nx * nz
    rows = rows_all // (2 * ny)
    strip = 32
    full = jnp.float32
    dma = pltpu.SemaphoreType.DMA
    parts = 2 * ny * seq
    piece = -(-small.shape[0] // (parts * 1024)) * 8
    small = jnp.pad(small, (0, parts * piece * 128 - small.shape[0])).reshape(ny, 2, nx, nz, piece, 128)
    most = max(2, ny, nx, nz)
    smalls = 2 * (ny + nx + nz - 2)
    large, summed, norm = pl.pallas_call(
        functools.partial(grad_sum_kernel, sizes),
        out_shape=(
            jax.ShapeDtypeStruct((3, rows, width), jnp.bfloat16),
            jax.ShapeDtypeStruct(small.shape, full),
            jax.ShapeDtypeStruct((8, 128), full),
        ),
        in_specs=[pl.BlockSpec(memory_space=pl.ANY)] * 3 + [VMEM_SPEC],
        out_specs=(VMEM_SPEC,) * 3,
        scratch_shapes=staged_scratch(sizes, 3, rows, strip, width)
        + [
            pltpu.VMEM((ny, nx, nz, piece, 128), full),
            pltpu.VMEM((ny - 1, nx, nz, piece, 128), full),
            pltpu.VMEM((nx - 1, nz, piece, 128), full),
            pltpu.VMEM((nz - 1, piece, 128), full),
            pltpu.VMEM((strip, width // seq), full),
            pltpu.VMEM((4, most, 8, 128), full),
            dma((smalls,)),
            dma((smalls,)),
            dma((4, most - 1)),
            dma((4, most - 1)),
        ],
        compiler_params=pltpu.CompilerParams(vmem_limit_bytes=56 * 2**20, collective_id=1, has_side_effects=True),
        cost_estimate=pl.CostEstimate(flops=10**8, bytes_accessed=20 * 10**6, transcendentals=0),
        name="grad_sum",
    )(*(g.reshape(ny, 2, rows, width) for g in (up, down, mixer)), small)
    return large, summed.reshape(-1), jnp.sum(norm)


def row_gather(sizes, own, full, width, pieces, sems):
    a_send, a_recv, b_send, b_recv, c_send, c_recv, d_send, d_recv, e_send, e_recv = sems
    ny = sizes[0]
    rows = own.shape[0]
    half = width // 2
    size = half // pieces
    (y, c, _, _), sibling, at_y, _, _ = place_of(sizes)
    dp, seq = lax.axis_index("dp"), lax.axis_index("seq")
    side = lax.rem(seq, 2)
    pair = (dp, seq + 1 - 2 * side)

    def at_rows(d):
        return pl.ds(pl.multiple_of(d * rows, rows), rows)

    def at_cols(which, p):
        return pl.ds(pl.multiple_of(which * half + p * size, size), size)

    def core_copy():
        return remote(own, full.at[at_rows(dp)], a_send.at[0], a_recv.at[0], sibling)

    def y_copy(i, p):
        _, device = at_y(i)
        cols = at_cols(side, p)
        return remote(own.at[:, cols], full.at[at_rows(dp), cols], b_send.at[i - 1, p], b_recv.at[ny - 1 - i, p], device)

    def pass_on(i, p, which, send, recv, device):
        other, _ = at_y(ny - i)
        part = full.at[at_rows(other * 2 + c), at_cols(which, p)]
        return remote(part, part, send.at[ny - 1 - i, p], recv.at[ny - 1 - i, p], device)

    def x_copy(i, p):
        return pass_on(i, p, side, c_send, c_recv, pair)

    def first_copy(i, p):
        return pass_on(i, p, side, d_send, d_recv, sibling)

    def second_copy(i, p):
        return pass_on(i, p, 1 - side, e_send, e_recv, sibling)

    every = [(i, p) for p in range(pieces) for i in range(1, ny)]

    def start():
        for i, p in every:
            y_copy(i, p).start()
        core_copy().start()

    def first_half(p):
        for i in range(1, ny):
            y_copy(i, p).wait_recv()
            x_copy(i, p).start()
            first_copy(i, p).start()

    def second_half(p):
        for i in range(1, ny):
            x_copy(i, p).wait_recv()
            second_copy(i, p).start()

    def finish():
        core_copy().wait()
        for i, p in every:
            y_copy(i, p).wait_send()
            x_copy(i, p).wait_send()
            first_copy(i, p).wait()
            second_copy(i, p).wait()

    return start, first_half, second_half, finish


def gather_sems(sizes, pieces):
    dma = pltpu.SemaphoreType.DMA
    return [dma((1,))] * 2 + [dma((sizes[0] - 1, pieces))] * 8


GATHER = 10


def greet_near(sizes, count):
    _, sibling, at_y, _, _ = place_of(sizes)
    dp, me = lax.axis_index("dp"), lax.axis_index("seq")
    others = [(dp, lax.rem(me + i, count)) for i in range(1, count)]
    greet([sibling] + [at_y(i)[1] for i in range(1, sizes[0])] + others)
    return others


def open_kernel(sizes, count, pieces, mixer, mlp, tok, first, w_in, w_out, up_out, down_out, before, firsts,
                own, mlp_in, mlp_sem, halo_send, halo_recv, first_send, first_recv, *sems):
    rows = own.shape[0]
    lane_count = own.shape[1]
    me, dp = lax.axis_index("seq"), lax.axis_index("dp")
    chunk = mlp_in.shape[2]
    chunks = rows // chunk

    def load(k):
        return pltpu.make_async_copy(mlp.at[:, k * chunk : (k + 1) * chunk], mlp_in.at[k % 2], mlp_sem.at[k % 2])

    load(0).start()
    own[...] = mixer[:, :lane_count].astype(jnp.bfloat16)
    others = greet_near(sizes, count)
    start, first_half, second_half, finish = row_gather(sizes, own, w_in, lane_count, pieces, sems)
    start()
    halo = remote(tok.at[tok.shape[0] - HALO :], before, halo_send, halo_recv, others[0])
    halo.start()
    announced = [
        remote(first, firsts.at[me], first_send.at[i], first_recv.at[count - 2 - i], device) for i, device in enumerate(others)
    ]
    for copy in announced:
        copy.start()
    firsts[me] = first[...]
    w_in[pl.ds(pl.multiple_of(dp * rows, rows), rows), :] = own[...]
    w_out[...] = mixer[:, lane_count:].astype(jnp.bfloat16)
    for k in range(max(chunks, pieces)):
        if k < chunks:
            if k + 1 < chunks:
                load(k + 1).start()
            load(k).wait()
            at = slice(k * chunk, (k + 1) * chunk)
            up_out[at] = mlp_in[k % 2, 0].astype(jnp.bfloat16)
            down_out[at] = mlp_in[k % 2, 1].astype(jnp.bfloat16)
        if k < pieces:
            first_half(k)
        if 2 <= k < pieces:
            second_half(k - 2)
    for k in range(max(0, pieces - 2), pieces):
        second_half(k)
    halo.wait()
    for copy in announced:
        copy.wait()
    finish()


def open_gather(mixer, mlp, tok, first, count):
    sizes = axis_sizes()
    rows, total = mixer.shape
    width = tok.shape[1]
    lane_count = total - width
    dp = 2 * sizes[0]
    pieces = 6
    half = jnp.bfloat16
    dma = pltpu.SemaphoreType.DMA
    chunk = rows // 4
    first = jnp.broadcast_to(first.reshape(1, 1), (8, 128))
    return pl.pallas_call(
        functools.partial(open_kernel, sizes, count, pieces),
        out_shape=(
            jax.ShapeDtypeStruct((rows * dp, lane_count), half),
            jax.ShapeDtypeStruct((rows, width), half),
            jax.ShapeDtypeStruct(mlp.shape[1:], half),
            jax.ShapeDtypeStruct(mlp.shape[1:], half),
            jax.ShapeDtypeStruct((HALO, width), half),
            jax.ShapeDtypeStruct((count, 8, 128), jnp.int32),
        ),
        in_specs=[VMEM_SPEC, pl.BlockSpec(memory_space=pl.ANY), VMEM_SPEC, VMEM_SPEC],
        out_specs=(VMEM_SPEC,) * 6,
        scratch_shapes=[
            pltpu.VMEM((rows, lane_count), half),
            pltpu.VMEM((2, 2, chunk, mlp.shape[2]), jnp.float32),
            dma((2,)),
            dma,
            dma,
            dma((count - 1,)),
            dma((count - 1,)),
        ]
        + gather_sems(sizes, pieces),
        compiler_params=pltpu.CompilerParams(vmem_limit_bytes=48 * 2**20, collective_id=3, has_side_effects=True),
        cost_estimate=pl.CostEstimate(flops=10**6, bytes_accessed=60 * 10**6, transcendentals=0),
        name="open_gather",
    )(mixer, mlp, tok, first)


def swap_kernel(sizes, pieces, value, own, swapped, full, swap_send, swap_recv, self_sem, *sems):
    count = value.shape[0]
    rows = own.shape[0]
    me, dp = lax.axis_index("seq"), lax.axis_index("dp")
    others = greet_near(sizes, count)
    start, first_half, second_half, finish = row_gather(sizes, own, full, own.shape[1], pieces, sems)
    start()
    copies = [
        remote(value.at[device[1]], swapped.at[me], swap_send.at[i], swap_recv.at[count - 2 - i], device)
        for i, device in enumerate(others)
    ]
    for copy in copies:
        copy.start()
    kept = [
        pltpu.make_async_copy(value.at[me], swapped.at[me], self_sem.at[0]),
        pltpu.make_async_copy(own, full.at[pl.ds(pl.multiple_of(dp * rows, rows), rows)], self_sem.at[1]),
    ]
    for copy in kept:
        copy.start()
    for p in range(pieces):
        first_half(p)
        if p > 0:
            second_half(p - 1)
    second_half(pieces - 1)
    for copy in kept + copies:
        copy.wait()
    finish()


def swap_with_rows(value, own, number):
    sizes = axis_sizes()
    count = value.shape[0]
    rows, width = own.shape
    pieces = 4
    dma = pltpu.SemaphoreType.DMA
    hbm = pl.BlockSpec(memory_space=pl.ANY)
    return pl.pallas_call(
        functools.partial(swap_kernel, sizes, pieces),
        out_shape=(
            jax.ShapeDtypeStruct(value.shape, value.dtype),
            jax.ShapeDtypeStruct((rows * 2 * sizes[0], width), own.dtype),
        ),
        in_specs=[hbm, VMEM_SPEC],
        out_specs=(hbm, hbm),
        scratch_shapes=[dma((count - 1,)), dma((count - 1,)), dma((2,))] + gather_sems(sizes, pieces),
        compiler_params=pltpu.CompilerParams(vmem_limit_bytes=16 * 2**20, collective_id=number, has_side_effects=True),
        cost_estimate=pl.CostEstimate(flops=10**6, bytes_accessed=40 * 10**6, transcendentals=0),
        name="swap_with_rows",
    )(value, own)


def swap_filter_kernel(value, features, first, last, codes, swapped, filt, swap_send, swap_recv, self_sem):
    count = value.shape[0]
    me, dp = lax.axis_index("seq"), lax.axis_index("dp")
    others = [(dp, lax.rem(me + i, count)) for i in range(1, count)]
    greet(others)
    copies = [
        remote(value.at[device[1]], swapped.at[me], swap_send.at[i], swap_recv.at[count - 2 - i], device)
        for i, device in enumerate(others)
    ]
    for copy in copies:
        copy.start()
    kept = pltpu.make_async_copy(value.at[me], swapped.at[me], self_sem)
    kept.start()
    rates = jnp.exp2(-codes[...].astype(jnp.float32))
    total = jnp.zeros_like(rates)
    step = 2 * PIECE
    for start in range(0, filt.shape[0], step):
        hidden = jnp.sin(jnp.dot(features[start : start + step], first[...], precision=highest, preferred_element_type=jnp.float32))
        raw = jnp.dot(hidden, last[...], precision=highest, preferred_element_type=jnp.float32)
        places = (lax.broadcasted_iota(jnp.int32, raw.shape, 0) + start).astype(jnp.float32)
        shaped = raw * jnp.exp(-places * rates)
        total = total + jnp.sum(shaped * shaped, axis=0, keepdims=True)
        filt[start : start + step] = shaped
    scale = lax.rsqrt(total + norm_eps)
    for start in range(0, filt.shape[0], step):
        filt[start : start + step] = filt[start : start + step] * scale
    kept.wait()
    for copy in copies:
        copy.wait()


def swap_with_filter(value, first, last, codes, length):
    count = value.shape[0]
    dma = pltpu.SemaphoreType.DMA
    hbm = pl.BlockSpec(memory_space=pl.ANY)
    places = np.arange(length, dtype=np.float32)[:, None]
    bands = np.arange(1, (first.shape[0] - 1) // 2 + 1, dtype=np.float32)[None, :]
    angles = (np.float32(2.0 * math.pi / length) * places * bands).astype(np.float32)
    features = np.concatenate([places / np.float32(length), np.cos(angles), np.sin(angles)], axis=1).astype(np.float32)
    return pl.pallas_call(
        swap_filter_kernel,
        out_shape=(
            jax.ShapeDtypeStruct(value.shape, value.dtype),
            jax.ShapeDtypeStruct((length, last.shape[1]), jnp.float32),
        ),
        in_specs=[hbm] + [VMEM_SPEC] * 4,
        out_specs=(hbm, VMEM_SPEC),
        scratch_shapes=[dma((count - 1,)), dma((count - 1,)), dma],
        compiler_params=pltpu.CompilerParams(vmem_limit_bytes=32 * 2**20, collective_id=4, has_side_effects=True),
        cost_estimate=pl.CostEstimate(flops=10**8, bytes_accessed=10 * 10**6, transcendentals=10**6),
        name="swap_with_filter",
    )(value, jnp.asarray(features), first, last, codes.reshape(1, -1))


def contract_rows(left, right):
    return lax.dot_general(
        left, right, (((0,), (0,)), ((), ())), preferred_element_type=jnp.float32
    )


def block_specs(shapes):
    return [pl.BlockSpec(shape, lambda j, n=len(shape): (0,) * n, pipeline_mode=pl.Buffered(1)) for shape in shapes]


def normalized(values):
    center = jnp.mean(values, axis=-1, keepdims=True)
    centred = values - center
    scale = lax.rsqrt(jnp.mean(centred * centred, axis=-1, keepdims=True) + norm_eps)
    return centred * scale, scale


def norm_back(grad, gain, scaled, scale):
    inner = grad * gain
    mean_inner = jnp.mean(inner, axis=-1, keepdims=True)
    mean_scaled = jnp.mean(inner * scaled, axis=-1, keepdims=True)
    return scale * (inner - mean_inner - scaled * mean_scaled)


def dot_cols(left, right):
    return lax.dot_general(left, right, (((1,), (1,)), ((), ())), preferred_element_type=jnp.float32)


LANES = 128
HALO = 8


def project_kernel(tok, before, prev, gain, w_v, w_one, w_zero, t_v, t_one, t_zero,
                   conv_in, factors, zero_out, projs, normed_out, normed, held):
    rows = tok.shape[0]
    keep = prev[0].astype(jnp.float32)

    @pl.when(pl.program_id(0) == 0)
    def _():
        scaled, _ = normalized(before[...].astype(jnp.float32))
        normed[:HALO] = (scaled * gain[...]).astype(jnp.bfloat16)
        for start in range(0, rows, PIECE):
            at = slice(start, start + PIECE)
            scaled, _ = normalized(tok[at].astype(jnp.float32))
            value = (scaled * gain[...]).astype(jnp.bfloat16)
            normed[start + HALO : start + PIECE + HALO] = value
            normed_out[at] = value

    shorts = []
    for i, (w, taps) in enumerate(((w_v, t_v), (w_one, t_one), (w_zero, t_zero))):
        proj = dot32(normed[...], w[...]).astype(jnp.bfloat16)
        projs[i] = proj
        held[...] = proj.astype(jnp.float32)
        held[:HALO] = held[:HALO] * keep
        shorts.append(
            taps[0:1] * held[HALO : HALO + rows]
            + taps[1:2] * held[HALO - 1 : HALO - 1 + rows]
            + taps[2:3] * held[HALO - 2 : HALO - 2 + rows]
        )
    factors[0] = shorts[1]
    factors[1] = shorts[0]
    zero_out[...] = shorts[2]
    product = (shorts[0] * shorts[1]).astype(jnp.bfloat16)
    for i in range(conv_in.shape[0]):
        conv_in[i] = product[:, i * LANES : (i + 1) * LANES]


def project(tok, before, has_prev, gain, w_in, taps):
    rows, width = tok.shape
    size = 256
    steps = width // size
    col = lambda part: (lambda j: (0, part * steps + j))
    parts = [pl.BlockSpec((width, size), col(i)) for i in range(3)]
    tap_parts = [pl.BlockSpec((3, size), col(i)) for i in range(3)]
    wide = lambda n, dtype: jax.ShapeDtypeStruct((n, width), dtype)
    stack = lambda m, n: pl.BlockSpec((m, n, size), lambda j: (0, 0, j))
    return pl.pallas_call(
        project_kernel,
        grid=(steps,),
        out_shape=[jax.ShapeDtypeStruct((width // LANES, rows, LANES), jnp.bfloat16)]
        + [jax.ShapeDtypeStruct((2, rows, width), jnp.float32), wide(rows, jnp.float32)]
        + [jax.ShapeDtypeStruct((3, rows + HALO, width), jnp.bfloat16), wide(rows, jnp.bfloat16)],
        in_specs=block_specs([(rows, width), (HALO, width)]) + [SMEM_SPEC] + block_specs([(1, width)]) + parts + tap_parts,
        out_specs=[pl.BlockSpec((size // LANES, rows, LANES), lambda j: (j, 0, 0))]
        + [stack(2, rows), pl.BlockSpec((rows, size), lambda j: (0, j)), stack(3, rows + HALO)]
        + block_specs([(rows, width)]),
        scratch_shapes=[pltpu.VMEM((rows + HALO, width), jnp.bfloat16), pltpu.VMEM((rows + HALO, size), jnp.float32)],
        compiler_params=pltpu.CompilerParams(vmem_limit_bytes=48 * 2**20),
        cost_estimate=pl.CostEstimate(flops=6 * rows * width * width, bytes_accessed=20 * 10**6, transcendentals=0),
        name="project",
    )(tok, before, has_prev, gain, w_in, w_in, w_in, taps, taps, taps)


def mlp_kernel(conv, conv_in, zero, tok, cot, skip, gain, w_out, w_up, w_down,
               output, act_out, up_out, gated, normed, d_resid, branch_out, conv_grad, d_mixed, d_zero, d_gain, d_skip,
               resid, down, d_normed):
    rows, width = tok.shape
    groups = width // LANES
    step = pl.program_id(0)

    @pl.when(step == 0)
    def _():
        for g in range(groups):
            at = slice(g * LANES, (g + 1) * LANES)
            mixed = conv[g].astype(jnp.float32) + skip[:, at] * conv_in[g].astype(jnp.float32)
            gated[:, at] = (zero[:, at] * mixed).astype(jnp.bfloat16)
        resid[...] = tok[...].astype(jnp.float32) + dot_cols(gated[...], w_out[...])
        for start in range(0, rows, PIECE):
            at = slice(start, start + PIECE)
            scaled, _ = normalized(resid[at])
            normed[at] = (scaled * gain[...]).astype(jnp.bfloat16)

    up = dot32(normed[...], w_up[...])
    d_act = dot32(cot[...], w_down[...])
    root = math.sqrt(2.0 / math.pi)
    square = up * up
    bent = jnp.tanh(root * up * (1.0 + 0.044715 * square))
    act = (0.5 * up * (1.0 + bent)).astype(jnp.bfloat16)
    slope = 0.5 * (1.0 + bent) + (0.5 * root) * up * (1.0 - bent * bent) * (1.0 + (3.0 * 0.044715) * square)
    g_up = (slope * d_act).astype(jnp.bfloat16)
    act_out[...] = act
    up_out[...] = g_up
    down_part = dot_cols(act, w_down[...])
    normed_part = dot_cols(g_up, w_up[...])

    @pl.when(step == 0)
    def _():
        down[...] = down_part
        d_normed[...] = normed_part

    @pl.when(step > 0)
    def _():
        down[...] += down_part
        d_normed[...] += normed_part

    @pl.when(step == pl.num_programs(0) - 1)
    def _():
        gain_sum = jnp.zeros((1, width), jnp.float32)
        for start in range(0, rows, PIECE):
            at = slice(start, start + PIECE)
            output[at] = (resid[at] + down[at]).astype(jnp.bfloat16)
            scaled, scale = normalized(resid[at])
            grad = d_normed[at]
            gain_sum = gain_sum + jnp.sum(grad * scaled, axis=0, keepdims=True)
            total = cot[at].astype(jnp.float32) + norm_back(grad, gain[...], scaled, scale)
            d_resid[at] = total
            branch_out[at] = total.astype(jnp.bfloat16)
        d_gain[...] = gain_sum
        down[...] = dot32(branch_out[...], w_out[...])
        for g in range(groups):
            at = slice(g * LANES, (g + 1) * LANES)
            source = conv_in[g].astype(jnp.float32)
            mixed = conv[g].astype(jnp.float32) + skip[:, at] * source
            d_gated = down[:, at]
            d_zero[:, at] = (d_gated * mixed).astype(jnp.bfloat16)
            grad = d_gated * zero[:, at]
            d_mixed[g] = grad
            conv_grad[g] = grad.astype(jnp.bfloat16)
            d_skip[:, at] = jnp.sum(grad * source, axis=0, keepdims=True)


def mlp_block(conv, conv_in, zero, tok, cot, skip, gain, w_out, w_up, w_down):
    rows, width = tok.shape
    hidden = w_down.shape[1]
    size = 512
    steps = hidden // size
    groups = width // LANES
    flat = lambda dtype: jax.ShapeDtypeStruct((rows, width), dtype)
    cut = lambda dtype: jax.ShapeDtypeStruct((groups, rows, LANES), dtype)
    row = jax.ShapeDtypeStruct((1, width), jnp.float32)
    big = jax.ShapeDtypeStruct((rows, hidden), jnp.bfloat16)
    half, full = jnp.bfloat16, jnp.float32
    ends = [flat(half), flat(half), flat(full), flat(half), cut(half), cut(full), flat(half), row, row]
    tile = pl.BlockSpec((rows, size), lambda j: (0, j))
    one = block_specs([(rows, width)])
    return pl.pallas_call(
        mlp_kernel,
        grid=(steps,),
        out_shape=[flat(half), big, big] + ends,
        in_specs=block_specs([conv.shape, conv.shape, zero.shape, tok.shape, cot.shape, (1, width), (1, width), w_out.shape])
        + [pl.BlockSpec((width, size), index) for index in (lambda j: (0, j),) * 2],
        out_specs=one + [tile, tile] + block_specs([e.shape for e in ends]),
        scratch_shapes=[pltpu.VMEM((rows, width), full)] * 3,
        compiler_params=pltpu.CompilerParams(vmem_limit_bytes=60 * 2**20),
        cost_estimate=pl.CostEstimate(flops=8 * rows * width * hidden + 4 * rows * width * width, bytes_accessed=50 * 10**6, transcendentals=rows * hidden),
        name="mlp_block",
    )(conv, conv_in, zero, tok, cot, skip, gain, w_out, w_up, w_down)


def project_back_kernel(back, d_mixed, other, d_zero, proj, after, prev, nxt, skip, taps, w_in, normed, branch, gated, tok, d_resid, gain,
                        d_mixer, d_taps, tokens_grad, d_gain, normed_t, branch_t, d_normed, held, wide_proj):
    rows = tok.shape[0]
    size = held.shape[1]
    step = pl.program_id(0)
    steps = pl.num_programs(0)
    part = step // (steps // 4)

    @pl.when(step == 0)
    def _():
        d_normed[...] = jnp.zeros_like(d_normed)
        normed_t[...] = normed[...].T
        branch_t[...] = branch[...].T

    def spread(ref):
        return jnp.concatenate([ref[i].astype(jnp.float32) for i in range(ref.shape[0])], axis=1)

    @pl.when(part < 2)
    def _():
        d_conv_in = skip[...] * spread(d_mixed) + spread(back)
        held[:rows] = (d_conv_in * other[...]).astype(jnp.bfloat16).astype(jnp.float32)

    @pl.when(part == 2)
    def _():
        held[:rows] = d_zero[...].astype(jnp.float32)

    @pl.when(part < 3)
    def _():
        held[rows:] = after[...].astype(jnp.float32) * nxt[0].astype(jnp.float32)
        g_proj = (
            taps[0:1] * held[:rows] + taps[1:2] * held[1 : rows + 1] + taps[2:3] * held[2 : rows + 2]
        ).astype(jnp.bfloat16)
        wide_proj[...] = proj[...].astype(jnp.float32)
        wide_proj[:HALO] = wide_proj[:HALO] * prev[0].astype(jnp.float32)
        d_taps[...] = jnp.concatenate(
            [jnp.sum(held[:rows] * wide_proj[HALO - i : HALO - i + rows], axis=0, keepdims=True) for i in range(3)], axis=0
        )
        d_normed[...] += dot_cols(g_proj, w_in[...])
        d_mixer[...] = dot32(normed_t[...], g_proj).astype(jnp.bfloat16)

    @pl.when(part == 3)
    def _():
        d_mixer[...] = dot32(branch_t[...], gated[...]).astype(jnp.bfloat16)

    @pl.when(step == steps - 1)
    def _():
        gain_sum = jnp.zeros((1, tok.shape[1]), jnp.float32)
        for start in range(0, rows, PIECE):
            at = slice(start, start + PIECE)
            scaled, scale = normalized(tok[at].astype(jnp.float32))
            grad = d_normed[at]
            gain_sum = gain_sum + jnp.sum(grad * scaled, axis=0, keepdims=True)
            tokens_grad[at] = (d_resid[at] + norm_back(grad, gain[...], scaled, scale)).astype(jnp.bfloat16)
        d_gain[...] = gain_sum


def project_back(back, d_mixed, shorts, d_zero, projs, after, has_prev, has_next, skip, taps, w_in, normed, branch, gated, tok, d_resid, gain):
    rows, width = tok.shape
    size = 512
    per = width // size
    steps = 4 * per
    half = jnp.bfloat16
    lane = lambda j: lax.rem(j, per)
    inner = lambda j: jnp.minimum(j, 3 * per - 1)
    group = pl.BlockSpec((size // LANES, rows, LANES), lambda j: (lane(j), 0, 0))
    third = lambda n: pl.BlockSpec((n, size), lambda j: (0, inner(j)))
    tile = pl.BlockSpec((rows, size), lambda j: (0, lane(j)))
    return pl.pallas_call(
        project_back_kernel,
        grid=(steps,),
        out_shape=[
            jax.ShapeDtypeStruct((width, 4 * width), half),
            jax.ShapeDtypeStruct((3, 3 * width), jnp.float32),
            jax.ShapeDtypeStruct((rows, width), half),
            jax.ShapeDtypeStruct((1, width), jnp.float32),
        ],
        in_specs=[group, group, pl.BlockSpec((None, rows, size), lambda j: (jnp.minimum(j // per, 1), 0, lane(j))), tile]
        + [pl.BlockSpec((None, rows + HALO, size), lambda j: (jnp.minimum(j // per, 2), 0, lane(j)))]
        + [third(HALO), SMEM_SPEC, SMEM_SPEC, pl.BlockSpec((1, size), lambda j: (0, lane(j))), third(3), third(width)]
        + block_specs([(rows, width)] * 2)
        + [tile]
        + block_specs([(rows, width)] * 2 + [(1, width)]),
        out_specs=[pl.BlockSpec((width, size), lambda j: (0, j)), third(3)] + block_specs([(rows, width), (1, width)]),
        scratch_shapes=[
            pltpu.VMEM((width, rows), half),
            pltpu.VMEM((width, rows), half),
            pltpu.VMEM((rows, width), jnp.float32),
            pltpu.VMEM((rows + HALO, size), jnp.float32),
            pltpu.VMEM((rows + HALO, size), jnp.float32),
        ],
        compiler_params=pltpu.CompilerParams(vmem_limit_bytes=60 * 2**20),
        cost_estimate=pl.CostEstimate(flops=14 * rows * width * width, bytes_accessed=50 * 10**6, transcendentals=0),
        name="project_back",
    )(back, d_mixed, shorts, d_zero, projs, after, has_prev, has_next, skip, taps, w_in, normed, branch, gated, tok, d_resid, gain)


def adam_update(master, moment, square, grad, factor, rate, decay):
    clipped = grad * factor
    moment_new = beta_one * moment + (1.0 - beta_one) * clipped
    square_new = beta_two * square + (1.0 - beta_two) * clipped * clipped
    moment_hat = moment_new / (1.0 - beta_one**ADAM_STEP)
    square_hat = square_new / (1.0 - beta_two**ADAM_STEP)
    master_new = master - rate * (moment_hat / (jnp.sqrt(square_hat) + adam_eps) + decay * master)
    return (master_new, moment_new, square_new)


def on_device(
    tokens,
    cotangent,
    seq_first,
    decay_code,
    mixer_master,
    mixer_moment,
    mixer_square,
    mlp_master,
    mlp_moment,
    mlp_square,
    channel_master,
    channel_moment,
    channel_square,
    filter_in_master,
    filter_in_moment,
    filter_in_square,
    filter_out_master,
    filter_out_moment,
    filter_out_square,
):
    block_rows = tokens.shape[1]
    model_width = tokens.shape[2]
    lane_count = 3 * model_width
    per = block_rows // PIECE
    seq_count = lax.axis_size("seq")
    long_blocks = max(seq_count // 4, 4)
    length = long_blocks * block_rows
    own_width = model_width // seq_count
    seq_index = lax.axis_index("seq")
    w_in, out_own, up_own, down_own, before, first_tiles = open_gather(
        mixer_master, mlp_master, tokens[0], seq_first, seq_count
    )
    firsts = first_tiles[:, 0, 0]
    w_out = lax.all_gather(out_own, "dp", axis=0, tiled=True)
    w_down = lax.all_gather(down_own, "dp", axis=0, tiled=True)
    blocks = jnp.arange(seq_count, dtype=jnp.int32)
    same = firsts[None, :] == firsts[:, None]
    lasts = jnp.max(jnp.where(same, blocks[None, :], 0), axis=1).astype(jnp.int32)
    own_first = firsts[seq_index]
    has_prev = (seq_index - own_first >= 1).astype(jnp.int32).reshape(1)
    has_next = (lasts[seq_index] > seq_index).astype(jnp.int32).reshape(1)
    conv_taps = channel_master[:, :lane_count]
    gain_one = channel_master[0:1, lane_count:]
    gain_two = channel_master[1:2, lane_count:]
    skip_gain = channel_master[2:3, lane_count:]
    own_codes = lax.dynamic_slice_in_dim(decay_code, seq_index * own_width, own_width, 0)
    own_last = lax.dynamic_slice_in_dim(filter_out_master, seq_index * own_width, own_width, 1)
    conv_input, factors, x_zero, projs, normed_b = project(tokens[0], before, has_prev, gain_one, w_in, conv_taps)
    swapped, filt = swap_with_filter(
        channel_order(conv_input, seq_count), filter_in_master, own_last, own_codes, length
    )
    pieces = swapped.reshape(seq_count * per, PIECE, own_width)
    conv_out = conv_forward(firsts, pieces, filt, per)
    conv, w_up = swap_with_rows(conv_out.reshape(seq_count, block_rows, own_width), up_own, 5)
    conv = lane_order(conv)
    (
        output, act_b, grad_up_b, gated_b, normed_two_b, d_resid, grad_branch_b, conv_grad, d_mixed, d_x_zero, d_gain_two, d_skip,
    ) = mlp_block(conv, conv_input, x_zero, tokens[0], cotangent[0], skip_gain, gain_two, w_out, w_up, w_down)
    grad_pieces = to_channels(conv_grad, seq_count).reshape(seq_count * per, PIECE, own_width)
    up_grad_b = contract_rows(normed_two_b, grad_up_b).astype(jnp.bfloat16)
    down_grad_b = contract_rows(cotangent[0], act_b).astype(jnp.bfloat16)
    conv_in_grad, filt_grad = conv_backward(firsts, lasts, pieces, grad_pieces, filt, per)
    back = to_tokens(conv_in_grad.reshape(seq_count, block_rows, own_width))
    head_grad = skip_gain.reshape(-1, 1, LANES) * d_mixed[:, :HALO] + back[:, :HALO].astype(jnp.float32)
    head_grad = head_grad.transpose(1, 0, 2).reshape(HALO, model_width)
    head = [head_grad * factors[0, :HALO], head_grad * factors[1, :HALO], d_x_zero[:HALO].astype(jnp.float32)]
    after = passed_along(jnp.concatenate(head, axis=1).astype(jnp.bfloat16), "seq", -1)
    _, filter_pull = jax.vjp(
        lambda first, last: make_filter(first, last, own_codes, length), filter_in_master, own_last
    )
    first_grad, own_last_grad = filter_pull(filt_grad)
    last_grad = lax.dynamic_update_slice_in_dim(
        jnp.zeros_like(filter_out_master), own_last_grad, seq_index * own_width, 1
    )
    mixer_grad_b, d_taps, tokens_grad, d_gain_one = project_back(
        back, d_mixed, factors, d_x_zero, projs, after, has_prev, has_next, skip_gain, conv_taps, w_in,
        normed_b, grad_branch_b, gated_b, tokens[0], d_resid, gain_one,
    )
    vectors = jnp.concatenate([d_gain_one, d_gain_two, d_skip], axis=0)
    channel_grad = jnp.concatenate([d_taps, vectors], axis=1)
    small_parts = (channel_grad, first_grad, last_grad)
    large_grads, small_sum, total = grad_sum(
        up_grad_b, down_grad_b, mixer_grad_b, jnp.concatenate([part.reshape(-1) for part in small_parts])
    )
    mlp_grad = large_grads[:2].astype(jnp.float32)
    mixer_grad = large_grads[2].astype(jnp.float32)
    ends = np.cumsum([part.size for part in small_parts])
    channel_grad, first_grad, last_grad = (
        small_sum[end - part.size : end].reshape(part.shape) for part, end in zip(small_parts, ends)
    )
    grad_norm = jnp.sqrt(total)
    factor = jnp.minimum(1.0, clip_limit / (grad_norm + 1e-06))
    mixer_new, mixer_moment_new, mixer_square_new = adam_update(
        mixer_master, mixer_moment, mixer_square, mixer_grad, factor, rate_matrix, weight_decay
    )
    mlp_new, mlp_moment_new, mlp_square_new = adam_update(
        mlp_master, mlp_moment, mlp_square, mlp_grad, factor, rate_matrix, weight_decay
    )
    channel_new, channel_moment_new, channel_square_new = adam_update(
        channel_master, channel_moment, channel_square, channel_grad, factor, rate_small, 0.0
    )
    filter_in_new, filter_in_moment_new, filter_in_square_new = adam_update(
        filter_in_master,
        filter_in_moment,
        filter_in_square,
        first_grad,
        factor,
        rate_small,
        weight_decay,
    )
    filter_out_new, filter_out_moment_new, filter_out_square_new = adam_update(
        filter_out_master,
        filter_out_moment,
        filter_out_square,
        last_grad,
        factor,
        rate_small,
        weight_decay,
    )
    return (
        output[None],
        tokens_grad[None],
        grad_norm.reshape(1),
        channel_grad,
        first_grad,
        last_grad,
        mixer_new,
        mixer_moment_new,
        mixer_square_new,
        mlp_new,
        mlp_moment_new,
        mlp_square_new,
        channel_new,
        channel_moment_new,
        channel_square_new,
        filter_in_new,
        filter_in_moment_new,
        filter_in_square_new,
        filter_out_new,
        filter_out_moment_new,
        filter_out_square_new,
    )


def solution(mesh):
    in_specs = (
        P("dp", "seq", None),
        P("dp", "seq", None),
        P("dp", "seq"),
        P(),
        P("dp", None),
        P("dp", None),
        P("dp", None),
        P(None, "dp", None),
        P(None, "dp", None),
        P(None, "dp", None),
        P(),
        P(),
        P(),
        P(),
        P(),
        P(),
        P(),
        P(),
        P(),
    )
    out_specs = (
        P("dp", "seq", None),
        P("dp", "seq", None),
        P(),
        P(),
        P(),
        P(),
        P("dp", None),
        P("dp", None),
        P("dp", None),
        P(None, "dp", None),
        P(None, "dp", None),
        P(None, "dp", None),
        P(),
        P(),
        P(),
        P(),
        P(),
        P(),
        P(),
        P(),
        P(),
    )
    return jax.shard_map(
        on_device, mesh=mesh, in_specs=in_specs, out_specs=out_specs, check_vma=False
    )
```

```python
import functools
import math

import jax
import jax.numpy as jnp
import numpy as np
from jax import lax
from jax.experimental import pallas as pl
from jax.experimental.pallas import tpu as pltpu
from jax.sharding import PartitionSpec as P

ADAM_STEP = 10


highest = lax.Precision.HIGHEST
norm_eps = 1e-05
clip_limit = 1.0
beta_one = 0.9
beta_two = 0.999
adam_eps = 1e-08
rate_matrix = 0.03
rate_small = 0.2
weight_decay = 0.1
PIECE = 128


def passed_along(value, axis, steps):
    count = lax.axis_size(axis)
    first, last = (max(0, -steps), min(count, count - steps))
    return lax.ppermute(value, axis, [(source, source + steps) for source in range(first, last)])


def filter_features(length, feature_count):
    places = jnp.arange(length, dtype=jnp.float32)[:, None]
    bands = jnp.arange(1, (feature_count - 1) // 2 + 1, dtype=jnp.float32)[None, :]
    angles = 2.0 * math.pi / length * places * bands
    return jnp.concatenate([places / length, jnp.cos(angles), jnp.sin(angles)], axis=1)


def make_filter(first_weight, last_weight, decay_code, length):
    features = filter_features(length, first_weight.shape[0])
    hidden = jnp.sin(jnp.dot(features, first_weight, precision=highest))
    raw_filter = jnp.dot(hidden, last_weight, precision=highest)
    rates = jnp.exp2(-decay_code.astype(jnp.float32))
    places = jnp.arange(length, dtype=jnp.float32)[:, None]
    shaped = raw_filter * jnp.exp(-places * rates[None, :])
    return shaped * lax.rsqrt(jnp.sum(shaped * shaped, axis=0, keepdims=True) + norm_eps)


def odd_tables(parts):
    freq = np.arange(PIECE)[:, None] * 2 + 1
    sample = np.arange(PIECE)[None, :]
    angles = (freq * sample % (4 * PIECE)) * (2.0 * math.pi / (4 * PIECE))
    pair = np.stack([np.cos(angles), -np.sin(angles)]).reshape(2, parts, PIECE // parts, PIECE)
    table = pair.transpose(1, 0, 2, 3).reshape(parts, 2 * PIECE // parts, PIECE).astype(np.float32)
    upper = table.astype(jnp.bfloat16)
    lower = (table - upper.astype(np.float32)).astype(jnp.bfloat16)
    swap = (0, 2, 1)
    forward = np.concatenate([upper, lower, upper], axis=2)
    backward = np.concatenate([upper.transpose(swap), lower.transpose(swap)], axis=1)
    return jnp.asarray(forward), jnp.asarray(backward)


def dot32(left, right):
    return jnp.dot(left, right, preferred_element_type=jnp.float32)


def split_two(value):
    upper = value.astype(jnp.bfloat16)
    return upper, (value - upper.astype(jnp.float32)).astype(jnp.bfloat16)


def freq_signs(rows, width):
    places = lax.broadcasted_iota(jnp.int32, (rows, width), 0)
    return 1.0 - 2.0 * (places % 2).astype(jnp.float32)


def side_by_side(ref, p, count):
    return jnp.concatenate([ref[p + i] for i in range(count)], axis=1)


def in_groups(count, body):
    size = 8

    def one(i, carry):
        for j in range(0, size, 2):
            body(i * size + j)
        return carry

    lax.fori_loop(0, count // size, one, 0)


def to_freq(table, ref, out, count, factor):
    lanes = ref.shape[2]

    def body(p):
        data = side_by_side(ref, p, 2)
        spec = dot32(table[:, : 2 * PIECE], jnp.concatenate([data, data], axis=0))
        if factor != 1.0:
            spec = spec * factor
        out[p] = spec[:, :lanes]
        out[p + 1] = spec[:, lanes:]

    in_groups(count, body)


def filter_spectrum(filt_ref, table, h_ref):
    half = table.shape[0] // 2
    lanes = filt_ref.shape[1]
    signs = freq_signs(half, lanes)
    prev = None
    for k in range(0, filt_ref.shape[0] // PIECE, 2):
        data = jnp.concatenate([filt_ref[i * PIECE : (i + 1) * PIECE, :] for i in (k, k + 1)], axis=1)
        upper, lower = split_two(data)
        both = dot32(table, jnp.concatenate([upper, upper, lower], axis=0))
        for i in range(2):
            spec = both[:, i * lanes : (i + 1) * lanes]
            if prev is None:
                h_ref[0] = spec
            else:
                h_ref[k + i, :half] = spec[:half] - signs * prev[half:]
                h_ref[k + i, half:] = spec[half:] + signs * prev[:half]
            prev = spec


def to_time(table, ref, count, factor, store):
    lanes = ref.shape[2]

    def body(p):
        value = dot32(table[:PIECE], side_by_side(ref, p, 2).astype(jnp.bfloat16))
        if factor != 1.0:
            value = value * factor
        store(p, value[:, :lanes])
        store(p + 1, value[:, lanes:])

    in_groups(count, body)


def emitter(part, parts, out_ref, acc_ref):
    def store(p, value):
        if parts == 1:
            out_ref[p] = value.astype(out_ref.dtype)
            return
        total = value if part == 0 else acc_ref[p] + value
        if part == parts - 1:
            out_ref[p] = total.astype(out_ref.dtype)
        else:
            acc_ref[p] = total

    return store


def conv_forward_kernel(per, first_ref, x_ref, filt_ref, f_ref, i_ref, o_ref, xs, hs, *rest):
    count, _, lanes = x_ref.shape
    blocks = count // per
    parts = f_ref.shape[0]
    half = PIECE // parts
    tiles = half // 8
    for part in range(parts):
        filter_spectrum(filt_ref, f_ref[part], hs)
        to_freq(f_ref[part], x_ref, xs, count, 1.0)

        def one_tile(step, carry):
            b = blocks - 1 - step // tiles
            row = pl.multiple_of((step % tiles) * 8, 8)
            re = pl.ds(row, 8)
            im = pl.ds(row + half, 8)

            def add_pairs(acc, a, lag, diagonal):
                acc = list(acc)
                for j in range(per):
                    sr, si = xs[a * per + j, re], xs[a * per + j, im]
                    for i in range(j if diagonal else 0, per):
                        hr, hi = hs[lag + i - j, re], hs[lag + i - j, im]
                        acc[2 * i] = acc[2 * i] + (sr * hr - si * hi)
                        acc[2 * i + 1] = acc[2 * i + 1] + (sr * hi + si * hr)
                return tuple(acc)

            acc = tuple(jnp.zeros((8, lanes), jnp.float32) for _ in range(2 * per))
            acc = add_pairs(acc, b, 0, True)
            acc = lax.fori_loop(first_ref[b], b, lambda a, c: add_pairs(c, a, (b - a) * per, False), acc)
            for i in range(per):
                xs[b * per + i, re] = acc[2 * i]
                xs[b * per + i, im] = acc[2 * i + 1]
            return carry

        lax.fori_loop(0, blocks * tiles, one_tile, 0)
        to_time(i_ref[part], xs, count, 1.0 / PIECE, emitter(part, parts, o_ref, rest[0] if rest else None))


def conv_backward_kernel(
    per, first_ref, last_ref, x_ref, g_ref, filt_ref, f_ref, i_ref, dx_ref, df_ref, xs, gs, hs, dh, *rest
):
    count, _, lanes = x_ref.shape
    blocks = count // per
    taps = filt_ref.shape[0] // PIECE
    parts = f_ref.shape[0]
    half = PIECE // parts
    tiles = half // 8
    for part in range(parts):
        filter_spectrum(filt_ref, f_ref[part], hs)
        to_freq(f_ref[part], x_ref, xs, count, 1.0)
        to_freq(f_ref[part], g_ref, gs, count, 1.0 / PIECE)
        dh[...] = jnp.zeros_like(dh)

        def one_tile(step, carry):
            a = step // tiles
            row = pl.multiple_of((step % tiles) * 8, 8)
            re = pl.ds(row, 8)
            im = pl.ds(row + half, 8)

            def add_pairs(acc, b, lag, diagonal):
                acc = list(acc)
                for delta in range(0 if diagonal else 1 - per, per):
                    hr, hi = hs[lag + delta, re], hs[lag + delta, im]
                    tr, ti = dh[lag + delta, re], dh[lag + delta, im]
                    for j in range(max(0, -delta), per - max(0, delta)):
                        sr, si = xs[a * per + j, re], xs[a * per + j, im]
                        gr, gi = gs[b * per + j + delta, re], gs[b * per + j + delta, im]
                        acc[2 * j] = acc[2 * j] + (hr * gr + hi * gi)
                        acc[2 * j + 1] = acc[2 * j + 1] + (hr * gi - hi * gr)
                        tr = tr + (sr * gr + si * gi)
                        ti = ti + (sr * gi - si * gr)
                    dh[lag + delta, re] = tr
                    dh[lag + delta, im] = ti
                return tuple(acc)

            acc = tuple(jnp.zeros((8, lanes), jnp.float32) for _ in range(2 * per))
            acc = add_pairs(acc, a, 0, True)
            acc = lax.fori_loop(a + 1, last_ref[a] + 1, lambda b, c: add_pairs(c, b, (b - a) * per, False), acc)
            for j in range(per):
                xs[a * per + j, re] = acc[2 * j]
                xs[a * per + j, im] = acc[2 * j + 1]
            return carry

        lax.fori_loop(0, blocks * tiles, one_tile, 0)
        to_time(i_ref[part], xs, count, 1.0, emitter(part, parts, dx_ref, rest[0] if rest else None))
        signs = freq_signs(half, lanes)
        back_u, back_l = i_ref[part, :PIECE], i_ref[part, PIECE:]
        for k in range(taps):
            grad = dh[k]
            if k + 1 < taps:
                grad = grad + jnp.concatenate([signs * dh[k + 1, half:], -signs * dh[k + 1, :half]], axis=0)
            upper, lower = split_two(grad)
            value = dot32(back_u, upper) + (dot32(back_l, upper) + dot32(back_u, lower))
            rows = slice(k * PIECE, (k + 1) * PIECE)
            df_ref[rows, :] = value if part == 0 else df_ref[rows, :] + value


VMEM_SPEC = pl.BlockSpec(memory_space=pltpu.VMEM)
SMEM_SPEC = pl.BlockSpec(memory_space=pltpu.SMEM)


def conv_parts(count):
    return 1 if count <= 64 else 4


def conv_forward(firsts, pieces, filt, per):
    count, _, lanes = pieces.shape
    taps = filt.shape[0] // PIECE
    parts = conv_parts(count)
    spec = (2 * PIECE // parts, lanes)
    scratch = [pltpu.VMEM((count,) + spec, jnp.float32), pltpu.VMEM((taps,) + spec, jnp.float32)]
    if parts > 1:
        scratch.append(pltpu.VMEM(pieces.shape, jnp.float32))
    return pl.pallas_call(
        functools.partial(conv_forward_kernel, per),
        out_shape=jax.ShapeDtypeStruct(pieces.shape, jnp.bfloat16),
        in_specs=[SMEM_SPEC] + [VMEM_SPEC] * 4,
        out_specs=VMEM_SPEC,
        scratch_shapes=scratch,
        compiler_params=pltpu.CompilerParams(vmem_limit_bytes=60 * 2**20),
        cost_estimate=pl.CostEstimate(flops=2 * 10**9, bytes_accessed=8 * 10**6, transcendentals=0),
        name="long_conv",
    )(firsts, pieces, filt, *odd_tables(parts))


def conv_backward(firsts, lasts, pieces, grads, filt, per):
    count, _, lanes = pieces.shape
    taps = filt.shape[0] // PIECE
    parts = conv_parts(count)
    spec = (2 * PIECE // parts, lanes)
    scratch = [pltpu.VMEM((n,) + spec, jnp.float32) for n in (count, count, taps, taps)]
    if parts > 1:
        scratch.append(pltpu.VMEM(pieces.shape, jnp.float32))
    return pl.pallas_call(
        functools.partial(conv_backward_kernel, per),
        out_shape=(
            jax.ShapeDtypeStruct(pieces.shape, jnp.bfloat16),
            jax.ShapeDtypeStruct(filt.shape, jnp.float32),
        ),
        in_specs=[SMEM_SPEC] * 2 + [VMEM_SPEC] * 5,
        out_specs=(VMEM_SPEC, VMEM_SPEC),
        scratch_shapes=scratch,
        compiler_params=pltpu.CompilerParams(vmem_limit_bytes=60 * 2**20),
        cost_estimate=pl.CostEstimate(flops=4 * 10**9, bytes_accessed=10**7, transcendentals=0),
        name="long_conv_back",
    )(firsts, lasts, pieces, grads, filt, *odd_tables(parts))


def channel_order(value, count):
    groups, rows, lanes = value.shape
    if groups != count:
        own = groups * lanes // count
        value = value.reshape(groups, rows, lanes // own, own).transpose(0, 2, 1, 3).reshape(count, rows, own)
    return value


def lane_order(value):
    _, rows, own = value.shape
    if own != LANES:
        value = value.reshape(-1, LANES // own, rows, own).transpose(0, 2, 1, 3).reshape(-1, rows, LANES)
    return value


def to_tokens(value):
    return lane_order(lax.all_to_all(value, "seq", 0, 0, tiled=True))


MESH_ID = pl.DeviceIdType.MESH
def remote(src, dst, send, recv, device):
    return pltpu.make_async_remote_copy(src, dst, send, recv, device_id=device, device_id_type=MESH_ID)


def greet(partners):
    barrier = pltpu.get_barrier_semaphore()
    for partner in partners:
        pl.semaphore_signal(barrier, inc=1, device_id=partner, device_id_type=MESH_ID)
    pl.semaphore_wait(barrier, len(partners))


def place_of(sizes):
    ny, nx, nz = sizes
    dp, seq = lax.axis_index("dp"), lax.axis_index("seq")
    y, c = dp // 2, dp % 2
    z, x = seq // nx, seq % nx

    def at_y(step):
        other = lax.rem(y + step, ny)
        return other, (other * 2 + c, seq)

    def at_x(step):
        other = lax.rem(x + step, nx)
        return other, (dp, z * nx + other)

    def at_z(step):
        other = lax.rem(z + step, nz)
        return other, (dp, other * nx + x)

    return (y, c, z, x), (y * 2 + 1 - c, seq), at_y, at_x, at_z


def axis_sizes():
    seq = lax.axis_size("seq")
    return lax.axis_size("dp") // 2, seq // 4, 4


def wide(ref):
    return ref[...].astype(jnp.float32)


def staged_sum(sizes, grads, out, sq, scratch):
    own, r0, r1, r2, r3, load_sem, s0, t0, s1, t1, s2, t2, s3, t3, s4, t4, s5, t5 = scratch
    ny, nx, nz = sizes
    strip = r0.shape[2]
    strips = out.shape[1] // strip
    width = out.shape[2]
    half, quarter = width // nx, width // nx // nz
    total = len(grads) * strips
    (y, c, z, x), sibling, at_y, at_x, at_z = place_of(sizes)

    def rows_of(k):
        return pl.ds(pl.multiple_of(lax.rem(k, strips) * strip, strip), strip)

    def cols(start, size):
        return pl.ds(pl.multiple_of(start * size, size), size)

    def core_copy(k, g):
        return remote(g.at[:, 1 - c, rows_of(k)], r0.at[k], s0.at[k], t0.at[k], sibling)

    def own_copy(k, g):
        slot = lax.rem(k, 4)
        return pltpu.make_async_copy(g.at[:, c, rows_of(k)], own.at[slot], load_sem.at[slot])

    def start_first(k):
        for i, g in enumerate(grads):

            @pl.when(k // strips == i)
            def _():
                core_copy(k, g).start()
                own_copy(k, g).start()

    def y_copy(k, i):
        other, device = at_y(i)
        return remote(r0.at[k, other], r1.at[k, ny - 1 - i], s1.at[k, i - 1], t1.at[k, ny - 1 - i], device)

    def x_copy(k, i):
        other, device = at_x(i)
        return remote(r1.at[k, 0, :, cols(other, half)], r2.at[k, nx - 1 - i], s2.at[k, i - 1], t2.at[k, nx - 1 - i], device)

    def z_copy(k, i):
        other, device = at_z(i)
        return remote(r2.at[k, 0, :, cols(other, quarter)], r3.at[k, nz - 1 - i], s3.at[k, i - 1], t3.at[k, nz - 1 - i], device)

    def z_back(k, i):
        other, device = at_z(i)
        part = out.at[k // strips, rows_of(k), cols(x * nz + z, quarter)]
        return remote(part, part, s4.at[k, i - 1], t4.at[k, nz - 1 - i], device)

    def x_back(k, i):
        other, device = at_x(i)
        part = out.at[k // strips, rows_of(k), cols(x, half)]
        return remote(part, part, s5.at[k, i - 1], t5.at[k, nx - 1 - i], device)

    def tiles(size, body):
        piece = min(size, TILE // strip)

        def one(i, carry):
            body(pl.ds(pl.multiple_of(i * piece, piece), piece))
            return carry

        lax.fori_loop(0, size // piece, one, 0)

    def begin():
        start_first(jnp.int32(0))
        start_first(jnp.int32(1))

    def step(t):
        @pl.when(t + 2 < total)
        def _():
            start_first(t + 2)

        @pl.when(t < total)
        def _():
            k, slot = t, lax.rem(t, 4)
            core_copy(k, grads[0]).wait_recv()
            own_copy(k, grads[0]).wait()
            for other in range(ny):

                def add(at):
                    r0[k, other, :, at] = (wide(r0.at[k, other, :, at]) + wide(own.at[slot, other, :, at])).astype(r0.dtype)

                tiles(width, add)
            for i in range(1, ny):
                y_copy(k, i).start()

        @pl.when((t >= OFFSETS[0]) & (t < total + OFFSETS[0]))
        def _():
            k = t - OFFSETS[0]
            for i in range(1, ny):
                y_copy(k, i).wait_recv()

            def add(at):
                value = wide(r0.at[k, y, :, at])
                for i in range(ny - 1):
                    value = value + wide(r1.at[k, i, :, at])
                r1[k, 0, :, at] = value.astype(r1.dtype)

            tiles(width, add)
            for i in range(1, nx):
                x_copy(k, i).start()

        @pl.when((t >= OFFSETS[1]) & (t < total + OFFSETS[1]))
        def _():
            k = t - OFFSETS[1]
            for i in range(1, nx):
                x_copy(k, i).wait_recv()

            def add(at):
                mine = pl.ds(pl.multiple_of(x * half + at.start, 128), at.size)
                value = wide(r1.at[k, 0, :, mine])
                for i in range(nx - 1):
                    value = value + wide(r2.at[k, i, :, at])
                r2[k, 0, :, at] = value.astype(r2.dtype)

            tiles(half, add)
            for i in range(1, nz):
                z_copy(k, i).start()

        @pl.when((t >= OFFSETS[2]) & (t < total + OFFSETS[2]))
        def _():
            k = t - OFFSETS[2]
            for i in range(1, nz):
                z_copy(k, i).wait_recv()
            value = wide(r2.at[k, 0, :, cols(z, quarter)])
            for i in range(nz - 1):
                value = value + wide(r3.at[k, i])
            sq[...] += value * value
            out[k // strips, rows_of(k), cols(x * nz + z, quarter)] = value.astype(out.dtype)
            for i in range(1, nz):
                z_back(k, i).start()

        @pl.when((t >= OFFSETS[3]) & (t < total + OFFSETS[3]))
        def _():
            k = t - OFFSETS[3]
            for i in range(1, nz):
                z_back(k, i).wait_recv()
            for i in range(1, nx):
                x_back(k, i).start()

    def retire(k):
        for i in range(1, nx):
            x_back(k, i).wait()
            x_copy(k, i).wait_send()
        for i in range(1, nz):
            z_copy(k, i).wait_send()
            z_back(k, i).wait_send()
        for i in range(1, ny):
            y_copy(k, i).wait_send()
        core_copy(k, grads[0]).wait_send()

    def finish(first):
        def one(k, carry):
            retire(k)
            return carry

        lax.fori_loop(first, total, one, 0)

    return begin, step, retire, finish, total + OFFSETS[3]


def staged_scratch(sizes, count, rows, strip, width):
    ny, nx, nz = sizes
    total = count * rows // strip
    half = jnp.bfloat16
    dma = pltpu.SemaphoreType.DMA
    pairs = [(total,), (total, ny - 1), (total, nx - 1), (total, nz - 1), (total, nz - 1), (total, nx - 1)]
    return [
        pltpu.VMEM((4, ny, strip, width), half),
        pltpu.VMEM((total, ny, strip, width), half),
        pltpu.VMEM((total, ny - 1, strip, width), half),
        pltpu.VMEM((total, nx - 1, strip, width // nx), half),
        pltpu.VMEM((total, nz - 1, strip, width // nx // nz), half),
        dma((4,)),
    ] + [dma(p) for p in pairs for _ in range(2)]


STAGED = 18
TILE = 65536
OFFSETS = (1, 2, 3, 4)
BEHIND = 8


def grad_sum_kernel(sizes, g0, g1, g2, small, out, small_out, norm, *scratch):
    staged, (b0, b1, b2, b3, sq, norms, small_send, small_recv, norm_send, norm_recv) = scratch[:STAGED], scratch[STAGED:]
    ny, nx, nz = sizes
    (y, c, z, x), sibling, at_y, at_x, at_z = place_of(sizes)
    partners = [sibling] + [at_y(i)[1] for i in range(1, ny)] + [at_x(i)[1] for i in range(1, nx)]
    greet(partners + [at_z(i)[1] for i in range(1, nz)])
    axes = ((2, c, None), (ny, y, at_y), (nx, x, at_x), (nz, z, at_z))
    base = (0, 1, ny, ny + nx - 1, ny + nx + nz - 2)

    def small_copies(stage):
        def numbered(first, pairs):
            return [
                remote(src, dst, small_send.at[first + i], small_recv.at[first + back], device)
                for i, back, src, dst, device in pairs
            ]

        def spread(axis, pick):
            count, _, at = axes[axis]
            return [(i - 1, count - 1 - i) + pick(i, *at(i)) for i in range(1, count)]

        if stage == 0:
            return numbered(0, [(0, 0, small.at[:, 1 - c], b0, sibling)])
        if stage == 1:
            return numbered(base[1], spread(1, lambda i, o, d: (b0.at[o], b1.at[ny - 1 - i], d)))
        if stage == 2:
            return numbered(base[2], spread(2, lambda i, o, d: (b1.at[0, o], b2.at[nx - 1 - i], d)))
        if stage == 3:
            return numbered(base[3], spread(3, lambda i, o, d: (b2.at[0, o], b3.at[nz - 1 - i], d)))
        again = base[4]
        if stage == 4:
            part = small_out.at[y, c, x, z]
            return numbered(again + base[3], spread(3, lambda i, o, d: (part, part, d)))
        if stage == 5:
            part = small_out.at[y, c, x]
            return numbered(again + base[2], spread(2, lambda i, o, d: (part, part, d)))
        if stage == 6:
            part = small_out.at[y, c]
            return numbered(again + base[1], spread(1, lambda i, o, d: (part, part, d)))
        part = small_out.at[:, c]
        return numbered(again, [(0, 0, part, part, sibling)])

    def small_step(stage):
        if stage > 0:
            for copy in small_copies(stage - 1):
                copy.wait_recv()
        if stage == 1:
            b0[...] += small[:, c]
        if stage == 2:
            value = b0[y]
            for i in range(ny - 1):
                value = value + b1[i]
            b1[0] = value
        if stage == 3:
            value = b1[0, x]
            for i in range(nx - 1):
                value = value + b2[i]
            b2[0] = value
        if stage == 4:
            value = b2[0, z]
            for i in range(nz - 1):
                value = value + b3[i]
            small_out[y, c, x, z] = value
            for row in range(0, value.shape[0], 8):
                sq[:8, :128] += value[row : row + 8] * value[row : row + 8]
        if stage < 8:
            for copy in small_copies(stage):
                copy.start()

    def norm_copies(stage):
        count, place, at = axes[stage]
        devices = [sibling] if at is None else [at(i)[1] for i in range(1, count)]
        return [
            remote(norms.at[stage, place], norms.at[stage, place], norm_send.at[stage, i], norm_recv.at[stage, len(devices) - 1 - i], device)
            for i, device in enumerate(devices)
        ]

    begin, step, retire, finish, steps = staged_sum(sizes, (g0, g1, g2), out, sq, staged)
    sq[...] = jnp.zeros_like(sq)
    begin()

    def one_step(t, carry):
        step(t)
        for stage in range(9):

            @pl.when(t == stage)
            def _():
                small_step(stage)

        @pl.when(t >= BEHIND)
        def _():
            retire(t - BEHIND)

        return carry

    lax.fori_loop(0, steps - 1, one_step, 0)
    tile = jnp.zeros((8, 128), jnp.float32)
    for row in range(0, sq.shape[0], 8):
        for col in range(0, sq.shape[1], 128):
            tile = tile + sq[row : row + 8, col : col + 128]
    for stage in range(4):
        count, place, _ = axes[stage]
        norms[stage, place] = tile
        for copy in norm_copies(stage):
            copy.start()
        if stage == 1:
            step(jnp.int32(steps - 1))
        for copy in norm_copies(stage):
            copy.wait_recv()
        tile = norms[stage, 0]
        for i in range(1, count):
            tile = tile + norms[stage, i]
    norm[...] = tile
    for stage in range(4):
        for copy in norm_copies(stage):
            copy.wait_send()
    for stage in range(8):
        for copy in small_copies(stage):
            copy.wait_send()
    finish(steps - 1 - BEHIND)


def grad_sum(up, down, mixer, small):
    sizes = ny, nx, nz = axis_sizes()
    rows_all, width = mixer.shape
    seq = nx * nz
    rows = rows_all // (2 * ny)
    strip = 32
    full = jnp.float32
    dma = pltpu.SemaphoreType.DMA
    parts = 2 * ny * seq
    piece = -(-small.shape[0] // (parts * 1024)) * 8
    small = jnp.pad(small, (0, parts * piece * 128 - small.shape[0])).reshape(ny, 2, nx, nz, piece, 128)
    most = max(2, ny, nx, nz)
    smalls = 2 * (ny + nx + nz - 2)
    large, summed, norm = pl.pallas_call(
        functools.partial(grad_sum_kernel, sizes),
        out_shape=(
            jax.ShapeDtypeStruct((3, rows, width), jnp.bfloat16),
            jax.ShapeDtypeStruct(small.shape, full),
            jax.ShapeDtypeStruct((8, 128), full),
        ),
        in_specs=[pl.BlockSpec(memory_space=pltpu.HBM)] * 3 + [VMEM_SPEC],
        out_specs=(VMEM_SPEC,) * 3,
        scratch_shapes=staged_scratch(sizes, 3, rows, strip, width)
        + [
            pltpu.VMEM((ny, nx, nz, piece, 128), full),
            pltpu.VMEM((ny - 1, nx, nz, piece, 128), full),
            pltpu.VMEM((nx - 1, nz, piece, 128), full),
            pltpu.VMEM((nz - 1, piece, 128), full),
            pltpu.VMEM((strip, width // seq), full),
            pltpu.VMEM((4, most, 8, 128), full),
            dma((smalls,)),
            dma((smalls,)),
            dma((4, most - 1)),
            dma((4, most - 1)),
        ],
        compiler_params=pltpu.CompilerParams(vmem_limit_bytes=35 * 2**20, collective_id=1, has_side_effects=True),
        cost_estimate=pl.CostEstimate(flops=10**8, bytes_accessed=20 * 10**6, transcendentals=0),
        name="grad_sum",
    )(*(g.reshape(ny, 2, rows, width) for g in (up, down, mixer)), small)
    return large, summed.reshape(-1), jnp.sum(norm)


def row_gather(sizes, own, full, width, pieces, sems):
    a_send, a_recv, b_send, b_recv, c_send, c_recv, d_send, d_recv, e_send, e_recv = sems
    ny = sizes[0]
    rows = own.shape[0]
    half = width // 2
    size = half // pieces
    (y, c, _, _), sibling, at_y, _, _ = place_of(sizes)
    dp, seq = lax.axis_index("dp"), lax.axis_index("seq")
    side = lax.rem(seq, 2)
    pair = (dp, seq + 1 - 2 * side)

    def at_rows(d):
        return pl.ds(pl.multiple_of(d * rows, rows), rows)

    def at_cols(which, p):
        return pl.ds(pl.multiple_of(which * half + p * size, size), size)

    def core_copy():
        return remote(own, full.at[at_rows(dp)], a_send.at[0], a_recv.at[0], sibling)

    def y_copy(i, p):
        _, device = at_y(i)
        cols = at_cols(side, p)
        return remote(own.at[:, cols], full.at[at_rows(dp), cols], b_send.at[i - 1, p], b_recv.at[ny - 1 - i, p], device)

    def pass_on(i, p, which, send, recv, device):
        other, _ = at_y(ny - i)
        part = full.at[at_rows(other * 2 + c), at_cols(which, p)]
        return remote(part, part, send.at[ny - 1 - i, p], recv.at[ny - 1 - i, p], device)

    def x_copy(i, p):
        return pass_on(i, p, side, c_send, c_recv, pair)

    def first_copy(i, p):
        return pass_on(i, p, side, d_send, d_recv, sibling)

    def second_copy(i, p):
        return pass_on(i, p, 1 - side, e_send, e_recv, sibling)

    every = [(i, p) for p in range(pieces) for i in range(1, ny)]

    def start():
        for i, p in every:
            y_copy(i, p).start()
        core_copy().start()

    def first_half(p):
        for i in range(1, ny):
            y_copy(i, p).wait_recv()
            x_copy(i, p).start()
            first_copy(i, p).start()

    def second_half(p):
        for i in range(1, ny):
            x_copy(i, p).wait_recv()
            second_copy(i, p).start()

    def finish():
        core_copy().wait()
        for i, p in every:
            y_copy(i, p).wait_send()
            x_copy(i, p).wait_send()
            first_copy(i, p).wait()
            second_copy(i, p).wait()

    return start, first_half, second_half, finish


def gather_sems(sizes, pieces):
    dma = pltpu.SemaphoreType.DMA
    return [dma((1,))] * 2 + [dma((sizes[0] - 1, pieces))] * 8


GATHER = 10


def greet_near(sizes, count):
    _, sibling, at_y, _, _ = place_of(sizes)
    dp, me = lax.axis_index("dp"), lax.axis_index("seq")
    others = [(dp, lax.rem(me + i, count)) for i in range(1, count)]
    greet([sibling] + [at_y(i)[1] for i in range(1, sizes[0])] + others)
    return others


def open_kernel(sizes, count, pieces, mixer, mlp, tok, first, w_in, w_out, up_out, down_out, before, firsts,
                own, mlp_in, mlp_sem, halo_send, halo_recv, first_send, first_recv, *sems):
    rows = own.shape[0]
    lane_count = own.shape[1]
    me, dp = lax.axis_index("seq"), lax.axis_index("dp")
    chunk = mlp_in.shape[2]
    chunks = rows // chunk

    def load(k):
        return pltpu.make_async_copy(mlp.at[:, k * chunk : (k + 1) * chunk], mlp_in.at[k % 2], mlp_sem.at[k % 2])

    load(0).start()
    own[...] = mixer[:, :lane_count].astype(jnp.bfloat16)
    others = greet_near(sizes, count)
    start, first_half, second_half, finish = row_gather(sizes, own, w_in, lane_count, pieces, sems)
    start()
    halo = remote(tok.at[tok.shape[0] - HALO :], before, halo_send, halo_recv, others[0])
    halo.start()
    announced = [
        remote(first, firsts.at[me], first_send.at[i], first_recv.at[count - 2 - i], device) for i, device in enumerate(others)
    ]
    for copy in announced:
        copy.start()
    firsts[me] = first[...]
    w_in[pl.ds(pl.multiple_of(dp * rows, rows), rows), :] = own[...]
    w_out[...] = mixer[:, lane_count:].astype(jnp.bfloat16)
    for k in range(max(chunks, pieces)):
        if k < chunks:
            if k + 1 < chunks:
                load(k + 1).start()
            load(k).wait()
            at = slice(k * chunk, (k + 1) * chunk)
            up_out[at] = mlp_in[k % 2, 0].astype(jnp.bfloat16)
            down_out[at] = mlp_in[k % 2, 1].astype(jnp.bfloat16)
        if k < pieces:
            first_half(k)
        if 2 <= k < pieces:
            second_half(k - 2)
    for k in range(max(0, pieces - 2), pieces):
        second_half(k)
    halo.wait()
    for copy in announced:
        copy.wait()
    finish()


def open_gather(mixer, mlp, tok, first, count):
    sizes = axis_sizes()
    rows, total = mixer.shape
    width = tok.shape[1]
    lane_count = total - width
    dp = 2 * sizes[0]
    pieces = 6
    half = jnp.bfloat16
    dma = pltpu.SemaphoreType.DMA
    chunk = rows // 4
    first = jnp.broadcast_to(first.reshape(1, 1), (8, 128))
    return pl.pallas_call(
        functools.partial(open_kernel, sizes, count, pieces),
        out_shape=(
            jax.ShapeDtypeStruct((rows * dp, lane_count), half),
            jax.ShapeDtypeStruct((rows, width), half),
            jax.ShapeDtypeStruct(mlp.shape[1:], half),
            jax.ShapeDtypeStruct(mlp.shape[1:], half),
            jax.ShapeDtypeStruct((HALO, width), half),
            jax.ShapeDtypeStruct((count, 8, 128), jnp.int32),
        ),
        in_specs=[VMEM_SPEC, pl.BlockSpec(memory_space=pltpu.HBM), VMEM_SPEC, VMEM_SPEC],
        out_specs=(VMEM_SPEC,) * 6,
        scratch_shapes=[
            pltpu.VMEM((rows, lane_count), half),
            pltpu.VMEM((2, 2, chunk, mlp.shape[2]), jnp.float32),
            dma((2,)),
            dma,
            dma,
            dma((count - 1,)),
            dma((count - 1,)),
        ]
        + gather_sems(sizes, pieces),
        compiler_params=pltpu.CompilerParams(vmem_limit_bytes=60 * 2**20, collective_id=3, has_side_effects=True),
        cost_estimate=pl.CostEstimate(flops=10**6, bytes_accessed=60 * 10**6, transcendentals=0),
        name="open_gather",
    )(mixer, mlp, tok, first)


def swap_kernel(sizes, pieces, value, own, swapped, full, swap_send, swap_recv, self_sem, *sems):
    count = value.shape[0]
    rows = own.shape[0]
    me, dp = lax.axis_index("seq"), lax.axis_index("dp")
    others = greet_near(sizes, count)
    start, first_half, second_half, finish = row_gather(sizes, own, full, own.shape[1], pieces, sems)
    start()
    copies = [
        remote(value.at[device[1]], swapped.at[me], swap_send.at[i], swap_recv.at[count - 2 - i], device)
        for i, device in enumerate(others)
    ]
    for copy in copies:
        copy.start()
    kept = [
        pltpu.make_async_copy(value.at[me], swapped.at[me], self_sem.at[0]),
        pltpu.make_async_copy(own, full.at[pl.ds(pl.multiple_of(dp * rows, rows), rows)], self_sem.at[1]),
    ]
    for copy in kept:
        copy.start()
    for p in range(pieces):
        first_half(p)
        if p > 0:
            second_half(p - 1)
    second_half(pieces - 1)
    for copy in kept + copies:
        copy.wait()
    finish()


def swap_with_rows(value, own, number):
    sizes = axis_sizes()
    count = value.shape[0]
    rows, width = own.shape
    pieces = 4
    dma = pltpu.SemaphoreType.DMA
    hbm = pl.BlockSpec(memory_space=pltpu.HBM)
    return pl.pallas_call(
        functools.partial(swap_kernel, sizes, pieces),
        out_shape=(
            jax.ShapeDtypeStruct(value.shape, value.dtype),
            jax.ShapeDtypeStruct((rows * 2 * sizes[0], width), own.dtype),
        ),
        in_specs=[hbm, VMEM_SPEC],
        out_specs=(hbm, hbm),
        scratch_shapes=[dma((count - 1,)), dma((count - 1,)), dma((2,))] + gather_sems(sizes, pieces),
        compiler_params=pltpu.CompilerParams(vmem_limit_bytes=60 * 2**20, collective_id=number, has_side_effects=True),
        cost_estimate=pl.CostEstimate(flops=10**6, bytes_accessed=40 * 10**6, transcendentals=0),
        name="swap_with_rows",
    )(value, own)


def swap_filter_kernel(value, features, first, last, codes, swapped, filt, swap_send, swap_recv, self_sem):
    count = value.shape[0]
    me, dp = lax.axis_index("seq"), lax.axis_index("dp")
    others = [(dp, lax.rem(me + i, count)) for i in range(1, count)]
    greet(others)
    copies = [
        remote(value.at[device[1]], swapped.at[me], swap_send.at[i], swap_recv.at[count - 2 - i], device)
        for i, device in enumerate(others)
    ]
    for copy in copies:
        copy.start()
    kept = pltpu.make_async_copy(value.at[me], swapped.at[me], self_sem)
    kept.start()
    rates = jnp.exp2(-codes[...].astype(jnp.float32))
    total = jnp.zeros_like(rates)
    step = 2 * PIECE
    for start in range(0, filt.shape[0], step):
        hidden = jnp.sin(jnp.dot(features[start : start + step], first[...], precision=highest, preferred_element_type=jnp.float32))
        raw = jnp.dot(hidden, last[...], precision=highest, preferred_element_type=jnp.float32)
        places = (lax.broadcasted_iota(jnp.int32, raw.shape, 0) + start).astype(jnp.float32)
        shaped = raw * jnp.exp(-places * rates)
        total = total + jnp.sum(shaped * shaped, axis=0, keepdims=True)
        filt[start : start + step] = shaped
    scale = lax.rsqrt(total + norm_eps)
    for start in range(0, filt.shape[0], step):
        filt[start : start + step] = filt[start : start + step] * scale
    kept.wait()
    for copy in copies:
        copy.wait()


def swap_with_filter(value, first, last, codes, length):
    count = value.shape[0]
    dma = pltpu.SemaphoreType.DMA
    hbm = pl.BlockSpec(memory_space=pltpu.HBM)
    places = np.arange(length, dtype=np.float32)[:, None]
    bands = np.arange(1, (first.shape[0] - 1) // 2 + 1, dtype=np.float32)[None, :]
    angles = (np.float32(2.0 * math.pi / length) * places * bands).astype(np.float32)
    features = np.concatenate([places / np.float32(length), np.cos(angles), np.sin(angles)], axis=1).astype(np.float32)
    return pl.pallas_call(
        swap_filter_kernel,
        out_shape=(
            jax.ShapeDtypeStruct(value.shape, value.dtype),
            jax.ShapeDtypeStruct((length, last.shape[1]), jnp.float32),
        ),
        in_specs=[hbm] + [VMEM_SPEC] * 4,
        out_specs=(hbm, VMEM_SPEC),
        scratch_shapes=[dma((count - 1,)), dma((count - 1,)), dma],
        compiler_params=pltpu.CompilerParams(vmem_limit_bytes=60 * 2**20, collective_id=4, has_side_effects=True),
        cost_estimate=pl.CostEstimate(flops=10**8, bytes_accessed=10 * 10**6, transcendentals=10**6),
        name="swap_with_filter",
    )(value, jnp.asarray(features), first, last, codes.reshape(1, -1))


GRAD_TILE = 512


def swap_grads_kernel(value, cot, normed, act, g_up, zero, swapped, d_up, d_down, after, left_t, right, made,
                      swap_send, swap_recv, self_sem, load_sem, store_sem, halo_send, halo_recv):
    count = value.shape[0]
    me, dp = lax.axis_index("seq"), lax.axis_index("dp")
    others = [(dp, lax.rem(me + i, count)) for i in range(1, count)]
    greet(others)
    copies = [
        remote(value.at[device[1]], swapped.at[me], swap_send.at[i], swap_recv.at[count - 2 - i], device)
        for i, device in enumerate(others)
    ]
    for copy in copies:
        copy.start()
    halo = remote(zero.at[:HALO], after, halo_send, halo_recv, others[-1])
    halo.start()
    kept = pltpu.make_async_copy(value.at[me], swapped.at[me], self_sem)
    kept.start()
    for left, source, target in ((cot, act, d_down), (normed, g_up, d_up)):
        tiles = source.shape[1] // GRAD_TILE

        def at(j):
            return pl.ds(pl.multiple_of(j * GRAD_TILE, GRAD_TILE), GRAD_TILE)

        def load(j):
            slot = lax.rem(j, 2)
            return pltpu.make_async_copy(source.at[:, at(j)], right.at[slot], load_sem.at[slot])

        def store(j):
            slot = lax.rem(j, 2)
            return pltpu.make_async_copy(made.at[slot], target.at[:, at(j)], store_sem.at[slot])

        load(jnp.int32(0)).start()
        left_t[...] = left[...].T

        def one(j, carry):
            slot = lax.rem(j, 2)

            @pl.when(j + 1 < tiles)
            def _():
                load(j + 1).start()

            load(j).wait()

            @pl.when(j >= 2)
            def _():
                store(j - 2).wait()

            made[slot] = dot32(left_t[...], right[slot]).astype(jnp.bfloat16)
            store(j).start()
            return carry

        lax.fori_loop(0, tiles, one, 0)
        store(jnp.int32(tiles - 2)).wait()
        store(jnp.int32(tiles - 1)).wait()
    kept.wait()
    halo.wait()
    for copy in copies:
        copy.wait()


def swap_with_grads(value, cot, normed, act, g_up, zero):
    count = value.shape[0]
    rows, width = cot.shape
    hidden = act.shape[1]
    half = jnp.bfloat16
    dma = pltpu.SemaphoreType.DMA
    hbm = pl.BlockSpec(memory_space=pltpu.HBM)
    return pl.pallas_call(
        swap_grads_kernel,
        out_shape=(
            jax.ShapeDtypeStruct(value.shape, value.dtype),
            jax.ShapeDtypeStruct((width, hidden), half),
            jax.ShapeDtypeStruct((width, hidden), half),
            jax.ShapeDtypeStruct((HALO, width), half),
        ),
        in_specs=[hbm, VMEM_SPEC, VMEM_SPEC, hbm, hbm, hbm],
        out_specs=(hbm,) * 4,
        scratch_shapes=[
            pltpu.VMEM((width, rows), half),
            pltpu.VMEM((2, rows, GRAD_TILE), half),
            pltpu.VMEM((2, width, GRAD_TILE), half),
            dma((count - 1,)),
            dma((count - 1,)),
            dma,
            dma((2,)),
            dma((2,)),
            dma,
            dma,
        ],
        compiler_params=pltpu.CompilerParams(vmem_limit_bytes=60 * 2**20, collective_id=6, has_side_effects=True),
        cost_estimate=pl.CostEstimate(flops=4 * rows * width * hidden, bytes_accessed=40 * 10**6, transcendentals=0),
        name="swap_with_grads",
    )(value, cot, normed, act, g_up, zero)


def block_specs(shapes):
    return [pl.BlockSpec(shape, lambda j, n=len(shape): (0,) * n, pipeline_mode=pl.Buffered(1)) for shape in shapes]


def normalized(values):
    center = jnp.mean(values, axis=-1, keepdims=True)
    centred = values - center
    scale = lax.rsqrt(jnp.mean(centred * centred, axis=-1, keepdims=True) + norm_eps)
    return centred * scale, scale


def norm_back(grad, gain, scaled, scale):
    inner = grad * gain
    mean_inner = jnp.mean(inner, axis=-1, keepdims=True)
    mean_scaled = jnp.mean(inner * scaled, axis=-1, keepdims=True)
    return scale * (inner - mean_inner - scaled * mean_scaled)


def dot_cols(left, right):
    return lax.dot_general(left, right, (((1,), (1,)), ((), ())), preferred_element_type=jnp.float32)


LANES = 128
HALO = 8


def project_kernel(tok, before, prev, gain, w_v, w_one, w_zero, t_v, t_one, t_zero,
                   conv_in, factors, zero_out, projs, normed_out, normed, held):
    rows = tok.shape[0]
    keep = prev[0].astype(jnp.float32)

    @pl.when(pl.program_id(0) == 0)
    def _():
        scaled, _ = normalized(before[...].astype(jnp.float32))
        normed[:HALO] = (scaled * gain[...]).astype(jnp.bfloat16)
        for start in range(0, rows, PIECE):
            at = slice(start, start + PIECE)
            scaled, _ = normalized(tok[at].astype(jnp.float32))
            value = (scaled * gain[...]).astype(jnp.bfloat16)
            normed[start + HALO : start + PIECE + HALO] = value
            normed_out[at] = value

    shorts = []
    for i, (w, taps) in enumerate(((w_v, t_v), (w_one, t_one), (w_zero, t_zero))):
        proj = dot32(normed[...], w[...]).astype(jnp.bfloat16)
        projs[i] = proj
        held[...] = proj.astype(jnp.float32)
        held[:HALO] = held[:HALO] * keep
        shorts.append(
            taps[0:1] * held[HALO : HALO + rows]
            + taps[1:2] * held[HALO - 1 : HALO - 1 + rows]
            + taps[2:3] * held[HALO - 2 : HALO - 2 + rows]
        )
    factors[0] = shorts[1]
    factors[1] = shorts[0]
    zero_out[...] = shorts[2]
    product = (shorts[0] * shorts[1]).astype(jnp.bfloat16)
    for i in range(conv_in.shape[0]):
        conv_in[i] = product[:, i * LANES : (i + 1) * LANES]


def project(tok, before, has_prev, gain, w_in, taps):
    rows, width = tok.shape
    size = 256
    steps = width // size
    col = lambda part: (lambda j: (0, part * steps + j))
    parts = [pl.BlockSpec((width, size), col(i)) for i in range(3)]
    tap_parts = [pl.BlockSpec((3, size), col(i)) for i in range(3)]
    wide = lambda n, dtype: jax.ShapeDtypeStruct((n, width), dtype)
    stack = lambda m, n: pl.BlockSpec((m, n, size), lambda j: (0, 0, j))
    return pl.pallas_call(
        project_kernel,
        grid=(steps,),
        out_shape=[jax.ShapeDtypeStruct((width // LANES, rows, LANES), jnp.bfloat16)]
        + [jax.ShapeDtypeStruct((2, rows, width), jnp.float32), wide(rows, jnp.float32)]
        + [jax.ShapeDtypeStruct((3, rows + HALO, width), jnp.bfloat16), wide(rows, jnp.bfloat16)],
        in_specs=block_specs([(rows, width), (HALO, width)]) + [SMEM_SPEC] + block_specs([(1, width)]) + parts + tap_parts,
        out_specs=[pl.BlockSpec((size // LANES, rows, LANES), lambda j: (j, 0, 0))]
        + [stack(2, rows), pl.BlockSpec((rows, size), lambda j: (0, j)), stack(3, rows + HALO)]
        + block_specs([(rows, width)]),
        scratch_shapes=[pltpu.VMEM((rows + HALO, width), jnp.bfloat16), pltpu.VMEM((rows + HALO, size), jnp.float32)],
        compiler_params=pltpu.CompilerParams(vmem_limit_bytes=60 * 2**20),
        cost_estimate=pl.CostEstimate(flops=6 * rows * width * width, bytes_accessed=20 * 10**6, transcendentals=0),
        name="project",
    )(tok, before, has_prev, gain, w_in, w_in, w_in, taps, taps, taps)


def mlp_kernel(conv, conv_in, zero, tok, cot, skip, gain, w_out, w_up, w_down,
               output, act_out, up_out, gated, normed, d_resid, branch_out, conv_grad, d_mixed, d_zero, d_gain, d_skip,
               resid, down, d_normed):
    rows, width = tok.shape
    groups = width // LANES
    step = pl.program_id(0)

    @pl.when(step == 0)
    def _():
        for g in range(groups):
            at = slice(g * LANES, (g + 1) * LANES)
            mixed = conv[g].astype(jnp.float32) + skip[:, at] * conv_in[g].astype(jnp.float32)
            gated[:, at] = (zero[:, at] * mixed).astype(jnp.bfloat16)
        resid[...] = tok[...].astype(jnp.float32) + dot_cols(gated[...], w_out[...])
        for start in range(0, rows, PIECE):
            at = slice(start, start + PIECE)
            scaled, _ = normalized(resid[at])
            normed[at] = (scaled * gain[...]).astype(jnp.bfloat16)

    up = dot32(normed[...], w_up[...])
    d_act = dot32(cot[...], w_down[...])
    root = math.sqrt(2.0 / math.pi)
    square = up * up
    bent = jnp.tanh(root * up * (1.0 + 0.044715 * square))
    act = (0.5 * up * (1.0 + bent)).astype(jnp.bfloat16)
    slope = 0.5 * (1.0 + bent) + (0.5 * root) * up * (1.0 - bent * bent) * (1.0 + (3.0 * 0.044715) * square)
    g_up = (slope * d_act).astype(jnp.bfloat16)
    act_out[...] = act
    up_out[...] = g_up
    down_part = dot_cols(act, w_down[...])
    normed_part = dot_cols(g_up, w_up[...])

    @pl.when(step == 0)
    def _():
        down[...] = down_part
        d_normed[...] = normed_part

    @pl.when(step > 0)
    def _():
        down[...] += down_part
        d_normed[...] += normed_part

    @pl.when(step == pl.num_programs(0) - 1)
    def _():
        gain_sum = jnp.zeros((1, width), jnp.float32)
        for start in range(0, rows, PIECE):
            at = slice(start, start + PIECE)
            output[at] = (resid[at] + down[at]).astype(jnp.bfloat16)
            scaled, scale = normalized(resid[at])
            grad = d_normed[at]
            gain_sum = gain_sum + jnp.sum(grad * scaled, axis=0, keepdims=True)
            total = cot[at].astype(jnp.float32) + norm_back(grad, gain[...], scaled, scale)
            d_resid[at] = total
            branch_out[at] = total.astype(jnp.bfloat16)
        d_gain[...] = gain_sum
        down[...] = dot32(branch_out[...], w_out[...])
        for g in range(groups):
            at = slice(g * LANES, (g + 1) * LANES)
            source = conv_in[g].astype(jnp.float32)
            mixed = conv[g].astype(jnp.float32) + skip[:, at] * source
            d_gated = down[:, at]
            d_zero[:, at] = (d_gated * mixed).astype(jnp.bfloat16)
            grad = d_gated * zero[:, at]
            d_mixed[g] = grad
            conv_grad[g] = grad.astype(jnp.bfloat16)
            d_skip[:, at] = jnp.sum(grad * source, axis=0, keepdims=True)


def mlp_block(conv, conv_in, zero, tok, cot, skip, gain, w_out, w_up, w_down):
    rows, width = tok.shape
    hidden = w_down.shape[1]
    size = 512
    steps = hidden // size
    groups = width // LANES
    flat = lambda dtype: jax.ShapeDtypeStruct((rows, width), dtype)
    cut = lambda dtype: jax.ShapeDtypeStruct((groups, rows, LANES), dtype)
    row = jax.ShapeDtypeStruct((1, width), jnp.float32)
    big = jax.ShapeDtypeStruct((rows, hidden), jnp.bfloat16)
    half, full = jnp.bfloat16, jnp.float32
    ends = [flat(half), flat(half), flat(full), flat(half), cut(half), cut(full), flat(half), row, row]
    tile = pl.BlockSpec((rows, size), lambda j: (0, j))
    one = block_specs([(rows, width)])
    return pl.pallas_call(
        mlp_kernel,
        grid=(steps,),
        out_shape=[flat(half), big, big] + ends,
        in_specs=block_specs([conv.shape, conv.shape, zero.shape, tok.shape, cot.shape, (1, width), (1, width), w_out.shape])
        + [pl.BlockSpec((width, size), index) for index in (lambda j: (0, j),) * 2],
        out_specs=one + [tile, tile] + block_specs([e.shape for e in ends]),
        scratch_shapes=[pltpu.VMEM((rows, width), full)] * 3,
        compiler_params=pltpu.CompilerParams(vmem_limit_bytes=60 * 2**20),
        cost_estimate=pl.CostEstimate(flops=8 * rows * width * hidden + 4 * rows * width * width, bytes_accessed=50 * 10**6, transcendentals=rows * hidden),
        name="mlp_block",
    )(conv, conv_in, zero, tok, cot, skip, gain, w_out, w_up, w_down)


def shifted_back(held, wide_proj, after, taps, proj, prev, nxt, d_taps):
    rows = held.shape[0] - HALO
    held[rows:] = after[...].astype(jnp.float32) * nxt[0].astype(jnp.float32)
    g_proj = (
        taps[0:1] * held[:rows] + taps[1:2] * held[1 : rows + 1] + taps[2:3] * held[2 : rows + 2]
    ).astype(jnp.bfloat16)
    wide_proj[...] = proj[...].astype(jnp.float32)
    wide_proj[:HALO] = wide_proj[:HALO] * prev[0].astype(jnp.float32)
    d_taps[...] = jnp.concatenate(
        [jnp.sum(held[:rows] * wide_proj[HALO - i : HALO - i + rows], axis=0, keepdims=True) for i in range(3)], axis=0
    )
    return g_proj


def back_early_kernel(d_zero, proj, after, prev, nxt, taps, w_in, normed, branch, gated,
                      d_mixer, d_taps, d_normed, normed_t, branch_t, held, wide_proj):
    rows = normed.shape[0]
    step = pl.program_id(0)
    per = pl.num_programs(0) // 2

    @pl.when(step == 0)
    def _():
        d_normed[...] = jnp.zeros_like(d_normed)
        normed_t[...] = normed[...].T
        branch_t[...] = branch[...].T

    @pl.when(step < per)
    def _():
        held[:rows] = d_zero[...].astype(jnp.float32)
        g_proj = shifted_back(held, wide_proj, after, taps, proj, prev, nxt, d_taps)
        d_normed[...] += dot_cols(g_proj, w_in[...])
        d_mixer[...] = dot32(normed_t[...], g_proj).astype(jnp.bfloat16)

    @pl.when(step >= per)
    def _():
        d_mixer[...] = dot32(branch_t[...], gated[...]).astype(jnp.bfloat16)


def project_back_early(d_zero, projs, after, has_prev, has_next, taps, w_in, normed, branch, gated):
    rows, width = normed.shape
    size = 512
    per = width // size
    half = jnp.bfloat16
    inner = lambda j: jnp.minimum(j, per - 1)
    third = lambda n: pl.BlockSpec((n, size), lambda j: (0, 2 * per + inner(j)))
    tile = lambda n: pl.BlockSpec((n, size), lambda j: (0, inner(j)))
    return pl.pallas_call(
        back_early_kernel,
        grid=(2 * per,),
        out_shape=[
            jax.ShapeDtypeStruct((width, 4 * width), half),
            jax.ShapeDtypeStruct((3, width), jnp.float32),
            jax.ShapeDtypeStruct((rows, width), jnp.float32),
        ],
        in_specs=[tile(rows), pl.BlockSpec((None, rows + HALO, size), lambda j: (2, 0, inner(j))), tile(HALO)]
        + [SMEM_SPEC, SMEM_SPEC, third(3), third(width)]
        + block_specs([(rows, width)] * 2)
        + [pl.BlockSpec((rows, size), lambda j: (0, jnp.maximum(j - per, 0)))],
        out_specs=[pl.BlockSpec((width, size), lambda j: (0, 2 * per + j)), tile(3)] + block_specs([(rows, width)]),
        scratch_shapes=[
            pltpu.VMEM((width, rows), half),
            pltpu.VMEM((width, rows), half),
            pltpu.VMEM((rows + HALO, size), jnp.float32),
            pltpu.VMEM((rows + HALO, size), jnp.float32),
        ],
        compiler_params=pltpu.CompilerParams(vmem_limit_bytes=60 * 2**20),
        cost_estimate=pl.CostEstimate(flops=6 * rows * width * width, bytes_accessed=20 * 10**6, transcendentals=0),
        name="project_back_early",
    )(d_zero, projs, after, has_prev, has_next, taps, w_in, normed, branch, gated)


def back_late_kernel(begun, back, d_mixed, other, proj, after, prev, nxt, skip, taps, w_in, normed, tok, d_resid, gain, start,
                     d_mixer, d_taps, tokens_grad, d_gain, normed_t, d_normed, held, wide_proj):
    rows = tok.shape[0]
    step = pl.program_id(0)

    @pl.when(step == 0)
    def _():
        d_normed[...] = start[...]
        normed_t[...] = normed[...].T

    def spread(ref):
        return jnp.concatenate([ref[i].astype(jnp.float32) for i in range(ref.shape[0])], axis=1)

    d_conv_in = skip[...] * spread(d_mixed) + spread(back)
    held[:rows] = (d_conv_in * other[...]).astype(jnp.bfloat16).astype(jnp.float32)
    g_proj = shifted_back(held, wide_proj, after, taps, proj, prev, nxt, d_taps)
    d_normed[...] += dot_cols(g_proj, w_in[...])
    d_mixer[...] = dot32(normed_t[...], g_proj).astype(jnp.bfloat16)

    @pl.when(step == pl.num_programs(0) - 1)
    def _():
        gain_sum = jnp.zeros((1, tok.shape[1]), jnp.float32)
        for first in range(0, rows, PIECE):
            at = slice(first, first + PIECE)
            scaled, scale = normalized(tok[at].astype(jnp.float32))
            grad = d_normed[at]
            gain_sum = gain_sum + jnp.sum(grad * scaled, axis=0, keepdims=True)
            tokens_grad[at] = (d_resid[at] + norm_back(grad, gain[...], scaled, scale)).astype(jnp.bfloat16)
        d_gain[...] = gain_sum


def project_back_late(begun, back, d_mixed, factors, projs, after, has_prev, has_next, skip, taps, w_in, normed, tok, d_resid, gain, start):
    rows, width = tok.shape
    size = 512
    per = width // size
    half = jnp.bfloat16
    lane = lambda j: j // 2
    part = lambda j: lax.rem(j, 2)
    place = lambda j: part(j) * per + lane(j)
    group = pl.BlockSpec((size // LANES, rows, LANES), lambda j: (lane(j), 0, 0))
    third = lambda n: pl.BlockSpec((n, size), lambda j: (0, place(j)))
    return pl.pallas_call(
        back_late_kernel,
        grid=(2 * per,),
        out_shape=[
            jax.ShapeDtypeStruct(begun.shape, half),
            jax.ShapeDtypeStruct((3, 2 * width), jnp.float32),
            jax.ShapeDtypeStruct((rows, width), half),
            jax.ShapeDtypeStruct((1, width), jnp.float32),
        ],
        in_specs=[pl.BlockSpec(memory_space=pl.ANY), group, group]
        + [pl.BlockSpec((None, rows, size), lambda j: (part(j), 0, lane(j)))]
        + [pl.BlockSpec((None, rows + HALO, size), lambda j: (part(j), 0, lane(j)))]
        + [third(HALO), SMEM_SPEC, SMEM_SPEC, pl.BlockSpec((1, size), lambda j: (0, lane(j))), third(3), third(width)]
        + block_specs([(rows, width)] * 3 + [(1, width), (rows, width)]),
        out_specs=[pl.BlockSpec((width, size), lambda j: (0, place(j))), third(3)] + block_specs([(rows, width), (1, width)]),
        scratch_shapes=[
            pltpu.VMEM((width, rows), half),
            pltpu.VMEM((rows, width), jnp.float32),
            pltpu.VMEM((rows + HALO, size), jnp.float32),
            pltpu.VMEM((rows + HALO, size), jnp.float32),
        ],
        input_output_aliases={0: 0},
        compiler_params=pltpu.CompilerParams(vmem_limit_bytes=60 * 2**20),
        cost_estimate=pl.CostEstimate(flops=8 * rows * width * width, bytes_accessed=30 * 10**6, transcendentals=0),
        name="project_back_late",
    )(begun, back, d_mixed, factors, projs, after, has_prev, has_next, skip, taps, w_in, normed, tok, d_resid, gain, start)


def adam_update(master, moment, square, grad, factor, rate, decay):
    clipped = grad * factor
    moment_new = beta_one * moment + (1.0 - beta_one) * clipped
    square_new = beta_two * square + (1.0 - beta_two) * clipped * clipped
    moment_hat = moment_new / (1.0 - beta_one**ADAM_STEP)
    square_hat = square_new / (1.0 - beta_two**ADAM_STEP)
    master_new = master - rate * (moment_hat / (jnp.sqrt(square_hat) + adam_eps) + decay * master)
    return (master_new, moment_new, square_new)


def on_device(
    tokens,
    cotangent,
    seq_first,
    decay_code,
    mixer_master,
    mixer_moment,
    mixer_square,
    mlp_master,
    mlp_moment,
    mlp_square,
    channel_master,
    channel_moment,
    channel_square,
    filter_in_master,
    filter_in_moment,
    filter_in_square,
    filter_out_master,
    filter_out_moment,
    filter_out_square,
):
    block_rows = tokens.shape[1]
    model_width = tokens.shape[2]
    lane_count = 3 * model_width
    per = block_rows // PIECE
    seq_count = lax.axis_size("seq")
    long_blocks = max(seq_count // 4, 4)
    length = long_blocks * block_rows
    own_width = model_width // seq_count
    seq_index = lax.axis_index("seq")
    w_in, out_own, up_own, down_own, before, first_tiles = open_gather(
        mixer_master, mlp_master, tokens[0], seq_first, seq_count
    )
    firsts = first_tiles[:, 0, 0]
    w_out = lax.all_gather(out_own, "dp", axis=0, tiled=True)
    w_down = lax.all_gather(down_own, "dp", axis=0, tiled=True)
    blocks = jnp.arange(seq_count, dtype=jnp.int32)
    same = firsts[None, :] == firsts[:, None]
    lasts = jnp.max(jnp.where(same, blocks[None, :], 0), axis=1).astype(jnp.int32)
    own_first = firsts[seq_index]
    has_prev = (seq_index - own_first >= 1).astype(jnp.int32).reshape(1)
    has_next = (lasts[seq_index] > seq_index).astype(jnp.int32).reshape(1)
    conv_taps = channel_master[:, :lane_count]
    gain_one = channel_master[0:1, lane_count:]
    gain_two = channel_master[1:2, lane_count:]
    skip_gain = channel_master[2:3, lane_count:]
    own_codes = lax.dynamic_slice_in_dim(decay_code, seq_index * own_width, own_width, 0)
    own_last = lax.dynamic_slice_in_dim(filter_out_master, seq_index * own_width, own_width, 1)
    conv_input, factors, x_zero, projs, normed_b = project(tokens[0], before, has_prev, gain_one, w_in, conv_taps)
    swapped, filt = swap_with_filter(
        channel_order(conv_input, seq_count), filter_in_master, own_last, own_codes, length
    )
    pieces = swapped.reshape(seq_count * per, PIECE, own_width)
    conv_out = conv_forward(firsts, pieces, filt, per)
    conv, w_up = swap_with_rows(conv_out.reshape(seq_count, block_rows, own_width), up_own, 5)
    conv = lane_order(conv)
    (
        output, act_b, grad_up_b, gated_b, normed_two_b, d_resid, grad_branch_b, conv_grad, d_mixed, d_x_zero, d_gain_two, d_skip,
    ) = mlp_block(conv, conv_input, x_zero, tokens[0], cotangent[0], skip_gain, gain_two, w_out, w_up, w_down)
    swapped_grad, up_grad_b, down_grad_b, after_zero = swap_with_grads(
        channel_order(conv_grad, seq_count), cotangent[0], normed_two_b, act_b, grad_up_b, d_x_zero
    )
    grad_pieces = swapped_grad.reshape(seq_count * per, PIECE, own_width)
    mixer_begun, d_taps_high, d_normed_begun = project_back_early(
        d_x_zero, projs, after_zero, has_prev, has_next, conv_taps, w_in, normed_b, grad_branch_b, gated_b
    )
    conv_in_grad, filt_grad = conv_backward(firsts, lasts, pieces, grad_pieces, filt, per)
    back = to_tokens(conv_in_grad.reshape(seq_count, block_rows, own_width))
    _, filter_pull = jax.vjp(
        lambda first, last: make_filter(first, last, own_codes, length), filter_in_master, own_last
    )
    first_grad, own_last_grad = filter_pull(filt_grad)
    back, mixer_begun, d_taps_high, d_normed_begun, first_grad, own_last_grad = lax.optimization_barrier(
        (back, mixer_begun, d_taps_high, d_normed_begun, first_grad, own_last_grad)
    )
    head_grad = skip_gain.reshape(-1, 1, LANES) * d_mixed[:, :HALO] + back[:, :HALO].astype(jnp.float32)
    head_grad = head_grad.transpose(1, 0, 2).reshape(HALO, model_width)
    head = [head_grad * factors[0, :HALO], head_grad * factors[1, :HALO]]
    after = passed_along(jnp.concatenate(head, axis=1).astype(jnp.bfloat16), "seq", -1)
    last_grad = lax.dynamic_update_slice_in_dim(
        jnp.zeros_like(filter_out_master), own_last_grad, seq_index * own_width, 1
    )
    mixer_grad_b, d_taps_low, tokens_grad, d_gain_one = project_back_late(
        mixer_begun, back, d_mixed, factors, projs, after, has_prev, has_next, skip_gain, conv_taps, w_in,
        normed_b, tokens[0], d_resid, gain_one, d_normed_begun,
    )
    d_taps = jnp.concatenate([d_taps_low, d_taps_high], axis=1)
    vectors = jnp.concatenate([d_gain_one, d_gain_two, d_skip], axis=0)
    channel_grad = jnp.concatenate([d_taps, vectors], axis=1)
    small_parts = (channel_grad, first_grad, last_grad)
    large_grads, small_sum, total = grad_sum(
        up_grad_b, down_grad_b, mixer_grad_b, jnp.concatenate([part.reshape(-1) for part in small_parts])
    )
    mlp_grad = large_grads[:2].astype(jnp.float32)
    mixer_grad = large_grads[2].astype(jnp.float32)
    ends = np.cumsum([part.size for part in small_parts])
    channel_grad, first_grad, last_grad = (
        small_sum[end - part.size : end].reshape(part.shape) for part, end in zip(small_parts, ends)
    )
    grad_norm = jnp.sqrt(total)
    factor = jnp.minimum(1.0, clip_limit / (grad_norm + 1e-06))
    mixer_new, mixer_moment_new, mixer_square_new = adam_update(
        mixer_master, mixer_moment, mixer_square, mixer_grad, factor, rate_matrix, weight_decay
    )
    mlp_new, mlp_moment_new, mlp_square_new = adam_update(
        mlp_master, mlp_moment, mlp_square, mlp_grad, factor, rate_matrix, weight_decay
    )
    channel_new, channel_moment_new, channel_square_new = adam_update(
        channel_master, channel_moment, channel_square, channel_grad, factor, rate_small, 0.0
    )
    filter_in_new, filter_in_moment_new, filter_in_square_new = adam_update(
        filter_in_master,
        filter_in_moment,
        filter_in_square,
        first_grad,
        factor,
        rate_small,
        weight_decay,
    )
    filter_out_new, filter_out_moment_new, filter_out_square_new = adam_update(
        filter_out_master,
        filter_out_moment,
        filter_out_square,
        last_grad,
        factor,
        rate_small,
        weight_decay,
    )
    return (
        output[None],
        tokens_grad[None],
        grad_norm.reshape(1),
        channel_grad,
        first_grad,
        last_grad,
        mixer_new,
        mixer_moment_new,
        mixer_square_new,
        mlp_new,
        mlp_moment_new,
        mlp_square_new,
        channel_new,
        channel_moment_new,
        channel_square_new,
        filter_in_new,
        filter_in_moment_new,
        filter_in_square_new,
        filter_out_new,
        filter_out_moment_new,
        filter_out_square_new,
    )


def solution(mesh):
    in_specs = (
        P("dp", "seq", None),
        P("dp", "seq", None),
        P("dp", "seq"),
        P(),
        P("dp", None),
        P("dp", None),
        P("dp", None),
        P(None, "dp", None),
        P(None, "dp", None),
        P(None, "dp", None),
        P(),
        P(),
        P(),
        P(),
        P(),
        P(),
        P(),
        P(),
        P(),
    )
    out_specs = (
        P("dp", "seq", None),
        P("dp", "seq", None),
        P(),
        P(),
        P(),
        P(),
        P("dp", None),
        P("dp", None),
        P("dp", None),
        P(None, "dp", None),
        P(None, "dp", None),
        P(None, "dp", None),
        P(),
        P(),
        P(),
        P(),
        P(),
        P(),
        P(),
        P(),
        P(),
    )
    return jax.shard_map(
        on_device, mesh=mesh, in_specs=in_specs, out_specs=out_specs, check_vma=False
    )
```

```python
import functools
import math

import jax
import jax.numpy as jnp
import numpy as np
from jax import lax
from jax.experimental import pallas as pl
from jax.experimental.pallas import tpu as pltpu
from jax.sharding import PartitionSpec as P

ADAM_STEP = 10


highest = lax.Precision.HIGHEST
norm_eps = 1e-05
clip_limit = 1.0
beta_one = 0.9
beta_two = 0.999
adam_eps = 1e-08
rate_matrix = 0.03
rate_small = 0.2
weight_decay = 0.1
PIECE = 128


def passed_along(value, axis, steps):
    count = lax.axis_size(axis)
    first, last = (max(0, -steps), min(count, count - steps))
    return lax.ppermute(value, axis, [(source, source + steps) for source in range(first, last)])


def filter_features(length, feature_count):
    places = jnp.arange(length, dtype=jnp.float32)[:, None]
    bands = jnp.arange(1, (feature_count - 1) // 2 + 1, dtype=jnp.float32)[None, :]
    angles = 2.0 * math.pi / length * places * bands
    return jnp.concatenate([places / length, jnp.cos(angles), jnp.sin(angles)], axis=1)


def make_filter(first_weight, last_weight, decay_code, length):
    features = filter_features(length, first_weight.shape[0])
    hidden = jnp.sin(jnp.dot(features, first_weight, precision=highest))
    raw_filter = jnp.dot(hidden, last_weight, precision=highest)
    rates = jnp.exp2(-decay_code.astype(jnp.float32))
    places = jnp.arange(length, dtype=jnp.float32)[:, None]
    shaped = raw_filter * jnp.exp(-places * rates[None, :])
    return shaped * lax.rsqrt(jnp.sum(shaped * shaped, axis=0, keepdims=True) + norm_eps)


def odd_tables(parts):
    freq = np.arange(PIECE)[:, None] * 2 + 1
    sample = np.arange(PIECE)[None, :]
    angles = (freq * sample % (4 * PIECE)) * (2.0 * math.pi / (4 * PIECE))
    pair = np.stack([np.cos(angles), -np.sin(angles)]).reshape(2, parts, PIECE // parts, PIECE)
    table = pair.transpose(1, 0, 2, 3).reshape(parts, 2 * PIECE // parts, PIECE).astype(np.float32)
    upper = table.astype(jnp.bfloat16)
    lower = (table - upper.astype(np.float32)).astype(jnp.bfloat16)
    swap = (0, 2, 1)
    forward = np.concatenate([upper, lower, upper], axis=2)
    backward = np.concatenate([upper.transpose(swap), lower.transpose(swap)], axis=1)
    return jnp.asarray(forward), jnp.asarray(backward)


def dot32(left, right):
    return jnp.dot(left, right, preferred_element_type=jnp.float32)


def split_two(value):
    upper = value.astype(jnp.bfloat16)
    return upper, (value - upper.astype(jnp.float32)).astype(jnp.bfloat16)


def freq_signs(rows, width):
    places = lax.broadcasted_iota(jnp.int32, (rows, width), 0)
    return 1.0 - 2.0 * (places % 2).astype(jnp.float32)


def side_by_side(ref, p, count):
    return jnp.concatenate([ref[p + i] for i in range(count)], axis=1)


def in_groups(count, body):
    size = 8

    def one(i, carry):
        for j in range(0, size, 2):
            body(i * size + j)
        return carry

    lax.fori_loop(0, count // size, one, 0)


def to_freq(table, ref, out, count, factor):
    lanes = ref.shape[2]

    def body(p):
        data = side_by_side(ref, p, 2)
        spec = dot32(table[:, : 2 * PIECE], jnp.concatenate([data, data], axis=0))
        if factor != 1.0:
            spec = spec * factor
        out[p] = spec[:, :lanes]
        out[p + 1] = spec[:, lanes:]

    in_groups(count, body)


def filter_spectrum(filt_ref, table, h_ref):
    half = table.shape[0] // 2
    lanes = filt_ref.shape[1]
    signs = freq_signs(half, lanes)
    prev = None
    for k in range(0, filt_ref.shape[0] // PIECE, 2):
        data = jnp.concatenate([filt_ref[i * PIECE : (i + 1) * PIECE, :] for i in (k, k + 1)], axis=1)
        upper, lower = split_two(data)
        both = dot32(table, jnp.concatenate([upper, upper, lower], axis=0))
        for i in range(2):
            spec = both[:, i * lanes : (i + 1) * lanes]
            if prev is None:
                h_ref[0] = spec
            else:
                h_ref[k + i, :half] = spec[:half] - signs * prev[half:]
                h_ref[k + i, half:] = spec[half:] + signs * prev[:half]
            prev = spec


def to_time(table, ref, count, factor, store):
    lanes = ref.shape[2]

    def body(p):
        value = dot32(table[:PIECE], side_by_side(ref, p, 2).astype(jnp.bfloat16))
        if factor != 1.0:
            value = value * factor
        store(p, value[:, :lanes])
        store(p + 1, value[:, lanes:])

    in_groups(count, body)


def emitter(part, parts, out_ref, acc_ref):
    def store(p, value):
        if parts == 1:
            out_ref[p] = value.astype(out_ref.dtype)
            return
        total = value if part == 0 else acc_ref[p] + value
        if part == parts - 1:
            out_ref[p] = total.astype(out_ref.dtype)
        else:
            acc_ref[p] = total

    return store


def conv_forward_kernel(per, first_ref, x_ref, filt_ref, f_ref, i_ref, o_ref, xs, hs, *rest):
    count, _, lanes = x_ref.shape
    blocks = count // per
    parts = f_ref.shape[0]
    half = PIECE // parts
    tiles = half // 8
    for part in range(parts):
        filter_spectrum(filt_ref, f_ref[part], hs)
        to_freq(f_ref[part], x_ref, xs, count, 1.0)

        def one_tile(step, carry):
            b = blocks - 1 - step // tiles
            row = pl.multiple_of((step % tiles) * 8, 8)
            re = pl.ds(row, 8)
            im = pl.ds(row + half, 8)

            def add_pairs(acc, a, lag, diagonal):
                acc = list(acc)
                for j in range(per):
                    sr, si = xs[a * per + j, re], xs[a * per + j, im]
                    for i in range(j if diagonal else 0, per):
                        hr, hi = hs[lag + i - j, re], hs[lag + i - j, im]
                        acc[2 * i] = acc[2 * i] + (sr * hr - si * hi)
                        acc[2 * i + 1] = acc[2 * i + 1] + (sr * hi + si * hr)
                return tuple(acc)

            acc = tuple(jnp.zeros((8, lanes), jnp.float32) for _ in range(2 * per))
            acc = add_pairs(acc, b, 0, True)
            acc = lax.fori_loop(first_ref[b], b, lambda a, c: add_pairs(c, a, (b - a) * per, False), acc)
            for i in range(per):
                xs[b * per + i, re] = acc[2 * i]
                xs[b * per + i, im] = acc[2 * i + 1]
            return carry

        lax.fori_loop(0, blocks * tiles, one_tile, 0)
        to_time(i_ref[part], xs, count, 1.0 / PIECE, emitter(part, parts, o_ref, rest[0] if rest else None))


def conv_backward_kernel(
    per, first_ref, last_ref, x_ref, g_ref, filt_ref, f_ref, i_ref, dx_ref, df_ref, xs, gs, hs, dh, *rest
):
    count, _, lanes = x_ref.shape
    blocks = count // per
    taps = filt_ref.shape[0] // PIECE
    parts = f_ref.shape[0]
    half = PIECE // parts
    tiles = half // 8
    for part in range(parts):
        filter_spectrum(filt_ref, f_ref[part], hs)
        to_freq(f_ref[part], x_ref, xs, count, 1.0)
        to_freq(f_ref[part], g_ref, gs, count, 1.0 / PIECE)
        dh[...] = jnp.zeros_like(dh)

        def one_tile(step, carry):
            a = step // tiles
            row = pl.multiple_of((step % tiles) * 8, 8)
            re = pl.ds(row, 8)
            im = pl.ds(row + half, 8)

            def add_pairs(acc, b, lag, diagonal):
                acc = list(acc)
                for delta in range(0 if diagonal else 1 - per, per):
                    hr, hi = hs[lag + delta, re], hs[lag + delta, im]
                    tr, ti = dh[lag + delta, re], dh[lag + delta, im]
                    for j in range(max(0, -delta), per - max(0, delta)):
                        sr, si = xs[a * per + j, re], xs[a * per + j, im]
                        gr, gi = gs[b * per + j + delta, re], gs[b * per + j + delta, im]
                        acc[2 * j] = acc[2 * j] + (hr * gr + hi * gi)
                        acc[2 * j + 1] = acc[2 * j + 1] + (hr * gi - hi * gr)
                        tr = tr + (sr * gr + si * gi)
                        ti = ti + (sr * gi - si * gr)
                    dh[lag + delta, re] = tr
                    dh[lag + delta, im] = ti
                return tuple(acc)

            acc = tuple(jnp.zeros((8, lanes), jnp.float32) for _ in range(2 * per))
            acc = add_pairs(acc, a, 0, True)
            acc = lax.fori_loop(a + 1, last_ref[a] + 1, lambda b, c: add_pairs(c, b, (b - a) * per, False), acc)
            for j in range(per):
                xs[a * per + j, re] = acc[2 * j]
                xs[a * per + j, im] = acc[2 * j + 1]
            return carry

        lax.fori_loop(0, blocks * tiles, one_tile, 0)
        to_time(i_ref[part], xs, count, 1.0, emitter(part, parts, dx_ref, rest[0] if rest else None))
        signs = freq_signs(half, lanes)
        back_u, back_l = i_ref[part, :PIECE], i_ref[part, PIECE:]
        for k in range(taps):
            grad = dh[k]
            if k + 1 < taps:
                grad = grad + jnp.concatenate([signs * dh[k + 1, half:], -signs * dh[k + 1, :half]], axis=0)
            upper, lower = split_two(grad)
            value = dot32(back_u, upper) + (dot32(back_l, upper) + dot32(back_u, lower))
            rows = slice(k * PIECE, (k + 1) * PIECE)
            df_ref[rows, :] = value if part == 0 else df_ref[rows, :] + value


VMEM_SPEC = pl.BlockSpec(memory_space=pltpu.VMEM)
SMEM_SPEC = pl.BlockSpec(memory_space=pltpu.SMEM)


def conv_parts(count):
    return 1 if count <= 64 else 4


def conv_forward(firsts, pieces, filt, per):
    count, _, lanes = pieces.shape
    taps = filt.shape[0] // PIECE
    parts = conv_parts(count)
    spec = (2 * PIECE // parts, lanes)
    scratch = [pltpu.VMEM((count,) + spec, jnp.float32), pltpu.VMEM((taps,) + spec, jnp.float32)]
    if parts > 1:
        scratch.append(pltpu.VMEM(pieces.shape, jnp.float32))
    return pl.pallas_call(
        functools.partial(conv_forward_kernel, per),
        out_shape=jax.ShapeDtypeStruct(pieces.shape, jnp.bfloat16),
        in_specs=[SMEM_SPEC] + [VMEM_SPEC] * 4,
        out_specs=VMEM_SPEC,
        scratch_shapes=scratch,
        compiler_params=pltpu.CompilerParams(vmem_limit_bytes=60 * 2**20),
        cost_estimate=pl.CostEstimate(flops=2 * 10**9, bytes_accessed=8 * 10**6, transcendentals=0),
        name="long_conv",
    )(firsts, pieces, filt, *odd_tables(parts))


def conv_backward(firsts, lasts, pieces, grads, filt, per):
    count, _, lanes = pieces.shape
    taps = filt.shape[0] // PIECE
    parts = conv_parts(count)
    spec = (2 * PIECE // parts, lanes)
    scratch = [pltpu.VMEM((n,) + spec, jnp.float32) for n in (count, count, taps, taps)]
    if parts > 1:
        scratch.append(pltpu.VMEM(pieces.shape, jnp.float32))
    return pl.pallas_call(
        functools.partial(conv_backward_kernel, per),
        out_shape=(
            jax.ShapeDtypeStruct(pieces.shape, jnp.bfloat16),
            jax.ShapeDtypeStruct(filt.shape, jnp.float32),
        ),
        in_specs=[SMEM_SPEC] * 2 + [VMEM_SPEC] * 5,
        out_specs=(VMEM_SPEC, VMEM_SPEC),
        scratch_shapes=scratch,
        compiler_params=pltpu.CompilerParams(vmem_limit_bytes=60 * 2**20),
        cost_estimate=pl.CostEstimate(flops=4 * 10**9, bytes_accessed=10**7, transcendentals=0),
        name="long_conv_back",
    )(firsts, lasts, pieces, grads, filt, *odd_tables(parts))


def channel_order(value, count):
    groups, rows, lanes = value.shape
    if groups != count:
        own = groups * lanes // count
        value = value.reshape(groups, rows, lanes // own, own).transpose(0, 2, 1, 3).reshape(count, rows, own)
    return value


def lane_order(value):
    _, rows, own = value.shape
    if own != LANES:
        value = value.reshape(-1, LANES // own, rows, own).transpose(0, 2, 1, 3).reshape(-1, rows, LANES)
    return value


def to_tokens(value):
    return lane_order(lax.all_to_all(value, "seq", 0, 0, tiled=True))


MESH_ID = pl.DeviceIdType.MESH
def remote(src, dst, send, recv, device):
    return pltpu.make_async_remote_copy(src, dst, send, recv, device_id=device, device_id_type=MESH_ID)


def greet(partners):
    barrier = pltpu.get_barrier_semaphore()
    for partner in partners:
        pl.semaphore_signal(barrier, inc=1, device_id=partner, device_id_type=MESH_ID)
    pl.semaphore_wait(barrier, len(partners))


def place_of(sizes):
    ny, nx, nz = sizes
    dp, seq = lax.axis_index("dp"), lax.axis_index("seq")
    y, c = dp // 2, dp % 2
    z, x = seq // nx, seq % nx

    def at_y(step):
        other = lax.rem(y + step, ny)
        return other, (other * 2 + c, seq)

    def at_x(step):
        other = lax.rem(x + step, nx)
        return other, (dp, z * nx + other)

    def at_z(step):
        other = lax.rem(z + step, nz)
        return other, (dp, other * nx + x)

    return (y, c, z, x), (y * 2 + 1 - c, seq), at_y, at_x, at_z


def axis_sizes():
    seq = lax.axis_size("seq")
    return lax.axis_size("dp") // 2, seq // 4, 4


def wide(ref):
    return ref[...].astype(jnp.float32)


def staged_sum(sizes, grads, out, sq, scratch):
    own, r0, r1, r2, r3, load_sem, s0, t0, s1, t1, s2, t2, s3, t3, s4, t4, s5, t5 = scratch
    ny, nx, nz = sizes
    strip = r0.shape[2]
    strips = out.shape[1] // strip
    width = out.shape[2]
    half, quarter = width // nx, width // nx // nz
    total = len(grads) * strips
    (y, c, z, x), sibling, at_y, at_x, at_z = place_of(sizes)

    def rows_of(k):
        return pl.ds(pl.multiple_of(lax.rem(k, strips) * strip, strip), strip)

    def cols(start, size):
        return pl.ds(pl.multiple_of(start * size, size), size)

    def core_copy(k, g):
        return remote(g.at[:, 1 - c, rows_of(k)], r0.at[k], s0.at[k], t0.at[k], sibling)

    def own_copy(k, g):
        slot = lax.rem(k, 4)
        return pltpu.make_async_copy(g.at[:, c, rows_of(k)], own.at[slot], load_sem.at[slot])

    def start_first(k):
        for i, g in enumerate(grads):

            @pl.when(k // strips == i)
            def _():
                core_copy(k, g).start()
                own_copy(k, g).start()

    def y_copy(k, i):
        other, device = at_y(i)
        return remote(r0.at[k, other], r1.at[k, ny - 1 - i], s1.at[k, i - 1], t1.at[k, ny - 1 - i], device)

    def x_copy(k, i):
        other, device = at_x(i)
        return remote(r1.at[k, 0, :, cols(other, half)], r2.at[k, nx - 1 - i], s2.at[k, i - 1], t2.at[k, nx - 1 - i], device)

    def z_copy(k, i):
        other, device = at_z(i)
        return remote(r2.at[k, 0, :, cols(other, quarter)], r3.at[k, nz - 1 - i], s3.at[k, i - 1], t3.at[k, nz - 1 - i], device)

    def z_back(k, i):
        other, device = at_z(i)
        part = out.at[k // strips, rows_of(k), cols(x * nz + z, quarter)]
        return remote(part, part, s4.at[k, i - 1], t4.at[k, nz - 1 - i], device)

    def x_back(k, i):
        other, device = at_x(i)
        part = out.at[k // strips, rows_of(k), cols(x, half)]
        return remote(part, part, s5.at[k, i - 1], t5.at[k, nx - 1 - i], device)

    def tiles(size, body):
        piece = min(size, TILE // strip)

        def one(i, carry):
            body(pl.ds(pl.multiple_of(i * piece, piece), piece))
            return carry

        lax.fori_loop(0, size // piece, one, 0)

    def begin():
        start_first(jnp.int32(0))
        start_first(jnp.int32(1))

    def step(t):
        @pl.when(t + 2 < total)
        def _():
            start_first(t + 2)

        @pl.when(t < total)
        def _():
            k, slot = t, lax.rem(t, 4)
            core_copy(k, grads[0]).wait_recv()
            own_copy(k, grads[0]).wait()
            for other in range(ny):

                def add(at):
                    r0[k, other, :, at] = (wide(r0.at[k, other, :, at]) + wide(own.at[slot, other, :, at])).astype(r0.dtype)

                tiles(width, add)
            for i in range(1, ny):
                y_copy(k, i).start()

        @pl.when((t >= OFFSETS[0]) & (t < total + OFFSETS[0]))
        def _():
            k = t - OFFSETS[0]
            for i in range(1, ny):
                y_copy(k, i).wait_recv()

            def add(at):
                value = wide(r0.at[k, y, :, at])
                for i in range(ny - 1):
                    value = value + wide(r1.at[k, i, :, at])
                r1[k, 0, :, at] = value.astype(r1.dtype)

            tiles(width, add)
            for i in range(1, nx):
                x_copy(k, i).start()

        @pl.when((t >= OFFSETS[1]) & (t < total + OFFSETS[1]))
        def _():
            k = t - OFFSETS[1]
            for i in range(1, nx):
                x_copy(k, i).wait_recv()

            def add(at):
                mine = pl.ds(pl.multiple_of(x * half + at.start, 128), at.size)
                value = wide(r1.at[k, 0, :, mine])
                for i in range(nx - 1):
                    value = value + wide(r2.at[k, i, :, at])
                r2[k, 0, :, at] = value.astype(r2.dtype)

            tiles(half, add)
            for i in range(1, nz):
                z_copy(k, i).start()

        @pl.when((t >= OFFSETS[2]) & (t < total + OFFSETS[2]))
        def _():
            k = t - OFFSETS[2]
            for i in range(1, nz):
                z_copy(k, i).wait_recv()
            value = wide(r2.at[k, 0, :, cols(z, quarter)])
            for i in range(nz - 1):
                value = value + wide(r3.at[k, i])
            sq[...] += value * value
            out[k // strips, rows_of(k), cols(x * nz + z, quarter)] = value.astype(out.dtype)
            for i in range(1, nz):
                z_back(k, i).start()

        @pl.when((t >= OFFSETS[3]) & (t < total + OFFSETS[3]))
        def _():
            k = t - OFFSETS[3]
            for i in range(1, nz):
                z_back(k, i).wait_recv()
            for i in range(1, nx):
                x_back(k, i).start()

    def retire(k):
        for i in range(1, nx):
            x_back(k, i).wait()
            x_copy(k, i).wait_send()
        for i in range(1, nz):
            z_copy(k, i).wait_send()
            z_back(k, i).wait_send()
        for i in range(1, ny):
            y_copy(k, i).wait_send()
        core_copy(k, grads[0]).wait_send()

    def finish(first):
        def one(k, carry):
            retire(k)
            return carry

        lax.fori_loop(first, total, one, 0)

    return begin, step, retire, finish, total + OFFSETS[3]


def staged_scratch(sizes, count, rows, strip, width):
    ny, nx, nz = sizes
    total = count * rows // strip
    half = jnp.bfloat16
    dma = pltpu.SemaphoreType.DMA
    pairs = [(total,), (total, ny - 1), (total, nx - 1), (total, nz - 1), (total, nz - 1), (total, nx - 1)]
    return [
        pltpu.VMEM((4, ny, strip, width), half),
        pltpu.VMEM((total, ny, strip, width), half),
        pltpu.VMEM((total, ny - 1, strip, width), half),
        pltpu.VMEM((total, nx - 1, strip, width // nx), half),
        pltpu.VMEM((total, nz - 1, strip, width // nx // nz), half),
        dma((4,)),
    ] + [dma(p) for p in pairs for _ in range(2)]


STAGED = 18
TILE = 65536
OFFSETS = (1, 2, 3, 4)
BEHIND = 8


def grad_sum_kernel(sizes, g0, g1, g2, small, out, small_out, norm, *scratch):
    staged, (b0, b1, b2, b3, sq, norms, small_send, small_recv, norm_send, norm_recv) = scratch[:STAGED], scratch[STAGED:]
    ny, nx, nz = sizes
    (y, c, z, x), sibling, at_y, at_x, at_z = place_of(sizes)
    partners = [sibling] + [at_y(i)[1] for i in range(1, ny)] + [at_x(i)[1] for i in range(1, nx)]
    greet(partners + [at_z(i)[1] for i in range(1, nz)])
    axes = ((2, c, None), (ny, y, at_y), (nx, x, at_x), (nz, z, at_z))
    base = (0, 1, ny, ny + nx - 1, ny + nx + nz - 2)

    def small_copies(stage):
        def numbered(first, pairs):
            return [
                remote(src, dst, small_send.at[first + i], small_recv.at[first + back], device)
                for i, back, src, dst, device in pairs
            ]

        def spread(axis, pick):
            count, _, at = axes[axis]
            return [(i - 1, count - 1 - i) + pick(i, *at(i)) for i in range(1, count)]

        if stage == 0:
            return numbered(0, [(0, 0, small.at[:, 1 - c], b0, sibling)])
        if stage == 1:
            return numbered(base[1], spread(1, lambda i, o, d: (b0.at[o], b1.at[ny - 1 - i], d)))
        if stage == 2:
            return numbered(base[2], spread(2, lambda i, o, d: (b1.at[0, o], b2.at[nx - 1 - i], d)))
        if stage == 3:
            return numbered(base[3], spread(3, lambda i, o, d: (b2.at[0, o], b3.at[nz - 1 - i], d)))
        again = base[4]
        if stage == 4:
            part = small_out.at[y, c, x, z]
            return numbered(again + base[3], spread(3, lambda i, o, d: (part, part, d)))
        if stage == 5:
            part = small_out.at[y, c, x]
            return numbered(again + base[2], spread(2, lambda i, o, d: (part, part, d)))
        if stage == 6:
            part = small_out.at[y, c]
            return numbered(again + base[1], spread(1, lambda i, o, d: (part, part, d)))
        part = small_out.at[:, c]
        return numbered(again, [(0, 0, part, part, sibling)])

    def small_step(stage):
        if stage > 0:
            for copy in small_copies(stage - 1):
                copy.wait_recv()
        if stage == 1:
            b0[...] += small[:, c]
        if stage == 2:
            value = b0[y]
            for i in range(ny - 1):
                value = value + b1[i]
            b1[0] = value
        if stage == 3:
            value = b1[0, x]
            for i in range(nx - 1):
                value = value + b2[i]
            b2[0] = value
        if stage == 4:
            value = b2[0, z]
            for i in range(nz - 1):
                value = value + b3[i]
            small_out[y, c, x, z] = value
            for row in range(0, value.shape[0], 8):
                sq[:8, :128] += value[row : row + 8] * value[row : row + 8]
        if stage < 8:
            for copy in small_copies(stage):
                copy.start()

    def norm_copies(stage):
        count, place, at = axes[stage]
        devices = [sibling] if at is None else [at(i)[1] for i in range(1, count)]
        return [
            remote(norms.at[stage, place], norms.at[stage, place], norm_send.at[stage, i], norm_recv.at[stage, len(devices) - 1 - i], device)
            for i, device in enumerate(devices)
        ]

    begin, step, retire, finish, steps = staged_sum(sizes, (g0, g1, g2), out, sq, staged)
    sq[...] = jnp.zeros_like(sq)
    begin()

    def one_step(t, carry):
        step(t)
        for stage in range(9):

            @pl.when(t == stage)
            def _():
                small_step(stage)

        @pl.when(t >= BEHIND)
        def _():
            retire(t - BEHIND)

        return carry

    lax.fori_loop(0, steps - 1, one_step, 0)
    tile = jnp.zeros((8, 128), jnp.float32)
    for row in range(0, sq.shape[0], 8):
        for col in range(0, sq.shape[1], 128):
            tile = tile + sq[row : row + 8, col : col + 128]
    for stage in range(4):
        count, place, _ = axes[stage]
        norms[stage, place] = tile
        for copy in norm_copies(stage):
            copy.start()
        if stage == 1:
            step(jnp.int32(steps - 1))
        for copy in norm_copies(stage):
            copy.wait_recv()
        tile = norms[stage, 0]
        for i in range(1, count):
            tile = tile + norms[stage, i]
    norm[...] = tile
    for stage in range(4):
        for copy in norm_copies(stage):
            copy.wait_send()
    for stage in range(8):
        for copy in small_copies(stage):
            copy.wait_send()
    finish(steps - 1 - BEHIND)


def grad_sum(up, down, mixer, small):
    sizes = ny, nx, nz = axis_sizes()
    rows_all, width = mixer.shape
    seq = nx * nz
    rows = rows_all // (2 * ny)
    strip = 32
    full = jnp.float32
    dma = pltpu.SemaphoreType.DMA
    parts = 2 * ny * seq
    piece = -(-small.shape[0] // (parts * 1024)) * 8
    small = jnp.pad(small, (0, parts * piece * 128 - small.shape[0])).reshape(ny, 2, nx, nz, piece, 128)
    most = max(2, ny, nx, nz)
    smalls = 2 * (ny + nx + nz - 2)
    large, summed, norm = pl.pallas_call(
        functools.partial(grad_sum_kernel, sizes),
        out_shape=(
            jax.ShapeDtypeStruct((3, rows, width), jnp.bfloat16),
            jax.ShapeDtypeStruct(small.shape, full),
            jax.ShapeDtypeStruct((8, 128), full),
        ),
        in_specs=[pl.BlockSpec(memory_space=pltpu.HBM)] * 3 + [VMEM_SPEC],
        out_specs=(VMEM_SPEC,) * 3,
        scratch_shapes=staged_scratch(sizes, 3, rows, strip, width)
        + [
            pltpu.VMEM((ny, nx, nz, piece, 128), full),
            pltpu.VMEM((ny - 1, nx, nz, piece, 128), full),
            pltpu.VMEM((nx - 1, nz, piece, 128), full),
            pltpu.VMEM((nz - 1, piece, 128), full),
            pltpu.VMEM((strip, width // seq), full),
            pltpu.VMEM((4, most, 8, 128), full),
            dma((smalls,)),
            dma((smalls,)),
            dma((4, most - 1)),
            dma((4, most - 1)),
        ],
        compiler_params=pltpu.CompilerParams(vmem_limit_bytes=35 * 2**20, collective_id=1, has_side_effects=True),
        cost_estimate=pl.CostEstimate(flops=10**8, bytes_accessed=20 * 10**6, transcendentals=0),
        name="grad_sum",
    )(*(g.reshape(ny, 2, rows, width) for g in (up, down, mixer)), small)
    return large, summed.reshape(-1), jnp.sum(norm)


def row_gather(sizes, own, full, width, pieces, sems):
    a_send, a_recv, b_send, b_recv, c_send, c_recv, d_send, d_recv, e_send, e_recv = sems
    ny = sizes[0]
    rows = own.shape[0]
    half = width // 2
    size = half // pieces
    (y, c, _, _), sibling, at_y, _, _ = place_of(sizes)
    dp, seq = lax.axis_index("dp"), lax.axis_index("seq")
    side = lax.rem(seq, 2)
    pair = (dp, seq + 1 - 2 * side)

    def at_rows(d):
        return pl.ds(pl.multiple_of(d * rows, rows), rows)

    def at_cols(which, p):
        return pl.ds(pl.multiple_of(which * half + p * size, size), size)

    def core_copy():
        return remote(own, full.at[at_rows(dp)], a_send.at[0], a_recv.at[0], sibling)

    def y_copy(i, p):
        _, device = at_y(i)
        cols = at_cols(side, p)
        return remote(own.at[:, cols], full.at[at_rows(dp), cols], b_send.at[i - 1, p], b_recv.at[ny - 1 - i, p], device)

    def pass_on(i, p, which, send, recv, device):
        other, _ = at_y(ny - i)
        part = full.at[at_rows(other * 2 + c), at_cols(which, p)]
        return remote(part, part, send.at[ny - 1 - i, p], recv.at[ny - 1 - i, p], device)

    def x_copy(i, p):
        return pass_on(i, p, side, c_send, c_recv, pair)

    def first_copy(i, p):
        return pass_on(i, p, side, d_send, d_recv, sibling)

    def second_copy(i, p):
        return pass_on(i, p, 1 - side, e_send, e_recv, sibling)

    every = [(i, p) for p in range(pieces) for i in range(1, ny)]

    def start():
        for i, p in every:
            y_copy(i, p).start()
        core_copy().start()

    def first_half(p):
        for i in range(1, ny):
            y_copy(i, p).wait_recv()
            x_copy(i, p).start()
            first_copy(i, p).start()

    def second_half(p):
        for i in range(1, ny):
            x_copy(i, p).wait_recv()
            second_copy(i, p).start()

    def finish():
        core_copy().wait()
        for i, p in every:
            y_copy(i, p).wait_send()
            x_copy(i, p).wait_send()
            first_copy(i, p).wait()
            second_copy(i, p).wait()

    return start, first_half, second_half, finish


def gather_sems(sizes, pieces):
    dma = pltpu.SemaphoreType.DMA
    return [dma((1,))] * 2 + [dma((sizes[0] - 1, pieces))] * 8


GATHER = 10


def greet_near(sizes, count):
    _, sibling, at_y, _, _ = place_of(sizes)
    dp, me = lax.axis_index("dp"), lax.axis_index("seq")
    others = [(dp, lax.rem(me + i, count)) for i in range(1, count)]
    greet([sibling] + [at_y(i)[1] for i in range(1, sizes[0])] + others)
    return others


def open_kernel(sizes, count, pieces, mixer, mlp, tok, first, w_in, w_out, up_out, down_out, before, firsts,
                own, mlp_in, mlp_sem, halo_send, halo_recv, first_send, first_recv, *sems):
    rows = own.shape[0]
    lane_count = own.shape[1]
    me, dp = lax.axis_index("seq"), lax.axis_index("dp")
    chunk = mlp_in.shape[2]
    chunks = rows // chunk

    def load(k):
        return pltpu.make_async_copy(mlp.at[:, k * chunk : (k + 1) * chunk], mlp_in.at[k % 2], mlp_sem.at[k % 2])

    load(0).start()
    own[...] = mixer[:, :lane_count].astype(jnp.bfloat16)
    others = greet_near(sizes, count)
    start, first_half, second_half, finish = row_gather(sizes, own, w_in, lane_count, pieces, sems)
    start()
    halo = remote(tok.at[tok.shape[0] - HALO :], before, halo_send, halo_recv, others[0])
    halo.start()
    announced = [
        remote(first, firsts.at[me], first_send.at[i], first_recv.at[count - 2 - i], device) for i, device in enumerate(others)
    ]
    for copy in announced:
        copy.start()
    firsts[me] = first[...]
    w_in[pl.ds(pl.multiple_of(dp * rows, rows), rows), :] = own[...]
    w_out[...] = mixer[:, lane_count:].astype(jnp.bfloat16)
    for k in range(max(chunks, pieces)):
        if k < chunks:
            if k + 1 < chunks:
                load(k + 1).start()
            load(k).wait()
            at = slice(k * chunk, (k + 1) * chunk)
            up_out[at] = mlp_in[k % 2, 0].astype(jnp.bfloat16)
            down_out[at] = mlp_in[k % 2, 1].astype(jnp.bfloat16)
        if k < pieces:
            first_half(k)
        if 2 <= k < pieces:
            second_half(k - 2)
    for k in range(max(0, pieces - 2), pieces):
        second_half(k)
    halo.wait()
    for copy in announced:
        copy.wait()
    finish()


def open_gather(mixer, mlp, tok, first, count):
    sizes = axis_sizes()
    rows, total = mixer.shape
    width = tok.shape[1]
    lane_count = total - width
    dp = 2 * sizes[0]
    pieces = 6
    half = jnp.bfloat16
    dma = pltpu.SemaphoreType.DMA
    chunk = rows // 4
    first = jnp.broadcast_to(first.reshape(1, 1), (8, 128))
    return pl.pallas_call(
        functools.partial(open_kernel, sizes, count, pieces),
        out_shape=(
            jax.ShapeDtypeStruct((rows * dp, lane_count), half),
            jax.ShapeDtypeStruct((rows, width), half),
            jax.ShapeDtypeStruct(mlp.shape[1:], half),
            jax.ShapeDtypeStruct(mlp.shape[1:], half),
            jax.ShapeDtypeStruct((HALO, width), half),
            jax.ShapeDtypeStruct((count, 8, 128), jnp.int32),
        ),
        in_specs=[VMEM_SPEC, pl.BlockSpec(memory_space=pltpu.HBM), VMEM_SPEC, VMEM_SPEC],
        out_specs=(VMEM_SPEC,) * 6,
        scratch_shapes=[
            pltpu.VMEM((rows, lane_count), half),
            pltpu.VMEM((2, 2, chunk, mlp.shape[2]), jnp.float32),
            dma((2,)),
            dma,
            dma,
            dma((count - 1,)),
            dma((count - 1,)),
        ]
        + gather_sems(sizes, pieces),
        compiler_params=pltpu.CompilerParams(vmem_limit_bytes=60 * 2**20, collective_id=3, has_side_effects=True),
        cost_estimate=pl.CostEstimate(flops=10**6, bytes_accessed=60 * 10**6, transcendentals=0),
        name="open_gather",
    )(mixer, mlp, tok, first)


def swap_kernel(sizes, pieces, value, own, swapped, full, swap_send, swap_recv, self_sem, *sems):
    count = value.shape[0]
    rows = own.shape[0]
    me, dp = lax.axis_index("seq"), lax.axis_index("dp")
    others = greet_near(sizes, count)
    start, first_half, second_half, finish = row_gather(sizes, own, full, own.shape[1], pieces, sems)
    start()
    copies = [
        remote(value.at[device[1]], swapped.at[me], swap_send.at[i], swap_recv.at[count - 2 - i], device)
        for i, device in enumerate(others)
    ]
    for copy in copies:
        copy.start()
    kept = [
        pltpu.make_async_copy(value.at[me], swapped.at[me], self_sem.at[0]),
        pltpu.make_async_copy(own, full.at[pl.ds(pl.multiple_of(dp * rows, rows), rows)], self_sem.at[1]),
    ]
    for copy in kept:
        copy.start()
    for p in range(pieces):
        first_half(p)
        if p > 0:
            second_half(p - 1)
    second_half(pieces - 1)
    for copy in kept + copies:
        copy.wait()
    finish()


def swap_with_rows(value, own, number):
    sizes = axis_sizes()
    count = value.shape[0]
    rows, width = own.shape
    pieces = 4
    dma = pltpu.SemaphoreType.DMA
    hbm = pl.BlockSpec(memory_space=pltpu.HBM)
    return pl.pallas_call(
        functools.partial(swap_kernel, sizes, pieces),
        out_shape=(
            jax.ShapeDtypeStruct(value.shape, value.dtype),
            jax.ShapeDtypeStruct((rows * 2 * sizes[0], width), own.dtype),
        ),
        in_specs=[hbm, VMEM_SPEC],
        out_specs=(hbm, hbm),
        scratch_shapes=[dma((count - 1,)), dma((count - 1,)), dma((2,))] + gather_sems(sizes, pieces),
        compiler_params=pltpu.CompilerParams(vmem_limit_bytes=60 * 2**20, collective_id=number, has_side_effects=True),
        cost_estimate=pl.CostEstimate(flops=10**6, bytes_accessed=40 * 10**6, transcendentals=0),
        name="swap_with_rows",
    )(value, own)


def swap_filter_kernel(sizes, pieces, value, own, features, first, last, codes, swapped, full, filt, swap_send, swap_recv, self_sem, *sems):
    count = value.shape[0]
    me, dp = lax.axis_index("seq"), lax.axis_index("dp")
    rows = own.shape[0]
    others = greet_near(sizes, count)
    start_rows, first_half, second_half, finish = row_gather(sizes, own, full, own.shape[1], pieces, sems)
    start_rows()
    copies = [
        remote(value.at[device[1]], swapped.at[me], swap_send.at[i], swap_recv.at[count - 2 - i], device)
        for i, device in enumerate(others)
    ]
    for copy in copies:
        copy.start()
    kept = [
        pltpu.make_async_copy(value.at[me], swapped.at[me], self_sem.at[0]),
        pltpu.make_async_copy(own, full.at[pl.ds(pl.multiple_of(dp * rows, rows), rows)], self_sem.at[1]),
    ]
    for copy in kept:
        copy.start()
    rates = jnp.exp2(-codes[...].astype(jnp.float32))
    total = jnp.zeros_like(rates)
    step = 2 * PIECE
    for start in range(0, filt.shape[0], step):
        hidden = jnp.sin(jnp.dot(features[start : start + step], first[...], precision=highest, preferred_element_type=jnp.float32))
        raw = jnp.dot(hidden, last[...], precision=highest, preferred_element_type=jnp.float32)
        places = (lax.broadcasted_iota(jnp.int32, raw.shape, 0) + start).astype(jnp.float32)
        shaped = raw * jnp.exp(-places * rates)
        total = total + jnp.sum(shaped * shaped, axis=0, keepdims=True)
        filt[start : start + step] = shaped
        turn = start // step
        if turn >= 4 and turn - 4 < pieces:
            first_half(turn - 4)
        if turn >= 6 and turn - 6 < pieces:
            second_half(turn - 6)
    scale = lax.rsqrt(total + norm_eps)
    for start in range(0, filt.shape[0], step):
        filt[start : start + step] = filt[start : start + step] * scale
    for copy in kept + copies:
        copy.wait()
    finish()


def swap_with_filter(value, own, first, last, codes, length):
    count = value.shape[0]
    sizes = axis_sizes()
    rows, width = own.shape
    pieces = 2
    dma = pltpu.SemaphoreType.DMA
    hbm = pl.BlockSpec(memory_space=pltpu.HBM)
    places = np.arange(length, dtype=np.float32)[:, None]
    bands = np.arange(1, (first.shape[0] - 1) // 2 + 1, dtype=np.float32)[None, :]
    angles = (np.float32(2.0 * math.pi / length) * places * bands).astype(np.float32)
    features = np.concatenate([places / np.float32(length), np.cos(angles), np.sin(angles)], axis=1).astype(np.float32)
    return pl.pallas_call(
        functools.partial(swap_filter_kernel, sizes, pieces),
        out_shape=(
            jax.ShapeDtypeStruct(value.shape, value.dtype),
            jax.ShapeDtypeStruct((rows * 2 * sizes[0], width), own.dtype),
            jax.ShapeDtypeStruct((length, last.shape[1]), jnp.float32),
        ),
        in_specs=[hbm] + [VMEM_SPEC] * 5,
        out_specs=(hbm, hbm, VMEM_SPEC),
        scratch_shapes=[dma((count - 1,)), dma((count - 1,)), dma((2,))] + gather_sems(sizes, pieces),
        compiler_params=pltpu.CompilerParams(vmem_limit_bytes=60 * 2**20, collective_id=4, has_side_effects=True),
        cost_estimate=pl.CostEstimate(flops=10**8, bytes_accessed=10 * 10**6, transcendentals=10**6),
        name="swap_with_filter",
    )(value, own, jnp.asarray(features), first, last, codes.reshape(1, -1))


GRAD_TILE = 512


def swap_grads_kernel(value, cot, normed, act, g_up, zero, swapped, d_up, d_down, after, left_t, right, made,
                      swap_send, swap_recv, self_sem, load_sem, store_sem, halo_send, halo_recv):
    count = value.shape[0]
    me, dp = lax.axis_index("seq"), lax.axis_index("dp")
    others = [(dp, lax.rem(me + i, count)) for i in range(1, count)]
    greet(others)
    copies = [
        remote(value.at[device[1]], swapped.at[me], swap_send.at[i], swap_recv.at[count - 2 - i], device)
        for i, device in enumerate(others)
    ]
    for copy in copies:
        copy.start()
    halo = remote(zero.at[:HALO], after, halo_send, halo_recv, others[-1])
    halo.start()
    kept = pltpu.make_async_copy(value.at[me], swapped.at[me], self_sem)
    kept.start()
    for left, source, target in ((cot, act, d_down), (normed, g_up, d_up)):
        tiles = source.shape[1] // GRAD_TILE

        def at(j):
            return pl.ds(pl.multiple_of(j * GRAD_TILE, GRAD_TILE), GRAD_TILE)

        def load(j):
            slot = lax.rem(j, 2)
            return pltpu.make_async_copy(source.at[:, at(j)], right.at[slot], load_sem.at[slot])

        def store(j):
            slot = lax.rem(j, 2)
            return pltpu.make_async_copy(made.at[slot], target.at[:, at(j)], store_sem.at[slot])

        load(jnp.int32(0)).start()
        left_t[...] = left[...].T

        def one(j, carry):
            slot = lax.rem(j, 2)

            @pl.when(j + 1 < tiles)
            def _():
                load(j + 1).start()

            load(j).wait()

            @pl.when(j >= 2)
            def _():
                store(j - 2).wait()

            made[slot] = dot32(left_t[...], right[slot]).astype(jnp.bfloat16)
            store(j).start()
            return carry

        lax.fori_loop(0, tiles, one, 0)
        store(jnp.int32(tiles - 2)).wait()
        store(jnp.int32(tiles - 1)).wait()
    kept.wait()
    halo.wait()
    for copy in copies:
        copy.wait()


def swap_with_grads(value, cot, normed, act, g_up, zero):
    count = value.shape[0]
    rows, width = cot.shape
    hidden = act.shape[1]
    half = jnp.bfloat16
    dma = pltpu.SemaphoreType.DMA
    hbm = pl.BlockSpec(memory_space=pltpu.HBM)
    return pl.pallas_call(
        swap_grads_kernel,
        out_shape=(
            jax.ShapeDtypeStruct(value.shape, value.dtype),
            jax.ShapeDtypeStruct((width, hidden), half),
            jax.ShapeDtypeStruct((width, hidden), half),
            jax.ShapeDtypeStruct((HALO, width), half),
        ),
        in_specs=[hbm, VMEM_SPEC, VMEM_SPEC, hbm, hbm, hbm],
        out_specs=(hbm,) * 4,
        scratch_shapes=[
            pltpu.VMEM((width, rows), half),
            pltpu.VMEM((2, rows, GRAD_TILE), half),
            pltpu.VMEM((2, width, GRAD_TILE), half),
            dma((count - 1,)),
            dma((count - 1,)),
            dma,
            dma((2,)),
            dma((2,)),
            dma,
            dma,
        ],
        compiler_params=pltpu.CompilerParams(vmem_limit_bytes=60 * 2**20, collective_id=6, has_side_effects=True),
        cost_estimate=pl.CostEstimate(flops=4 * rows * width * hidden, bytes_accessed=40 * 10**6, transcendentals=0),
        name="swap_with_grads",
    )(value, cot, normed, act, g_up, zero)


def block_specs(shapes):
    return [pl.BlockSpec(shape, lambda j, n=len(shape): (0,) * n, pipeline_mode=pl.Buffered(1)) for shape in shapes]


def normalized(values):
    center = jnp.mean(values, axis=-1, keepdims=True)
    centred = values - center
    scale = lax.rsqrt(jnp.mean(centred * centred, axis=-1, keepdims=True) + norm_eps)
    return centred * scale, scale


def norm_back(grad, gain, scaled, scale):
    inner = grad * gain
    mean_inner = jnp.mean(inner, axis=-1, keepdims=True)
    mean_scaled = jnp.mean(inner * scaled, axis=-1, keepdims=True)
    return scale * (inner - mean_inner - scaled * mean_scaled)


def dot_cols(left, right):
    return lax.dot_general(left, right, (((1,), (1,)), ((), ())), preferred_element_type=jnp.float32)


LANES = 128
HALO = 8


def project_kernel(tok, before, prev, gain, w_v, w_one, w_zero, t_v, t_one, t_zero,
                   conv_in, factors, zero_out, projs, normed_out, normed, held):
    rows = tok.shape[0]
    keep = prev[0].astype(jnp.float32)

    @pl.when(pl.program_id(0) == 0)
    def _():
        scaled, _ = normalized(before[...].astype(jnp.float32))
        normed[:HALO] = (scaled * gain[...]).astype(jnp.bfloat16)
        for start in range(0, rows, PIECE):
            at = slice(start, start + PIECE)
            scaled, _ = normalized(tok[at].astype(jnp.float32))
            value = (scaled * gain[...]).astype(jnp.bfloat16)
            normed[start + HALO : start + PIECE + HALO] = value
            normed_out[at] = value

    shorts = []
    for i, (w, taps) in enumerate(((w_v, t_v), (w_one, t_one), (w_zero, t_zero))):
        proj = dot32(normed[...], w[...]).astype(jnp.bfloat16)
        projs[i] = proj
        held[...] = proj.astype(jnp.float32)
        held[:HALO] = held[:HALO] * keep
        shorts.append(
            taps[0:1] * held[HALO : HALO + rows]
            + taps[1:2] * held[HALO - 1 : HALO - 1 + rows]
            + taps[2:3] * held[HALO - 2 : HALO - 2 + rows]
        )
    factors[0] = shorts[1]
    factors[1] = shorts[0]
    zero_out[...] = shorts[2]
    product = (shorts[0] * shorts[1]).astype(jnp.bfloat16)
    for i in range(conv_in.shape[0]):
        conv_in[i] = product[:, i * LANES : (i + 1) * LANES]


def project(tok, before, has_prev, gain, w_in, taps):
    rows, width = tok.shape
    size = 256
    steps = width // size
    col = lambda part: (lambda j: (0, part * steps + j))
    parts = [pl.BlockSpec((width, size), col(i)) for i in range(3)]
    tap_parts = [pl.BlockSpec((3, size), col(i)) for i in range(3)]
    wide = lambda n, dtype: jax.ShapeDtypeStruct((n, width), dtype)
    stack = lambda m, n: pl.BlockSpec((m, n, size), lambda j: (0, 0, j))
    return pl.pallas_call(
        project_kernel,
        grid=(steps,),
        out_shape=[jax.ShapeDtypeStruct((width // LANES, rows, LANES), jnp.bfloat16)]
        + [jax.ShapeDtypeStruct((2, rows, width), jnp.float32), wide(rows, jnp.float32)]
        + [jax.ShapeDtypeStruct((3, rows + HALO, width), jnp.bfloat16), wide(rows, jnp.bfloat16)],
        in_specs=block_specs([(rows, width), (HALO, width)]) + [SMEM_SPEC] + block_specs([(1, width)]) + parts + tap_parts,
        out_specs=[pl.BlockSpec((size // LANES, rows, LANES), lambda j: (j, 0, 0))]
        + [stack(2, rows), pl.BlockSpec((rows, size), lambda j: (0, j)), stack(3, rows + HALO)]
        + block_specs([(rows, width)]),
        scratch_shapes=[pltpu.VMEM((rows + HALO, width), jnp.bfloat16), pltpu.VMEM((rows + HALO, size), jnp.float32)],
        compiler_params=pltpu.CompilerParams(vmem_limit_bytes=60 * 2**20),
        cost_estimate=pl.CostEstimate(flops=6 * rows * width * width, bytes_accessed=20 * 10**6, transcendentals=0),
        name="project",
    )(tok, before, has_prev, gain, w_in, w_in, w_in, taps, taps, taps)


def mlp_kernel(conv, conv_in, zero, tok, cot, skip, gain, w_out, w_up, w_down,
               output, act_out, up_out, gated, normed, d_resid, branch_out, conv_grad, d_mixed, d_zero, d_gain, d_skip,
               resid, down, d_normed):
    rows, width = tok.shape
    groups = width // LANES
    step = pl.program_id(0)

    @pl.when(step == 0)
    def _():
        for g in range(groups):
            at = slice(g * LANES, (g + 1) * LANES)
            mixed = conv[g].astype(jnp.float32) + skip[:, at] * conv_in[g].astype(jnp.float32)
            gated[:, at] = (zero[:, at] * mixed).astype(jnp.bfloat16)
        resid[...] = tok[...].astype(jnp.float32) + dot_cols(gated[...], w_out[...])
        for start in range(0, rows, PIECE):
            at = slice(start, start + PIECE)
            scaled, _ = normalized(resid[at])
            normed[at] = (scaled * gain[...]).astype(jnp.bfloat16)

    up = dot32(normed[...], w_up[...])
    d_act = dot32(cot[...], w_down[...])
    root = math.sqrt(2.0 / math.pi)
    square = up * up
    bent = jnp.tanh(root * up * (1.0 + 0.044715 * square))
    act = (0.5 * up * (1.0 + bent)).astype(jnp.bfloat16)
    slope = 0.5 * (1.0 + bent) + (0.5 * root) * up * (1.0 - bent * bent) * (1.0 + (3.0 * 0.044715) * square)
    g_up = (slope * d_act).astype(jnp.bfloat16)
    act_out[...] = act
    up_out[...] = g_up
    down_part = dot_cols(act, w_down[...])
    normed_part = dot_cols(g_up, w_up[...])

    @pl.when(step == 0)
    def _():
        down[...] = down_part
        d_normed[...] = normed_part

    @pl.when(step > 0)
    def _():
        down[...] += down_part
        d_normed[...] += normed_part

    @pl.when(step == pl.num_programs(0) - 1)
    def _():
        gain_sum = jnp.zeros((1, width), jnp.float32)
        for start in range(0, rows, PIECE):
            at = slice(start, start + PIECE)
            output[at] = (resid[at] + down[at]).astype(jnp.bfloat16)
            scaled, scale = normalized(resid[at])
            grad = d_normed[at]
            gain_sum = gain_sum + jnp.sum(grad * scaled, axis=0, keepdims=True)
            total = cot[at].astype(jnp.float32) + norm_back(grad, gain[...], scaled, scale)
            d_resid[at] = total
            branch_out[at] = total.astype(jnp.bfloat16)
        d_gain[...] = gain_sum
        down[...] = dot32(branch_out[...], w_out[...])
        for g in range(groups):
            at = slice(g * LANES, (g + 1) * LANES)
            source = conv_in[g].astype(jnp.float32)
            mixed = conv[g].astype(jnp.float32) + skip[:, at] * source
            d_gated = down[:, at]
            d_zero[:, at] = (d_gated * mixed).astype(jnp.bfloat16)
            grad = d_gated * zero[:, at]
            d_mixed[g] = grad
            conv_grad[g] = grad.astype(jnp.bfloat16)
            d_skip[:, at] = jnp.sum(grad * source, axis=0, keepdims=True)


def mlp_block(conv, conv_in, zero, tok, cot, skip, gain, w_out, w_up, w_down):
    rows, width = tok.shape
    hidden = w_down.shape[1]
    size = 512
    steps = hidden // size
    groups = width // LANES
    flat = lambda dtype: jax.ShapeDtypeStruct((rows, width), dtype)
    cut = lambda dtype: jax.ShapeDtypeStruct((groups, rows, LANES), dtype)
    row = jax.ShapeDtypeStruct((1, width), jnp.float32)
    big = jax.ShapeDtypeStruct((rows, hidden), jnp.bfloat16)
    half, full = jnp.bfloat16, jnp.float32
    ends = [flat(half), flat(half), flat(full), flat(half), cut(half), cut(full), flat(half), row, row]
    tile = pl.BlockSpec((rows, size), lambda j: (0, j))
    one = block_specs([(rows, width)])
    return pl.pallas_call(
        mlp_kernel,
        grid=(steps,),
        out_shape=[flat(half), big, big] + ends,
        in_specs=block_specs([conv.shape, conv.shape, zero.shape, tok.shape, cot.shape, (1, width), (1, width), w_out.shape])
        + [pl.BlockSpec((width, size), index) for index in (lambda j: (0, j),) * 2],
        out_specs=one + [tile, tile] + block_specs([e.shape for e in ends]),
        scratch_shapes=[pltpu.VMEM((rows, width), full)] * 3,
        compiler_params=pltpu.CompilerParams(vmem_limit_bytes=60 * 2**20),
        cost_estimate=pl.CostEstimate(flops=8 * rows * width * hidden + 4 * rows * width * width, bytes_accessed=50 * 10**6, transcendentals=rows * hidden),
        name="mlp_block",
    )(conv, conv_in, zero, tok, cot, skip, gain, w_out, w_up, w_down)


def shifted_back(held, wide_proj, after, taps, proj, prev, nxt, d_taps):
    rows = held.shape[0] - HALO
    held[rows:] = after[...].astype(jnp.float32) * nxt[0].astype(jnp.float32)
    g_proj = (
        taps[0:1] * held[:rows] + taps[1:2] * held[1 : rows + 1] + taps[2:3] * held[2 : rows + 2]
    ).astype(jnp.bfloat16)
    wide_proj[...] = proj[...].astype(jnp.float32)
    wide_proj[:HALO] = wide_proj[:HALO] * prev[0].astype(jnp.float32)
    d_taps[...] = jnp.concatenate(
        [jnp.sum(held[:rows] * wide_proj[HALO - i : HALO - i + rows], axis=0, keepdims=True) for i in range(3)], axis=0
    )
    return g_proj


def back_early_kernel(d_zero, proj, after, prev, nxt, taps, w_in, normed, branch, gated,
                      d_mixer, d_taps, d_normed, normed_t, branch_t, held, wide_proj):
    rows = normed.shape[0]
    step = pl.program_id(0)
    per = pl.num_programs(0) // 2

    @pl.when(step == 0)
    def _():
        d_normed[...] = jnp.zeros_like(d_normed)
        normed_t[...] = normed[...].T
        branch_t[...] = branch[...].T

    @pl.when(step < per)
    def _():
        held[:rows] = d_zero[...].astype(jnp.float32)
        g_proj = shifted_back(held, wide_proj, after, taps, proj, prev, nxt, d_taps)
        d_normed[...] += dot_cols(g_proj, w_in[...])
        d_mixer[...] = dot32(normed_t[...], g_proj).astype(jnp.bfloat16)

    @pl.when(step >= per)
    def _():
        d_mixer[...] = dot32(branch_t[...], gated[...]).astype(jnp.bfloat16)


def project_back_early(d_zero, projs, after, has_prev, has_next, taps, w_in, normed, branch, gated):
    rows, width = normed.shape
    size = 512
    per = width // size
    half = jnp.bfloat16
    inner = lambda j: jnp.minimum(j, per - 1)
    third = lambda n: pl.BlockSpec((n, size), lambda j: (0, 2 * per + inner(j)))
    tile = lambda n: pl.BlockSpec((n, size), lambda j: (0, inner(j)))
    return pl.pallas_call(
        back_early_kernel,
        grid=(2 * per,),
        out_shape=[
            jax.ShapeDtypeStruct((width, 4 * width), half),
            jax.ShapeDtypeStruct((3, width), jnp.float32),
            jax.ShapeDtypeStruct((rows, width), jnp.float32),
        ],
        in_specs=[tile(rows), pl.BlockSpec((None, rows + HALO, size), lambda j: (2, 0, inner(j))), tile(HALO)]
        + [SMEM_SPEC, SMEM_SPEC, third(3), third(width)]
        + block_specs([(rows, width)] * 2)
        + [pl.BlockSpec((rows, size), lambda j: (0, jnp.maximum(j - per, 0)))],
        out_specs=[pl.BlockSpec((width, size), lambda j: (0, 2 * per + j)), tile(3)] + block_specs([(rows, width)]),
        scratch_shapes=[
            pltpu.VMEM((width, rows), half),
            pltpu.VMEM((width, rows), half),
            pltpu.VMEM((rows + HALO, size), jnp.float32),
            pltpu.VMEM((rows + HALO, size), jnp.float32),
        ],
        compiler_params=pltpu.CompilerParams(vmem_limit_bytes=60 * 2**20),
        cost_estimate=pl.CostEstimate(flops=6 * rows * width * width, bytes_accessed=20 * 10**6, transcendentals=0),
        name="project_back_early",
    )(d_zero, projs, after, has_prev, has_next, taps, w_in, normed, branch, gated)


def back_late_kernel(begun, back, d_mixed, other, proj, after, prev, nxt, skip, taps, w_in, normed, tok, d_resid, gain, start,
                     d_mixer, d_taps, tokens_grad, d_gain, normed_t, d_normed, held, wide_proj):
    rows = tok.shape[0]
    step = pl.program_id(0)

    @pl.when(step == 0)
    def _():
        d_normed[...] = start[...]
        normed_t[...] = normed[...].T

    def spread(ref):
        return jnp.concatenate([ref[i].astype(jnp.float32) for i in range(ref.shape[0])], axis=1)

    d_conv_in = skip[...] * spread(d_mixed) + spread(back)
    held[:rows] = (d_conv_in * other[...]).astype(jnp.bfloat16).astype(jnp.float32)
    g_proj = shifted_back(held, wide_proj, after, taps, proj, prev, nxt, d_taps)
    d_normed[...] += dot_cols(g_proj, w_in[...])
    d_mixer[...] = dot32(normed_t[...], g_proj).astype(jnp.bfloat16)

    @pl.when(step == pl.num_programs(0) - 1)
    def _():
        gain_sum = jnp.zeros((1, tok.shape[1]), jnp.float32)
        for first in range(0, rows, PIECE):
            at = slice(first, first + PIECE)
            scaled, scale = normalized(tok[at].astype(jnp.float32))
            grad = d_normed[at]
            gain_sum = gain_sum + jnp.sum(grad * scaled, axis=0, keepdims=True)
            tokens_grad[at] = (d_resid[at] + norm_back(grad, gain[...], scaled, scale)).astype(jnp.bfloat16)
        d_gain[...] = gain_sum


def project_back_late(begun, back, d_mixed, factors, projs, after, has_prev, has_next, skip, taps, w_in, normed, tok, d_resid, gain, start):
    rows, width = tok.shape
    size = 512
    per = width // size
    half = jnp.bfloat16
    lane = lambda j: j // 2
    part = lambda j: lax.rem(j, 2)
    place = lambda j: part(j) * per + lane(j)
    group = pl.BlockSpec((size // LANES, rows, LANES), lambda j: (lane(j), 0, 0))
    third = lambda n: pl.BlockSpec((n, size), lambda j: (0, place(j)))
    return pl.pallas_call(
        back_late_kernel,
        grid=(2 * per,),
        out_shape=[
            jax.ShapeDtypeStruct(begun.shape, half),
            jax.ShapeDtypeStruct((3, 2 * width), jnp.float32),
            jax.ShapeDtypeStruct((rows, width), half),
            jax.ShapeDtypeStruct((1, width), jnp.float32),
        ],
        in_specs=[pl.BlockSpec(memory_space=pl.ANY), group, group]
        + [pl.BlockSpec((None, rows, size), lambda j: (part(j), 0, lane(j)))]
        + [pl.BlockSpec((None, rows + HALO, size), lambda j: (part(j), 0, lane(j)))]
        + [third(HALO), SMEM_SPEC, SMEM_SPEC, pl.BlockSpec((1, size), lambda j: (0, lane(j))), third(3), third(width)]
        + block_specs([(rows, width)] * 3 + [(1, width), (rows, width)]),
        out_specs=[pl.BlockSpec((width, size), lambda j: (0, place(j))), third(3)] + block_specs([(rows, width), (1, width)]),
        scratch_shapes=[
            pltpu.VMEM((width, rows), half),
            pltpu.VMEM((rows, width), jnp.float32),
            pltpu.VMEM((rows + HALO, size), jnp.float32),
            pltpu.VMEM((rows + HALO, size), jnp.float32),
        ],
        input_output_aliases={0: 0},
        compiler_params=pltpu.CompilerParams(vmem_limit_bytes=60 * 2**20),
        cost_estimate=pl.CostEstimate(flops=8 * rows * width * width, bytes_accessed=30 * 10**6, transcendentals=0),
        name="project_back_late",
    )(begun, back, d_mixed, factors, projs, after, has_prev, has_next, skip, taps, w_in, normed, tok, d_resid, gain, start)


def adam_update(master, moment, square, grad, factor, rate, decay):
    clipped = grad * factor
    moment_new = beta_one * moment + (1.0 - beta_one) * clipped
    square_new = beta_two * square + (1.0 - beta_two) * clipped * clipped
    moment_hat = moment_new / (1.0 - beta_one**ADAM_STEP)
    square_hat = square_new / (1.0 - beta_two**ADAM_STEP)
    master_new = master - rate * (moment_hat / (jnp.sqrt(square_hat) + adam_eps) + decay * master)
    return (master_new, moment_new, square_new)


def on_device(
    tokens,
    cotangent,
    seq_first,
    decay_code,
    mixer_master,
    mixer_moment,
    mixer_square,
    mlp_master,
    mlp_moment,
    mlp_square,
    channel_master,
    channel_moment,
    channel_square,
    filter_in_master,
    filter_in_moment,
    filter_in_square,
    filter_out_master,
    filter_out_moment,
    filter_out_square,
):
    block_rows = tokens.shape[1]
    model_width = tokens.shape[2]
    lane_count = 3 * model_width
    per = block_rows // PIECE
    seq_count = lax.axis_size("seq")
    long_blocks = max(seq_count // 4, 4)
    length = long_blocks * block_rows
    own_width = model_width // seq_count
    seq_index = lax.axis_index("seq")
    w_in, out_own, up_own, down_own, before, first_tiles = open_gather(
        mixer_master, mlp_master, tokens[0], seq_first, seq_count
    )
    firsts = first_tiles[:, 0, 0]
    w_down = lax.all_gather(down_own, "dp", axis=0, tiled=True)
    blocks = jnp.arange(seq_count, dtype=jnp.int32)
    same = firsts[None, :] == firsts[:, None]
    lasts = jnp.max(jnp.where(same, blocks[None, :], 0), axis=1).astype(jnp.int32)
    own_first = firsts[seq_index]
    has_prev = (seq_index - own_first >= 1).astype(jnp.int32).reshape(1)
    has_next = (lasts[seq_index] > seq_index).astype(jnp.int32).reshape(1)
    conv_taps = channel_master[:, :lane_count]
    gain_one = channel_master[0:1, lane_count:]
    gain_two = channel_master[1:2, lane_count:]
    skip_gain = channel_master[2:3, lane_count:]
    own_codes = lax.dynamic_slice_in_dim(decay_code, seq_index * own_width, own_width, 0)
    own_last = lax.dynamic_slice_in_dim(filter_out_master, seq_index * own_width, own_width, 1)
    conv_input, factors, x_zero, projs, normed_b = project(tokens[0], before, has_prev, gain_one, w_in, conv_taps)
    swapped, w_out, filt = swap_with_filter(
        channel_order(conv_input, seq_count), out_own, filter_in_master, own_last, own_codes, length
    )
    pieces = swapped.reshape(seq_count * per, PIECE, own_width)
    conv_out = conv_forward(firsts, pieces, filt, per)
    conv, w_up = swap_with_rows(conv_out.reshape(seq_count, block_rows, own_width), up_own, 5)
    conv = lane_order(conv)
    (
        output, act_b, grad_up_b, gated_b, normed_two_b, d_resid, grad_branch_b, conv_grad, d_mixed, d_x_zero, d_gain_two, d_skip,
    ) = mlp_block(conv, conv_input, x_zero, tokens[0], cotangent[0], skip_gain, gain_two, w_out, w_up, w_down)
    swapped_grad, up_grad_b, down_grad_b, after_zero = swap_with_grads(
        channel_order(conv_grad, seq_count), cotangent[0], normed_two_b, act_b, grad_up_b, d_x_zero
    )
    grad_pieces = swapped_grad.reshape(seq_count * per, PIECE, own_width)
    mixer_begun, d_taps_high, d_normed_begun = project_back_early(
        d_x_zero, projs, after_zero, has_prev, has_next, conv_taps, w_in, normed_b, grad_branch_b, gated_b
    )
    conv_in_grad, filt_grad = conv_backward(firsts, lasts, pieces, grad_pieces, filt, per)
    back = to_tokens(conv_in_grad.reshape(seq_count, block_rows, own_width))
    _, filter_pull = jax.vjp(
        lambda first, last: make_filter(first, last, own_codes, length), filter_in_master, own_last
    )
    first_grad, own_last_grad = filter_pull(filt_grad)
    back, mixer_begun, d_taps_high, d_normed_begun, first_grad, own_last_grad = lax.optimization_barrier(
        (back, mixer_begun, d_taps_high, d_normed_begun, first_grad, own_last_grad)
    )
    head_grad = skip_gain.reshape(-1, 1, LANES) * d_mixed[:, :HALO] + back[:, :HALO].astype(jnp.float32)
    head_grad = head_grad.transpose(1, 0, 2).reshape(HALO, model_width)
    head = [head_grad * factors[0, :HALO], head_grad * factors[1, :HALO]]
    after = passed_along(jnp.concatenate(head, axis=1).astype(jnp.bfloat16), "seq", -1)
    last_grad = lax.dynamic_update_slice_in_dim(
        jnp.zeros_like(filter_out_master), own_last_grad, seq_index * own_width, 1
    )
    mixer_grad_b, d_taps_low, tokens_grad, d_gain_one = project_back_late(
        mixer_begun, back, d_mixed, factors, projs, after, has_prev, has_next, skip_gain, conv_taps, w_in,
        normed_b, tokens[0], d_resid, gain_one, d_normed_begun,
    )
    d_taps = jnp.concatenate([d_taps_low, d_taps_high], axis=1)
    vectors = jnp.concatenate([d_gain_one, d_gain_two, d_skip], axis=0)
    channel_grad = jnp.concatenate([d_taps, vectors], axis=1)
    small_parts = (channel_grad, first_grad, last_grad)
    large_grads, small_sum, total = grad_sum(
        up_grad_b, down_grad_b, mixer_grad_b, jnp.concatenate([part.reshape(-1) for part in small_parts])
    )
    mlp_grad = large_grads[:2].astype(jnp.float32)
    mixer_grad = large_grads[2].astype(jnp.float32)
    ends = np.cumsum([part.size for part in small_parts])
    channel_grad, first_grad, last_grad = (
        small_sum[end - part.size : end].reshape(part.shape) for part, end in zip(small_parts, ends)
    )
    grad_norm = jnp.sqrt(total)
    factor = jnp.minimum(1.0, clip_limit / (grad_norm + 1e-06))
    mixer_new, mixer_moment_new, mixer_square_new = adam_update(
        mixer_master, mixer_moment, mixer_square, mixer_grad, factor, rate_matrix, weight_decay
    )
    mlp_new, mlp_moment_new, mlp_square_new = adam_update(
        mlp_master, mlp_moment, mlp_square, mlp_grad, factor, rate_matrix, weight_decay
    )
    channel_new, channel_moment_new, channel_square_new = adam_update(
        channel_master, channel_moment, channel_square, channel_grad, factor, rate_small, 0.0
    )
    filter_in_new, filter_in_moment_new, filter_in_square_new = adam_update(
        filter_in_master,
        filter_in_moment,
        filter_in_square,
        first_grad,
        factor,
        rate_small,
        weight_decay,
    )
    filter_out_new, filter_out_moment_new, filter_out_square_new = adam_update(
        filter_out_master,
        filter_out_moment,
        filter_out_square,
        last_grad,
        factor,
        rate_small,
        weight_decay,
    )
    return (
        output[None],
        tokens_grad[None],
        grad_norm.reshape(1),
        channel_grad,
        first_grad,
        last_grad,
        mixer_new,
        mixer_moment_new,
        mixer_square_new,
        mlp_new,
        mlp_moment_new,
        mlp_square_new,
        channel_new,
        channel_moment_new,
        channel_square_new,
        filter_in_new,
        filter_in_moment_new,
        filter_in_square_new,
        filter_out_new,
        filter_out_moment_new,
        filter_out_square_new,
    )


def solution(mesh):
    in_specs = (
        P("dp", "seq", None),
        P("dp", "seq", None),
        P("dp", "seq"),
        P(),
        P("dp", None),
        P("dp", None),
        P("dp", None),
        P(None, "dp", None),
        P(None, "dp", None),
        P(None, "dp", None),
        P(),
        P(),
        P(),
        P(),
        P(),
        P(),
        P(),
        P(),
        P(),
    )
    out_specs = (
        P("dp", "seq", None),
        P("dp", "seq", None),
        P(),
        P(),
        P(),
        P(),
        P("dp", None),
        P("dp", None),
        P("dp", None),
        P(None, "dp", None),
        P(None, "dp", None),
        P(None, "dp", None),
        P(),
        P(),
        P(),
        P(),
        P(),
        P(),
        P(),
        P(),
        P(),
    )
    return jax.shard_map(
        on_device, mesh=mesh, in_specs=in_specs, out_specs=out_specs, check_vma=False
    )
```

```python
import functools
import math

import jax
import jax.numpy as jnp
import numpy as np
from jax import lax
from jax.experimental import pallas as pl
from jax.experimental.pallas import tpu as pltpu
from jax.sharding import PartitionSpec as P

ADAM_STEP = 10


highest = lax.Precision.HIGHEST
norm_eps = 1e-05
clip_limit = 1.0
beta_one = 0.9
beta_two = 0.999
adam_eps = 1e-08
rate_matrix = 0.03
rate_small = 0.2
weight_decay = 0.1
PIECE = 128


def passed_along(value, axis, steps):
    count = lax.axis_size(axis)
    first, last = (max(0, -steps), min(count, count - steps))
    return lax.ppermute(value, axis, [(source, source + steps) for source in range(first, last)])


def filter_features(length, feature_count):
    places = jnp.arange(length, dtype=jnp.float32)[:, None]
    bands = jnp.arange(1, (feature_count - 1) // 2 + 1, dtype=jnp.float32)[None, :]
    angles = 2.0 * math.pi / length * places * bands
    return jnp.concatenate([places / length, jnp.cos(angles), jnp.sin(angles)], axis=1)


def make_filter(first_weight, last_weight, decay_code, length):
    features = filter_features(length, first_weight.shape[0])
    hidden = jnp.sin(jnp.dot(features, first_weight, precision=highest))
    raw_filter = jnp.dot(hidden, last_weight, precision=highest)
    rates = jnp.exp2(-decay_code.astype(jnp.float32))
    places = jnp.arange(length, dtype=jnp.float32)[:, None]
    shaped = raw_filter * jnp.exp(-places * rates[None, :])
    return shaped * lax.rsqrt(jnp.sum(shaped * shaped, axis=0, keepdims=True) + norm_eps)


def odd_tables(parts):
    freq = np.arange(PIECE)[:, None] * 2 + 1
    sample = np.arange(PIECE)[None, :]
    angles = (freq * sample % (4 * PIECE)) * (2.0 * math.pi / (4 * PIECE))
    pair = np.stack([np.cos(angles), -np.sin(angles)]).reshape(2, parts, PIECE // parts, PIECE)
    table = pair.transpose(1, 0, 2, 3).reshape(parts, 2 * PIECE // parts, PIECE).astype(np.float32)
    upper = table.astype(jnp.bfloat16)
    lower = (table - upper.astype(np.float32)).astype(jnp.bfloat16)
    swap = (0, 2, 1)
    forward = np.concatenate([upper, lower, upper], axis=2)
    backward = np.concatenate([upper.transpose(swap), lower.transpose(swap)], axis=1)
    return jnp.asarray(forward), jnp.asarray(backward)


def dot32(left, right):
    return jnp.dot(left, right, preferred_element_type=jnp.float32)


def split_two(value):
    upper = value.astype(jnp.bfloat16)
    return upper, (value - upper.astype(jnp.float32)).astype(jnp.bfloat16)


def freq_signs(rows, width):
    places = lax.broadcasted_iota(jnp.int32, (rows, width), 0)
    return 1.0 - 2.0 * (places % 2).astype(jnp.float32)


def side_by_side(ref, p, count):
    return jnp.concatenate([ref[p + i] for i in range(count)], axis=1)


def in_groups(count, body):
    size = 8

    def one(i, carry):
        for j in range(0, size, 2):
            body(i * size + j)
        return carry

    lax.fori_loop(0, count // size, one, 0)


def to_freq(table, ref, out, count, factor):
    lanes = ref.shape[2]

    def body(p):
        data = side_by_side(ref, p, 2)
        spec = dot32(table[:, : 2 * PIECE], jnp.concatenate([data, data], axis=0))
        if factor != 1.0:
            spec = spec * factor
        out[p] = spec[:, :lanes]
        out[p + 1] = spec[:, lanes:]

    in_groups(count, body)


def filter_spectrum(filt_ref, table, h_ref):
    half = table.shape[0] // 2
    lanes = filt_ref.shape[1]
    signs = freq_signs(half, lanes)
    prev = None
    for k in range(0, filt_ref.shape[0] // PIECE, 2):
        data = jnp.concatenate([filt_ref[i * PIECE : (i + 1) * PIECE, :] for i in (k, k + 1)], axis=1)
        upper, lower = split_two(data)
        both = dot32(table, jnp.concatenate([upper, upper, lower], axis=0))
        for i in range(2):
            spec = both[:, i * lanes : (i + 1) * lanes]
            if prev is None:
                h_ref[0] = spec
            else:
                h_ref[k + i, :half] = spec[:half] - signs * prev[half:]
                h_ref[k + i, half:] = spec[half:] + signs * prev[:half]
            prev = spec


def to_time(table, ref, count, factor, store):
    lanes = ref.shape[2]

    def body(p):
        value = dot32(table[:PIECE], side_by_side(ref, p, 2).astype(jnp.bfloat16))
        if factor != 1.0:
            value = value * factor
        store(p, value[:, :lanes])
        store(p + 1, value[:, lanes:])

    in_groups(count, body)


def emitter(part, parts, out_ref, acc_ref):
    def store(p, value):
        if parts == 1:
            out_ref[p] = value.astype(out_ref.dtype)
            return
        total = value if part == 0 else acc_ref[p] + value
        if part == parts - 1:
            out_ref[p] = total.astype(out_ref.dtype)
        else:
            acc_ref[p] = total

    return store


def conv_forward_kernel(per, first_ref, x_ref, filt_ref, f_ref, i_ref, o_ref, xs, hs, *rest):
    count, _, lanes = x_ref.shape
    blocks = count // per
    parts = f_ref.shape[0]
    half = PIECE // parts
    tiles = half // 8
    for part in range(parts):
        filter_spectrum(filt_ref, f_ref[part], hs)
        to_freq(f_ref[part], x_ref, xs, count, 1.0)

        def one_tile(step, carry):
            b = blocks - 1 - step // tiles
            row = pl.multiple_of((step % tiles) * 8, 8)
            re = pl.ds(row, 8)
            im = pl.ds(row + half, 8)

            def add_pairs(acc, a, lag, diagonal):
                acc = list(acc)
                for j in range(per):
                    sr, si = xs[a * per + j, re], xs[a * per + j, im]
                    for i in range(j if diagonal else 0, per):
                        hr, hi = hs[lag + i - j, re], hs[lag + i - j, im]
                        acc[2 * i] = acc[2 * i] + (sr * hr - si * hi)
                        acc[2 * i + 1] = acc[2 * i + 1] + (sr * hi + si * hr)
                return tuple(acc)

            acc = tuple(jnp.zeros((8, lanes), jnp.float32) for _ in range(2 * per))
            acc = add_pairs(acc, b, 0, True)
            acc = lax.fori_loop(first_ref[b], b, lambda a, c: add_pairs(c, a, (b - a) * per, False), acc)
            for i in range(per):
                xs[b * per + i, re] = acc[2 * i]
                xs[b * per + i, im] = acc[2 * i + 1]
            return carry

        lax.fori_loop(0, blocks * tiles, one_tile, 0)
        to_time(i_ref[part], xs, count, 1.0 / PIECE, emitter(part, parts, o_ref, rest[0] if rest else None))


def conv_backward_kernel(
    per, first_ref, last_ref, x_ref, g_ref, filt_ref, f_ref, i_ref, dx_ref, df_ref, xs, gs, hs, dh, *rest
):
    count, _, lanes = x_ref.shape
    blocks = count // per
    taps = filt_ref.shape[0] // PIECE
    parts = f_ref.shape[0]
    half = PIECE // parts
    tiles = half // 8
    for part in range(parts):
        filter_spectrum(filt_ref, f_ref[part], hs)
        to_freq(f_ref[part], x_ref, xs, count, 1.0)
        to_freq(f_ref[part], g_ref, gs, count, 1.0 / PIECE)
        dh[...] = jnp.zeros_like(dh)

        def one_tile(step, carry):
            a = step // tiles
            row = pl.multiple_of((step % tiles) * 8, 8)
            re = pl.ds(row, 8)
            im = pl.ds(row + half, 8)

            def add_pairs(acc, b, lag, diagonal):
                acc = list(acc)
                for delta in range(0 if diagonal else 1 - per, per):
                    hr, hi = hs[lag + delta, re], hs[lag + delta, im]
                    tr, ti = dh[lag + delta, re], dh[lag + delta, im]
                    for j in range(max(0, -delta), per - max(0, delta)):
                        sr, si = xs[a * per + j, re], xs[a * per + j, im]
                        gr, gi = gs[b * per + j + delta, re], gs[b * per + j + delta, im]
                        acc[2 * j] = acc[2 * j] + (hr * gr + hi * gi)
                        acc[2 * j + 1] = acc[2 * j + 1] + (hr * gi - hi * gr)
                        tr = tr + (sr * gr + si * gi)
                        ti = ti + (sr * gi - si * gr)
                    dh[lag + delta, re] = tr
                    dh[lag + delta, im] = ti
                return tuple(acc)

            acc = tuple(jnp.zeros((8, lanes), jnp.float32) for _ in range(2 * per))
            acc = add_pairs(acc, a, 0, True)
            acc = lax.fori_loop(a + 1, last_ref[a] + 1, lambda b, c: add_pairs(c, b, (b - a) * per, False), acc)
            for j in range(per):
                xs[a * per + j, re] = acc[2 * j]
                xs[a * per + j, im] = acc[2 * j + 1]
            return carry

        lax.fori_loop(0, blocks * tiles, one_tile, 0)
        to_time(i_ref[part], xs, count, 1.0, emitter(part, parts, dx_ref, rest[0] if rest else None))
        signs = freq_signs(half, lanes)
        back_u, back_l = i_ref[part, :PIECE], i_ref[part, PIECE:]
        for k in range(taps):
            grad = dh[k]
            if k + 1 < taps:
                grad = grad + jnp.concatenate([signs * dh[k + 1, half:], -signs * dh[k + 1, :half]], axis=0)
            upper, lower = split_two(grad)
            value = dot32(back_u, upper) + (dot32(back_l, upper) + dot32(back_u, lower))
            rows = slice(k * PIECE, (k + 1) * PIECE)
            df_ref[rows, :] = value if part == 0 else df_ref[rows, :] + value


VMEM_SPEC = pl.BlockSpec(memory_space=pltpu.VMEM)
SMEM_SPEC = pl.BlockSpec(memory_space=pltpu.SMEM)


def conv_parts(count):
    return 1 if count <= 64 else 4


def conv_forward(firsts, pieces, filt, per):
    count, _, lanes = pieces.shape
    taps = filt.shape[0] // PIECE
    parts = conv_parts(count)
    spec = (2 * PIECE // parts, lanes)
    scratch = [pltpu.VMEM((count,) + spec, jnp.float32), pltpu.VMEM((taps,) + spec, jnp.float32)]
    if parts > 1:
        scratch.append(pltpu.VMEM(pieces.shape, jnp.float32))
    return pl.pallas_call(
        functools.partial(conv_forward_kernel, per),
        out_shape=jax.ShapeDtypeStruct(pieces.shape, jnp.bfloat16),
        in_specs=[SMEM_SPEC] + [VMEM_SPEC] * 4,
        out_specs=VMEM_SPEC,
        scratch_shapes=scratch,
        compiler_params=pltpu.CompilerParams(vmem_limit_bytes=60 * 2**20),
        cost_estimate=pl.CostEstimate(flops=2 * 10**9, bytes_accessed=8 * 10**6, transcendentals=0),
        name="long_conv",
    )(firsts, pieces, filt, *odd_tables(parts))


def conv_backward(firsts, lasts, pieces, grads, filt, per):
    count, _, lanes = pieces.shape
    taps = filt.shape[0] // PIECE
    parts = conv_parts(count)
    spec = (2 * PIECE // parts, lanes)
    scratch = [pltpu.VMEM((n,) + spec, jnp.float32) for n in (count, count, taps, taps)]
    if parts > 1:
        scratch.append(pltpu.VMEM(pieces.shape, jnp.float32))
    return pl.pallas_call(
        functools.partial(conv_backward_kernel, per),
        out_shape=(
            jax.ShapeDtypeStruct(pieces.shape, jnp.bfloat16),
            jax.ShapeDtypeStruct(filt.shape, jnp.float32),
        ),
        in_specs=[SMEM_SPEC] * 2 + [VMEM_SPEC] * 5,
        out_specs=(VMEM_SPEC, VMEM_SPEC),
        scratch_shapes=scratch,
        compiler_params=pltpu.CompilerParams(vmem_limit_bytes=60 * 2**20),
        cost_estimate=pl.CostEstimate(flops=4 * 10**9, bytes_accessed=10**7, transcendentals=0),
        name="long_conv_back",
    )(firsts, lasts, pieces, grads, filt, *odd_tables(parts))


def channel_order(value, count):
    groups, rows, lanes = value.shape
    if groups != count:
        own = groups * lanes // count
        value = value.reshape(groups, rows, lanes // own, own).transpose(0, 2, 1, 3).reshape(count, rows, own)
    return value


def lane_order(value):
    _, rows, own = value.shape
    if own != LANES:
        value = value.reshape(-1, LANES // own, rows, own).transpose(0, 2, 1, 3).reshape(-1, rows, LANES)
    return value


def to_tokens(value):
    return lane_order(lax.all_to_all(value, "seq", 0, 0, tiled=True))


MESH_ID = pl.DeviceIdType.MESH
def remote(src, dst, send, recv, device):
    return pltpu.make_async_remote_copy(src, dst, send, recv, device_id=device, device_id_type=MESH_ID)


def greet(partners):
    barrier = pltpu.get_barrier_semaphore()
    for partner in partners:
        pl.semaphore_signal(barrier, inc=1, device_id=partner, device_id_type=MESH_ID)
    pl.semaphore_wait(barrier, len(partners))


def place_of(sizes):
    ny, nx, nz = sizes
    dp, seq = lax.axis_index("dp"), lax.axis_index("seq")
    y, c = dp // 2, dp % 2
    z, x = seq // nx, seq % nx

    def at_y(step):
        other = lax.rem(y + step, ny)
        return other, (other * 2 + c, seq)

    def at_x(step):
        other = lax.rem(x + step, nx)
        return other, (dp, z * nx + other)

    def at_z(step):
        other = lax.rem(z + step, nz)
        return other, (dp, other * nx + x)

    return (y, c, z, x), (y * 2 + 1 - c, seq), at_y, at_x, at_z


def axis_sizes():
    seq = lax.axis_size("seq")
    return lax.axis_size("dp") // 2, seq // 4, 4


def wide(ref):
    return ref[...].astype(jnp.float32)


def staged_sum(sizes, grads, out, sq, scratch):
    own, r0, r1, r2, r3, load_sem, s0, t0, s1, t1, s2, t2, s3, t3, s4, t4, s5, t5 = scratch
    ny, nx, nz = sizes
    strip = r0.shape[2]
    strips = out.shape[1] // strip
    width = out.shape[2]
    half, quarter = width // nx, width // nx // nz
    total = len(grads) * strips
    (y, c, z, x), sibling, at_y, at_x, at_z = place_of(sizes)

    def rows_of(k):
        return pl.ds(pl.multiple_of(lax.rem(k, strips) * strip, strip), strip)

    def cols(start, size):
        return pl.ds(pl.multiple_of(start * size, size), size)

    def core_copy(k, g):
        return remote(g.at[:, 1 - c, rows_of(k)], r0.at[k], s0.at[k], t0.at[k], sibling)

    def own_copy(k, g):
        slot = lax.rem(k, 4)
        return pltpu.make_async_copy(g.at[:, c, rows_of(k)], own.at[slot], load_sem.at[slot])

    def start_first(k):
        for i, g in enumerate(grads):

            @pl.when(k // strips == i)
            def _():
                core_copy(k, g).start()
                own_copy(k, g).start()

    def y_copy(k, i):
        other, device = at_y(i)
        return remote(r0.at[k, other], r1.at[k, ny - 1 - i], s1.at[k, i - 1], t1.at[k, ny - 1 - i], device)

    def x_copy(k, i):
        other, device = at_x(i)
        return remote(r1.at[k, 0, :, cols(other, half)], r2.at[k, nx - 1 - i], s2.at[k, i - 1], t2.at[k, nx - 1 - i], device)

    def z_copy(k, i):
        other, device = at_z(i)
        return remote(r2.at[k, 0, :, cols(other, quarter)], r3.at[k, nz - 1 - i], s3.at[k, i - 1], t3.at[k, nz - 1 - i], device)

    def z_back(k, i):
        other, device = at_z(i)
        part = out.at[k // strips, rows_of(k), cols(x * nz + z, quarter)]
        return remote(part, part, s4.at[k, i - 1], t4.at[k, nz - 1 - i], device)

    def x_back(k, i):
        other, device = at_x(i)
        part = out.at[k // strips, rows_of(k), cols(x, half)]
        return remote(part, part, s5.at[k, i - 1], t5.at[k, nx - 1 - i], device)

    def tiles(size, body):
        piece = min(size, TILE // strip)

        def one(i, carry):
            body(pl.ds(pl.multiple_of(i * piece, piece), piece))
            return carry

        lax.fori_loop(0, size // piece, one, 0)

    def begin():
        start_first(jnp.int32(0))
        start_first(jnp.int32(1))

    def step(t):
        @pl.when(t + 2 < total)
        def _():
            start_first(t + 2)

        @pl.when(t < total)
        def _():
            k, slot = t, lax.rem(t, 4)
            core_copy(k, grads[0]).wait_recv()
            own_copy(k, grads[0]).wait()
            for other in range(ny):

                def add(at):
                    r0[k, other, :, at] = (wide(r0.at[k, other, :, at]) + wide(own.at[slot, other, :, at])).astype(r0.dtype)

                tiles(width, add)
            for i in range(1, ny):
                y_copy(k, i).start()

        @pl.when((t >= OFFSETS[0]) & (t < total + OFFSETS[0]))
        def _():
            k = t - OFFSETS[0]
            for i in range(1, ny):
                y_copy(k, i).wait_recv()

            def add(at):
                value = wide(r0.at[k, y, :, at])
                for i in range(ny - 1):
                    value = value + wide(r1.at[k, i, :, at])
                r1[k, 0, :, at] = value.astype(r1.dtype)

            tiles(width, add)
            for i in range(1, nx):
                x_copy(k, i).start()

        @pl.when((t >= OFFSETS[1]) & (t < total + OFFSETS[1]))
        def _():
            k = t - OFFSETS[1]
            for i in range(1, nx):
                x_copy(k, i).wait_recv()

            def add(at):
                mine = pl.ds(pl.multiple_of(x * half + at.start, 128), at.size)
                value = wide(r1.at[k, 0, :, mine])
                for i in range(nx - 1):
                    value = value + wide(r2.at[k, i, :, at])
                r2[k, 0, :, at] = value.astype(r2.dtype)

            tiles(half, add)
            for i in range(1, nz):
                z_copy(k, i).start()

        @pl.when((t >= OFFSETS[2]) & (t < total + OFFSETS[2]))
        def _():
            k = t - OFFSETS[2]
            for i in range(1, nz):
                z_copy(k, i).wait_recv()
            value = wide(r2.at[k, 0, :, cols(z, quarter)])
            for i in range(nz - 1):
                value = value + wide(r3.at[k, i])
            sq[...] += value * value
            out[k // strips, rows_of(k), cols(x * nz + z, quarter)] = value.astype(out.dtype)
            for i in range(1, nz):
                z_back(k, i).start()

        @pl.when((t >= OFFSETS[3]) & (t < total + OFFSETS[3]))
        def _():
            k = t - OFFSETS[3]
            for i in range(1, nz):
                z_back(k, i).wait_recv()
            for i in range(1, nx):
                x_back(k, i).start()

    def retire(k):
        for i in range(1, nx):
            x_back(k, i).wait()
            x_copy(k, i).wait_send()
        for i in range(1, nz):
            z_copy(k, i).wait_send()
            z_back(k, i).wait_send()
        for i in range(1, ny):
            y_copy(k, i).wait_send()
        core_copy(k, grads[0]).wait_send()

    def finish(first):
        def one(k, carry):
            retire(k)
            return carry

        lax.fori_loop(first, total, one, 0)

    return begin, step, retire, finish, total + OFFSETS[3]


def staged_scratch(sizes, count, rows, strip, width):
    ny, nx, nz = sizes
    total = count * rows // strip
    half = jnp.bfloat16
    dma = pltpu.SemaphoreType.DMA
    pairs = [(total,), (total, ny - 1), (total, nx - 1), (total, nz - 1), (total, nz - 1), (total, nx - 1)]
    return [
        pltpu.VMEM((4, ny, strip, width), half),
        pltpu.VMEM((total, ny, strip, width), half),
        pltpu.VMEM((total, ny - 1, strip, width), half),
        pltpu.VMEM((total, nx - 1, strip, width // nx), half),
        pltpu.VMEM((total, nz - 1, strip, width // nx // nz), half),
        dma((4,)),
    ] + [dma(p) for p in pairs for _ in range(2)]


STAGED = 18
TILE = 65536
OFFSETS = (1, 2, 3, 4)
BEHIND = 8


def grad_sum_kernel(sizes, g0, g1, g2, small, out, small_out, norm, *scratch):
    staged, (b0, b1, b2, b3, sq, norms, small_send, small_recv, norm_send, norm_recv) = scratch[:STAGED], scratch[STAGED:]
    ny, nx, nz = sizes
    (y, c, z, x), sibling, at_y, at_x, at_z = place_of(sizes)
    partners = [sibling] + [at_y(i)[1] for i in range(1, ny)] + [at_x(i)[1] for i in range(1, nx)]
    greet(partners + [at_z(i)[1] for i in range(1, nz)])
    axes = ((2, c, None), (ny, y, at_y), (nx, x, at_x), (nz, z, at_z))
    base = (0, 1, ny, ny + nx - 1, ny + nx + nz - 2)

    def small_copies(stage):
        def numbered(first, pairs):
            return [
                remote(src, dst, small_send.at[first + i], small_recv.at[first + back], device)
                for i, back, src, dst, device in pairs
            ]

        def spread(axis, pick):
            count, _, at = axes[axis]
            return [(i - 1, count - 1 - i) + pick(i, *at(i)) for i in range(1, count)]

        if stage == 0:
            return numbered(0, [(0, 0, small.at[:, 1 - c], b0, sibling)])
        if stage == 1:
            return numbered(base[1], spread(1, lambda i, o, d: (b0.at[o], b1.at[ny - 1 - i], d)))
        if stage == 2:
            return numbered(base[2], spread(2, lambda i, o, d: (b1.at[0, o], b2.at[nx - 1 - i], d)))
        if stage == 3:
            return numbered(base[3], spread(3, lambda i, o, d: (b2.at[0, o], b3.at[nz - 1 - i], d)))
        again = base[4]
        if stage == 4:
            part = small_out.at[y, c, x, z]
            return numbered(again + base[3], spread(3, lambda i, o, d: (part, part, d)))
        if stage == 5:
            part = small_out.at[y, c, x]
            return numbered(again + base[2], spread(2, lambda i, o, d: (part, part, d)))
        if stage == 6:
            part = small_out.at[y, c]
            return numbered(again + base[1], spread(1, lambda i, o, d: (part, part, d)))
        part = small_out.at[:, c]
        return numbered(again, [(0, 0, part, part, sibling)])

    def small_step(stage):
        if stage > 0:
            for copy in small_copies(stage - 1):
                copy.wait_recv()
        if stage == 1:
            b0[...] += small[:, c]
        if stage == 2:
            value = b0[y]
            for i in range(ny - 1):
                value = value + b1[i]
            b1[0] = value
        if stage == 3:
            value = b1[0, x]
            for i in range(nx - 1):
                value = value + b2[i]
            b2[0] = value
        if stage == 4:
            value = b2[0, z]
            for i in range(nz - 1):
                value = value + b3[i]
            small_out[y, c, x, z] = value
            for row in range(0, value.shape[0], 8):
                sq[:8, :128] += value[row : row + 8] * value[row : row + 8]
        if stage < 8:
            for copy in small_copies(stage):
                copy.start()

    def norm_copies(stage):
        count, place, at = axes[stage]
        devices = [sibling] if at is None else [at(i)[1] for i in range(1, count)]
        return [
            remote(norms.at[stage, place], norms.at[stage, place], norm_send.at[stage, i], norm_recv.at[stage, len(devices) - 1 - i], device)
            for i, device in enumerate(devices)
        ]

    begin, step, retire, finish, steps = staged_sum(sizes, (g0, g1, g2), out, sq, staged)
    sq[...] = jnp.zeros_like(sq)
    begin()

    def one_step(t, carry):
        step(t)
        for stage in range(9):

            @pl.when(t == stage)
            def _():
                small_step(stage)

        @pl.when(t >= BEHIND)
        def _():
            retire(t - BEHIND)

        return carry

    lax.fori_loop(0, steps - 1, one_step, 0)
    tile = jnp.zeros((8, 128), jnp.float32)
    for row in range(0, sq.shape[0], 8):
        for col in range(0, sq.shape[1], 128):
            tile = tile + sq[row : row + 8, col : col + 128]
    for stage in range(4):
        count, place, _ = axes[stage]
        norms[stage, place] = tile
        for copy in norm_copies(stage):
            copy.start()
        if stage == 1:
            step(jnp.int32(steps - 1))
        for copy in norm_copies(stage):
            copy.wait_recv()
        tile = norms[stage, 0]
        for i in range(1, count):
            tile = tile + norms[stage, i]
    norm[...] = tile
    for stage in range(4):
        for copy in norm_copies(stage):
            copy.wait_send()
    for stage in range(8):
        for copy in small_copies(stage):
            copy.wait_send()
    finish(steps - 1 - BEHIND)


def grad_sum(up, down, mixer, small):
    sizes = ny, nx, nz = axis_sizes()
    rows_all, width = mixer.shape
    seq = nx * nz
    rows = rows_all // (2 * ny)
    strip = 32
    full = jnp.float32
    dma = pltpu.SemaphoreType.DMA
    parts = 2 * ny * seq
    piece = -(-small.shape[0] // (parts * 1024)) * 8
    small = jnp.pad(small, (0, parts * piece * 128 - small.shape[0])).reshape(ny, 2, nx, nz, piece, 128)
    most = max(2, ny, nx, nz)
    smalls = 2 * (ny + nx + nz - 2)
    large, summed, norm = pl.pallas_call(
        functools.partial(grad_sum_kernel, sizes),
        out_shape=(
            jax.ShapeDtypeStruct((3, rows, width), jnp.bfloat16),
            jax.ShapeDtypeStruct(small.shape, full),
            jax.ShapeDtypeStruct((8, 128), full),
        ),
        in_specs=[pl.BlockSpec(memory_space=pltpu.HBM)] * 3 + [VMEM_SPEC],
        out_specs=(VMEM_SPEC,) * 3,
        scratch_shapes=staged_scratch(sizes, 3, rows, strip, width)
        + [
            pltpu.VMEM((ny, nx, nz, piece, 128), full),
            pltpu.VMEM((ny - 1, nx, nz, piece, 128), full),
            pltpu.VMEM((nx - 1, nz, piece, 128), full),
            pltpu.VMEM((nz - 1, piece, 128), full),
            pltpu.VMEM((strip, width // seq), full),
            pltpu.VMEM((4, most, 8, 128), full),
            dma((smalls,)),
            dma((smalls,)),
            dma((4, most - 1)),
            dma((4, most - 1)),
        ],
        compiler_params=pltpu.CompilerParams(vmem_limit_bytes=35 * 2**20, collective_id=1, has_side_effects=True),
        cost_estimate=pl.CostEstimate(flops=10**8, bytes_accessed=20 * 10**6, transcendentals=0),
        name="grad_sum",
    )(*(g.reshape(ny, 2, rows, width) for g in (up, down, mixer)), small)
    return large, summed.reshape(-1), jnp.sum(norm)


def row_gather(sizes, own, full, width, pieces, sems, direct=0):
    a_send, a_recv, b_send, b_recv, c_send, c_recv, d_send, d_recv, e_send, e_recv = sems
    ny = sizes[0]
    rows = own.shape[0]
    half = width // 2
    size = half // pieces
    (y, c, _, _), sibling, at_y, _, _ = place_of(sizes)
    dp, seq = lax.axis_index("dp"), lax.axis_index("seq")
    side = lax.rem(seq, 2)
    pair = (dp, seq + 1 - 2 * side)

    def at_rows(d):
        return pl.ds(pl.multiple_of(d * rows, rows), rows)

    def at_cols(which, p):
        return pl.ds(pl.multiple_of(which * half + p * size, size), size)

    def core_copy():
        return remote(own, full.at[at_rows(dp)], a_send.at[0], a_recv.at[0], sibling)

    def y_copy(i, p):
        _, device = at_y(i)
        cols = at_cols(side, p)
        return remote(own.at[:, cols], full.at[at_rows(dp), cols], b_send.at[i - 1, p], b_recv.at[ny - 1 - i, p], device)

    def pass_on(i, p, which, send, recv, device):
        other, _ = at_y(ny - i)
        part = full.at[at_rows(other * 2 + c), at_cols(which, p)]
        return remote(part, part, send.at[ny - 1 - i, p], recv.at[ny - 1 - i, p], device)

    def x_copy(i, p):
        if p < pieces - direct:
            return pass_on(i, p, side, c_send, c_recv, pair)
        _, device = at_y(i)
        cols = at_cols(1 - side, p)
        return remote(own.at[:, cols], full.at[at_rows(dp), cols], c_send.at[i - 1, p], c_recv.at[ny - 1 - i, p], device)

    def first_copy(i, p):
        return pass_on(i, p, side, d_send, d_recv, sibling)

    def second_copy(i, p):
        return pass_on(i, p, 1 - side, e_send, e_recv, sibling)

    every = [(i, p) for p in range(pieces) for i in range(1, ny)]

    def start():
        for i, p in every:
            y_copy(i, p).start()
            if p >= pieces - direct:
                x_copy(i, p).start()
        core_copy().start()

    def first_half(p):
        for i in range(1, ny):
            y_copy(i, p).wait_recv()
            if p < pieces - direct:
                x_copy(i, p).start()
            first_copy(i, p).start()

    def second_half(p):
        for i in range(1, ny):
            x_copy(i, p).wait_recv()
            second_copy(i, p).start()

    def finish():
        core_copy().wait()
        for i, p in every:
            y_copy(i, p).wait_send()
            x_copy(i, p).wait_send()
            first_copy(i, p).wait()
            second_copy(i, p).wait()

    return start, first_half, second_half, finish


def gather_sems(sizes, pieces):
    dma = pltpu.SemaphoreType.DMA
    return [dma((1,))] * 2 + [dma((sizes[0] - 1, pieces))] * 8


GATHER = 10


def greet_near(sizes, count):
    _, sibling, at_y, _, _ = place_of(sizes)
    dp, me = lax.axis_index("dp"), lax.axis_index("seq")
    others = [(dp, lax.rem(me + i, count)) for i in range(1, count)]
    greet([sibling] + [at_y(i)[1] for i in range(1, sizes[0])] + others)
    return others


def open_kernel(sizes, count, pieces, mixer, mlp, tok, first, w_in, w_out, up_out, down_out, before, firsts,
                own, mlp_in, mlp_sem, halo_send, halo_recv, first_send, first_recv, *sems):
    rows = own.shape[0]
    lane_count = own.shape[1]
    me, dp = lax.axis_index("seq"), lax.axis_index("dp")
    chunk = mlp_in.shape[2]
    chunks = rows // chunk

    def load(k):
        return pltpu.make_async_copy(mlp.at[:, k * chunk : (k + 1) * chunk], mlp_in.at[k % 2], mlp_sem.at[k % 2])

    load(0).start()
    own[...] = mixer[:, :lane_count].astype(jnp.bfloat16)
    others = greet_near(sizes, count)
    start, first_half, second_half, finish = row_gather(sizes, own, w_in, lane_count, pieces, sems)
    start()
    halo = remote(tok.at[tok.shape[0] - HALO :], before, halo_send, halo_recv, others[0])
    halo.start()
    announced = [
        remote(first, firsts.at[me], first_send.at[i], first_recv.at[count - 2 - i], device) for i, device in enumerate(others)
    ]
    for copy in announced:
        copy.start()
    firsts[me] = first[...]
    w_in[pl.ds(pl.multiple_of(dp * rows, rows), rows), :] = own[...]
    w_out[...] = mixer[:, lane_count:].astype(jnp.bfloat16)
    for k in range(max(chunks, pieces)):
        if k < chunks:
            if k + 1 < chunks:
                load(k + 1).start()
            load(k).wait()
            at = slice(k * chunk, (k + 1) * chunk)
            up_out[at] = mlp_in[k % 2, 0].astype(jnp.bfloat16)
            down_out[at] = mlp_in[k % 2, 1].astype(jnp.bfloat16)
        if k < pieces:
            first_half(k)
        if 2 <= k < pieces:
            second_half(k - 2)
    for k in range(max(0, pieces - 2), pieces):
        second_half(k)
    halo.wait()
    for copy in announced:
        copy.wait()
    finish()


def open_gather(mixer, mlp, tok, first, count):
    sizes = axis_sizes()
    rows, total = mixer.shape
    width = tok.shape[1]
    lane_count = total - width
    dp = 2 * sizes[0]
    pieces = 6
    half = jnp.bfloat16
    dma = pltpu.SemaphoreType.DMA
    chunk = rows // 4
    first = jnp.broadcast_to(first.reshape(1, 1), (8, 128))
    return pl.pallas_call(
        functools.partial(open_kernel, sizes, count, pieces),
        out_shape=(
            jax.ShapeDtypeStruct((rows * dp, lane_count), half),
            jax.ShapeDtypeStruct((rows, width), half),
            jax.ShapeDtypeStruct(mlp.shape[1:], half),
            jax.ShapeDtypeStruct(mlp.shape[1:], half),
            jax.ShapeDtypeStruct((HALO, width), half),
            jax.ShapeDtypeStruct((count, 8, 128), jnp.int32),
        ),
        in_specs=[VMEM_SPEC, pl.BlockSpec(memory_space=pltpu.HBM), VMEM_SPEC, VMEM_SPEC],
        out_specs=(VMEM_SPEC,) * 6,
        scratch_shapes=[
            pltpu.VMEM((rows, lane_count), half),
            pltpu.VMEM((2, 2, chunk, mlp.shape[2]), jnp.float32),
            dma((2,)),
            dma,
            dma,
            dma((count - 1,)),
            dma((count - 1,)),
        ]
        + gather_sems(sizes, pieces),
        compiler_params=pltpu.CompilerParams(vmem_limit_bytes=60 * 2**20, collective_id=3, has_side_effects=True),
        cost_estimate=pl.CostEstimate(flops=10**6, bytes_accessed=60 * 10**6, transcendentals=0),
        name="open_gather",
    )(mixer, mlp, tok, first)


def swap_kernel(sizes, pieces, value, own, swapped, full, swap_send, swap_recv, self_sem, *sems):
    count = value.shape[0]
    rows = own.shape[0]
    me, dp = lax.axis_index("seq"), lax.axis_index("dp")
    others = greet_near(sizes, count)
    start, first_half, second_half, finish = row_gather(sizes, own, full, own.shape[1], pieces, sems, 1)
    start()
    copies = [
        remote(value.at[device[1]], swapped.at[me], swap_send.at[i], swap_recv.at[count - 2 - i], device)
        for i, device in enumerate(others)
    ]
    for copy in copies:
        copy.start()
    kept = [
        pltpu.make_async_copy(value.at[me], swapped.at[me], self_sem.at[0]),
        pltpu.make_async_copy(own, full.at[pl.ds(pl.multiple_of(dp * rows, rows), rows)], self_sem.at[1]),
    ]
    for copy in kept:
        copy.start()
    for p in range(pieces):
        first_half(p)
        if p > 0:
            second_half(p - 1)
    second_half(pieces - 1)
    for copy in kept + copies:
        copy.wait()
    finish()


def swap_with_rows(value, own, number):
    sizes = axis_sizes()
    count = value.shape[0]
    rows, width = own.shape
    pieces = 4
    dma = pltpu.SemaphoreType.DMA
    hbm = pl.BlockSpec(memory_space=pltpu.HBM)
    return pl.pallas_call(
        functools.partial(swap_kernel, sizes, pieces),
        out_shape=(
            jax.ShapeDtypeStruct(value.shape, value.dtype),
            jax.ShapeDtypeStruct((rows * 2 * sizes[0], width), own.dtype),
        ),
        in_specs=[hbm, VMEM_SPEC],
        out_specs=(hbm, hbm),
        scratch_shapes=[dma((count - 1,)), dma((count - 1,)), dma((2,))] + gather_sems(sizes, pieces),
        compiler_params=pltpu.CompilerParams(vmem_limit_bytes=60 * 2**20, collective_id=number, has_side_effects=True),
        cost_estimate=pl.CostEstimate(flops=10**6, bytes_accessed=40 * 10**6, transcendentals=0),
        name="swap_with_rows",
    )(value, own)


def swap_filter_kernel(sizes, pieces, value, own, features, first, last, codes, swapped, full, filt, swap_send, swap_recv, self_sem, *sems):
    count = value.shape[0]
    me, dp = lax.axis_index("seq"), lax.axis_index("dp")
    rows = own.shape[0]
    others = greet_near(sizes, count)
    start_rows, first_half, second_half, finish = row_gather(sizes, own, full, own.shape[1], pieces, sems)
    start_rows()
    copies = [
        remote(value.at[device[1]], swapped.at[me], swap_send.at[i], swap_recv.at[count - 2 - i], device)
        for i, device in enumerate(others)
    ]
    for copy in copies:
        copy.start()
    kept = [
        pltpu.make_async_copy(value.at[me], swapped.at[me], self_sem.at[0]),
        pltpu.make_async_copy(own, full.at[pl.ds(pl.multiple_of(dp * rows, rows), rows)], self_sem.at[1]),
    ]
    for copy in kept:
        copy.start()
    rates = jnp.exp2(-codes[...].astype(jnp.float32))
    total = jnp.zeros_like(rates)
    step = 2 * PIECE
    for start in range(0, filt.shape[0], step):
        hidden = jnp.sin(jnp.dot(features[start : start + step], first[...], precision=highest, preferred_element_type=jnp.float32))
        raw = jnp.dot(hidden, last[...], precision=highest, preferred_element_type=jnp.float32)
        places = (lax.broadcasted_iota(jnp.int32, raw.shape, 0) + start).astype(jnp.float32)
        shaped = raw * jnp.exp(-places * rates)
        total = total + jnp.sum(shaped * shaped, axis=0, keepdims=True)
        filt[start : start + step] = shaped
        turn = start // step
        if turn >= 4 and turn - 4 < pieces:
            first_half(turn - 4)
        if turn >= 6 and turn - 6 < pieces:
            second_half(turn - 6)
    scale = lax.rsqrt(total + norm_eps)
    for start in range(0, filt.shape[0], step):
        filt[start : start + step] = filt[start : start + step] * scale
    for copy in kept + copies:
        copy.wait()
    finish()


def swap_with_filter(value, own, first, last, codes, length):
    count = value.shape[0]
    sizes = axis_sizes()
    rows, width = own.shape
    pieces = 2
    dma = pltpu.SemaphoreType.DMA
    hbm = pl.BlockSpec(memory_space=pltpu.HBM)
    places = np.arange(length, dtype=np.float32)[:, None]
    bands = np.arange(1, (first.shape[0] - 1) // 2 + 1, dtype=np.float32)[None, :]
    angles = (np.float32(2.0 * math.pi / length) * places * bands).astype(np.float32)
    features = np.concatenate([places / np.float32(length), np.cos(angles), np.sin(angles)], axis=1).astype(np.float32)
    return pl.pallas_call(
        functools.partial(swap_filter_kernel, sizes, pieces),
        out_shape=(
            jax.ShapeDtypeStruct(value.shape, value.dtype),
            jax.ShapeDtypeStruct((rows * 2 * sizes[0], width), own.dtype),
            jax.ShapeDtypeStruct((length, last.shape[1]), jnp.float32),
        ),
        in_specs=[hbm] + [VMEM_SPEC] * 5,
        out_specs=(hbm, hbm, VMEM_SPEC),
        scratch_shapes=[dma((count - 1,)), dma((count - 1,)), dma((2,))] + gather_sems(sizes, pieces),
        compiler_params=pltpu.CompilerParams(vmem_limit_bytes=60 * 2**20, collective_id=4, has_side_effects=True),
        cost_estimate=pl.CostEstimate(flops=10**8, bytes_accessed=10 * 10**6, transcendentals=10**6),
        name="swap_with_filter",
    )(value, own, jnp.asarray(features), first, last, codes.reshape(1, -1))


GRAD_TILE = 512


def swap_grads_kernel(value, cot, normed, act, g_up, zero, swapped, d_up, d_down, after, left_t, right, made,
                      swap_send, swap_recv, self_sem, load_sem, store_sem, halo_send, halo_recv):
    count = value.shape[0]
    me, dp = lax.axis_index("seq"), lax.axis_index("dp")
    others = [(dp, lax.rem(me + i, count)) for i in range(1, count)]
    greet(others)
    copies = [
        remote(value.at[device[1]], swapped.at[me], swap_send.at[i], swap_recv.at[count - 2 - i], device)
        for i, device in enumerate(others)
    ]
    for copy in copies:
        copy.start()
    halo = remote(zero.at[:HALO], after, halo_send, halo_recv, others[-1])
    halo.start()
    kept = pltpu.make_async_copy(value.at[me], swapped.at[me], self_sem)
    kept.start()
    for left, source, target in ((cot, act, d_down), (normed, g_up, d_up)):
        tiles = source.shape[1] // GRAD_TILE

        def at(j):
            return pl.ds(pl.multiple_of(j * GRAD_TILE, GRAD_TILE), GRAD_TILE)

        def load(j):
            slot = lax.rem(j, 2)
            return pltpu.make_async_copy(source.at[:, at(j)], right.at[slot], load_sem.at[slot])

        def store(j):
            slot = lax.rem(j, 2)
            return pltpu.make_async_copy(made.at[slot], target.at[:, at(j)], store_sem.at[slot])

        load(jnp.int32(0)).start()
        left_t[...] = left[...].T

        def one(j, carry):
            slot = lax.rem(j, 2)

            @pl.when(j + 1 < tiles)
            def _():
                load(j + 1).start()

            load(j).wait()

            @pl.when(j >= 2)
            def _():
                store(j - 2).wait()

            made[slot] = dot32(left_t[...], right[slot]).astype(jnp.bfloat16)
            store(j).start()
            return carry

        lax.fori_loop(0, tiles, one, 0)
        store(jnp.int32(tiles - 2)).wait()
        store(jnp.int32(tiles - 1)).wait()
    kept.wait()
    halo.wait()
    for copy in copies:
        copy.wait()


def swap_with_grads(value, cot, normed, act, g_up, zero):
    count = value.shape[0]
    rows, width = cot.shape
    hidden = act.shape[1]
    half = jnp.bfloat16
    dma = pltpu.SemaphoreType.DMA
    hbm = pl.BlockSpec(memory_space=pltpu.HBM)
    return pl.pallas_call(
        swap_grads_kernel,
        out_shape=(
            jax.ShapeDtypeStruct(value.shape, value.dtype),
            jax.ShapeDtypeStruct((width, hidden), half),
            jax.ShapeDtypeStruct((width, hidden), half),
            jax.ShapeDtypeStruct((HALO, width), half),
        ),
        in_specs=[hbm, VMEM_SPEC, VMEM_SPEC, hbm, hbm, hbm],
        out_specs=(hbm,) * 4,
        scratch_shapes=[
            pltpu.VMEM((width, rows), half),
            pltpu.VMEM((2, rows, GRAD_TILE), half),
            pltpu.VMEM((2, width, GRAD_TILE), half),
            dma((count - 1,)),
            dma((count - 1,)),
            dma,
            dma((2,)),
            dma((2,)),
            dma,
            dma,
        ],
        compiler_params=pltpu.CompilerParams(vmem_limit_bytes=60 * 2**20, collective_id=6, has_side_effects=True),
        cost_estimate=pl.CostEstimate(flops=4 * rows * width * hidden, bytes_accessed=40 * 10**6, transcendentals=0),
        name="swap_with_grads",
    )(value, cot, normed, act, g_up, zero)


def block_specs(shapes):
    return [pl.BlockSpec(shape, lambda j, n=len(shape): (0,) * n, pipeline_mode=pl.Buffered(1)) for shape in shapes]


def normalized(values):
    center = jnp.mean(values, axis=-1, keepdims=True)
    centred = values - center
    scale = lax.rsqrt(jnp.mean(centred * centred, axis=-1, keepdims=True) + norm_eps)
    return centred * scale, scale


def norm_back(grad, gain, scaled, scale):
    inner = grad * gain
    mean_inner = jnp.mean(inner, axis=-1, keepdims=True)
    mean_scaled = jnp.mean(inner * scaled, axis=-1, keepdims=True)
    return scale * (inner - mean_inner - scaled * mean_scaled)


def dot_cols(left, right):
    return lax.dot_general(left, right, (((1,), (1,)), ((), ())), preferred_element_type=jnp.float32)


LANES = 128
HALO = 8


def project_kernel(tok, before, prev, gain, w_v, w_one, w_zero, t_v, t_one, t_zero,
                   conv_in, factors, zero_out, projs, normed_out, normed, held):
    rows = tok.shape[0]
    keep = prev[0].astype(jnp.float32)

    @pl.when(pl.program_id(0) == 0)
    def _():
        scaled, _ = normalized(before[...].astype(jnp.float32))
        normed[:HALO] = (scaled * gain[...]).astype(jnp.bfloat16)
        for start in range(0, rows, PIECE):
            at = slice(start, start + PIECE)
            scaled, _ = normalized(tok[at].astype(jnp.float32))
            value = (scaled * gain[...]).astype(jnp.bfloat16)
            normed[start + HALO : start + PIECE + HALO] = value
            normed_out[at] = value

    shorts = []
    for i, (w, taps) in enumerate(((w_v, t_v), (w_one, t_one), (w_zero, t_zero))):
        proj = dot32(normed[...], w[...]).astype(jnp.bfloat16)
        projs[i] = proj
        held[...] = proj.astype(jnp.float32)
        held[:HALO] = held[:HALO] * keep
        shorts.append(
            taps[0:1] * held[HALO : HALO + rows]
            + taps[1:2] * held[HALO - 1 : HALO - 1 + rows]
            + taps[2:3] * held[HALO - 2 : HALO - 2 + rows]
        )
    factors[0] = shorts[1]
    factors[1] = shorts[0]
    zero_out[...] = shorts[2]
    product = (shorts[0] * shorts[1]).astype(jnp.bfloat16)
    for i in range(conv_in.shape[0]):
        conv_in[i] = product[:, i * LANES : (i + 1) * LANES]


def project(tok, before, has_prev, gain, w_in, taps):
    rows, width = tok.shape
    size = 256
    steps = width // size
    col = lambda part: (lambda j: (0, part * steps + j))
    parts = [pl.BlockSpec((width, size), col(i)) for i in range(3)]
    tap_parts = [pl.BlockSpec((3, size), col(i)) for i in range(3)]
    wide = lambda n, dtype: jax.ShapeDtypeStruct((n, width), dtype)
    stack = lambda m, n: pl.BlockSpec((m, n, size), lambda j: (0, 0, j))
    return pl.pallas_call(
        project_kernel,
        grid=(steps,),
        out_shape=[jax.ShapeDtypeStruct((width // LANES, rows, LANES), jnp.bfloat16)]
        + [jax.ShapeDtypeStruct((2, rows, width), jnp.float32), wide(rows, jnp.float32)]
        + [jax.ShapeDtypeStruct((3, rows + HALO, width), jnp.bfloat16), wide(rows, jnp.bfloat16)],
        in_specs=block_specs([(rows, width), (HALO, width)]) + [SMEM_SPEC] + block_specs([(1, width)]) + parts + tap_parts,
        out_specs=[pl.BlockSpec((size // LANES, rows, LANES), lambda j: (j, 0, 0))]
        + [stack(2, rows), pl.BlockSpec((rows, size), lambda j: (0, j)), stack(3, rows + HALO)]
        + block_specs([(rows, width)]),
        scratch_shapes=[pltpu.VMEM((rows + HALO, width), jnp.bfloat16), pltpu.VMEM((rows + HALO, size), jnp.float32)],
        compiler_params=pltpu.CompilerParams(vmem_limit_bytes=60 * 2**20),
        cost_estimate=pl.CostEstimate(flops=6 * rows * width * width, bytes_accessed=20 * 10**6, transcendentals=0),
        name="project",
    )(tok, before, has_prev, gain, w_in, w_in, w_in, taps, taps, taps)


def mlp_kernel(conv, conv_in, zero, tok, cot, skip, gain, w_out, w_up, w_down,
               output, act_out, up_out, gated, normed, d_resid, branch_out, conv_grad, d_mixed, d_zero, d_gain, d_skip,
               resid, down, d_normed):
    rows, width = tok.shape
    groups = width // LANES
    step = pl.program_id(0)

    @pl.when(step == 0)
    def _():
        for g in range(groups):
            at = slice(g * LANES, (g + 1) * LANES)
            mixed = conv[g].astype(jnp.float32) + skip[:, at] * conv_in[g].astype(jnp.float32)
            gated[:, at] = (zero[:, at] * mixed).astype(jnp.bfloat16)
        resid[...] = tok[...].astype(jnp.float32) + dot_cols(gated[...], w_out[...])
        for start in range(0, rows, PIECE):
            at = slice(start, start + PIECE)
            scaled, _ = normalized(resid[at])
            normed[at] = (scaled * gain[...]).astype(jnp.bfloat16)

    up = dot32(normed[...], w_up[...])
    d_act = dot32(cot[...], w_down[...])
    root = math.sqrt(2.0 / math.pi)
    square = up * up
    bent = jnp.tanh(root * up * (1.0 + 0.044715 * square))
    act = (0.5 * up * (1.0 + bent)).astype(jnp.bfloat16)
    slope = 0.5 * (1.0 + bent) + (0.5 * root) * up * (1.0 - bent * bent) * (1.0 + (3.0 * 0.044715) * square)
    g_up = (slope * d_act).astype(jnp.bfloat16)
    act_out[...] = act
    up_out[...] = g_up
    down_part = dot_cols(act, w_down[...])
    normed_part = dot_cols(g_up, w_up[...])

    @pl.when(step == 0)
    def _():
        down[...] = down_part
        d_normed[...] = normed_part

    @pl.when(step > 0)
    def _():
        down[...] += down_part
        d_normed[...] += normed_part

    @pl.when(step == pl.num_programs(0) - 1)
    def _():
        gain_sum = jnp.zeros((1, width), jnp.float32)
        for start in range(0, rows, PIECE):
            at = slice(start, start + PIECE)
            output[at] = (resid[at] + down[at]).astype(jnp.bfloat16)
            scaled, scale = normalized(resid[at])
            grad = d_normed[at]
            gain_sum = gain_sum + jnp.sum(grad * scaled, axis=0, keepdims=True)
            total = cot[at].astype(jnp.float32) + norm_back(grad, gain[...], scaled, scale)
            d_resid[at] = total
            branch_out[at] = total.astype(jnp.bfloat16)
        d_gain[...] = gain_sum
        down[...] = dot32(branch_out[...], w_out[...])
        for g in range(groups):
            at = slice(g * LANES, (g + 1) * LANES)
            source = conv_in[g].astype(jnp.float32)
            mixed = conv[g].astype(jnp.float32) + skip[:, at] * source
            d_gated = down[:, at]
            d_zero[:, at] = (d_gated * mixed).astype(jnp.bfloat16)
            grad = d_gated * zero[:, at]
            d_mixed[g] = grad
            conv_grad[g] = grad.astype(jnp.bfloat16)
            d_skip[:, at] = jnp.sum(grad * source, axis=0, keepdims=True)


def mlp_block(conv, conv_in, zero, tok, cot, skip, gain, w_out, w_up, w_down):
    rows, width = tok.shape
    hidden = w_down.shape[1]
    size = 512
    steps = hidden // size
    groups = width // LANES
    flat = lambda dtype: jax.ShapeDtypeStruct((rows, width), dtype)
    cut = lambda dtype: jax.ShapeDtypeStruct((groups, rows, LANES), dtype)
    row = jax.ShapeDtypeStruct((1, width), jnp.float32)
    big = jax.ShapeDtypeStruct((rows, hidden), jnp.bfloat16)
    half, full = jnp.bfloat16, jnp.float32
    ends = [flat(half), flat(half), flat(full), flat(half), cut(half), cut(full), flat(half), row, row]
    tile = pl.BlockSpec((rows, size), lambda j: (0, j))
    one = block_specs([(rows, width)])
    return pl.pallas_call(
        mlp_kernel,
        grid=(steps,),
        out_shape=[flat(half), big, big] + ends,
        in_specs=block_specs([conv.shape, conv.shape, zero.shape, tok.shape, cot.shape, (1, width), (1, width), w_out.shape])
        + [pl.BlockSpec((width, size), index) for index in (lambda j: (0, j),) * 2],
        out_specs=one + [tile, tile] + block_specs([e.shape for e in ends]),
        scratch_shapes=[pltpu.VMEM((rows, width), full)] * 3,
        compiler_params=pltpu.CompilerParams(vmem_limit_bytes=60 * 2**20),
        cost_estimate=pl.CostEstimate(flops=8 * rows * width * hidden + 4 * rows * width * width, bytes_accessed=50 * 10**6, transcendentals=rows * hidden),
        name="mlp_block",
    )(conv, conv_in, zero, tok, cot, skip, gain, w_out, w_up, w_down)


def shifted_back(held, wide_proj, after, taps, proj, prev, nxt, d_taps):
    rows = held.shape[0] - HALO
    held[rows:] = after[...].astype(jnp.float32) * nxt[0].astype(jnp.float32)
    g_proj = (
        taps[0:1] * held[:rows] + taps[1:2] * held[1 : rows + 1] + taps[2:3] * held[2 : rows + 2]
    ).astype(jnp.bfloat16)
    wide_proj[...] = proj[...].astype(jnp.float32)
    wide_proj[:HALO] = wide_proj[:HALO] * prev[0].astype(jnp.float32)
    d_taps[...] = jnp.concatenate(
        [jnp.sum(held[:rows] * wide_proj[HALO - i : HALO - i + rows], axis=0, keepdims=True) for i in range(3)], axis=0
    )
    return g_proj


def back_early_kernel(d_zero, proj, after, prev, nxt, taps, w_in, normed, branch, gated,
                      d_mixer, d_taps, d_normed, normed_t, branch_t, held, wide_proj):
    rows = normed.shape[0]
    step = pl.program_id(0)
    per = pl.num_programs(0) // 2

    @pl.when(step == 0)
    def _():
        d_normed[...] = jnp.zeros_like(d_normed)
        normed_t[...] = normed[...].T
        branch_t[...] = branch[...].T

    @pl.when(step < per)
    def _():
        held[:rows] = d_zero[...].astype(jnp.float32)
        g_proj = shifted_back(held, wide_proj, after, taps, proj, prev, nxt, d_taps)
        d_normed[...] += dot_cols(g_proj, w_in[...])
        d_mixer[...] = dot32(normed_t[...], g_proj).astype(jnp.bfloat16)

    @pl.when(step >= per)
    def _():
        d_mixer[...] = dot32(branch_t[...], gated[...]).astype(jnp.bfloat16)


def project_back_early(d_zero, projs, after, has_prev, has_next, taps, w_in, normed, branch, gated):
    rows, width = normed.shape
    size = 512
    per = width // size
    half = jnp.bfloat16
    inner = lambda j: jnp.minimum(j, per - 1)
    third = lambda n: pl.BlockSpec((n, size), lambda j: (0, 2 * per + inner(j)))
    tile = lambda n: pl.BlockSpec((n, size), lambda j: (0, inner(j)))
    return pl.pallas_call(
        back_early_kernel,
        grid=(2 * per,),
        out_shape=[
            jax.ShapeDtypeStruct((width, 4 * width), half),
            jax.ShapeDtypeStruct((3, width), jnp.float32),
            jax.ShapeDtypeStruct((rows, width), jnp.float32),
        ],
        in_specs=[tile(rows), pl.BlockSpec((None, rows + HALO, size), lambda j: (2, 0, inner(j))), tile(HALO)]
        + [SMEM_SPEC, SMEM_SPEC, third(3), third(width)]
        + block_specs([(rows, width)] * 2)
        + [pl.BlockSpec((rows, size), lambda j: (0, jnp.maximum(j - per, 0)))],
        out_specs=[pl.BlockSpec((width, size), lambda j: (0, 2 * per + j)), tile(3)] + block_specs([(rows, width)]),
        scratch_shapes=[
            pltpu.VMEM((width, rows), half),
            pltpu.VMEM((width, rows), half),
            pltpu.VMEM((rows + HALO, size), jnp.float32),
            pltpu.VMEM((rows + HALO, size), jnp.float32),
        ],
        compiler_params=pltpu.CompilerParams(vmem_limit_bytes=60 * 2**20),
        cost_estimate=pl.CostEstimate(flops=6 * rows * width * width, bytes_accessed=20 * 10**6, transcendentals=0),
        name="project_back_early",
    )(d_zero, projs, after, has_prev, has_next, taps, w_in, normed, branch, gated)


def back_late_kernel(begun, back, d_mixed, other, proj, after, prev, nxt, skip, taps, w_in, normed, tok, d_resid, gain, start,
                     d_mixer, d_taps, tokens_grad, d_gain, normed_t, d_normed, held, wide_proj):
    rows = tok.shape[0]
    step = pl.program_id(0)

    @pl.when(step == 0)
    def _():
        d_normed[...] = start[...]
        normed_t[...] = normed[...].T

    def spread(ref):
        return jnp.concatenate([ref[i].astype(jnp.float32) for i in range(ref.shape[0])], axis=1)

    d_conv_in = skip[...] * spread(d_mixed) + spread(back)
    held[:rows] = (d_conv_in * other[...]).astype(jnp.bfloat16).astype(jnp.float32)
    g_proj = shifted_back(held, wide_proj, after, taps, proj, prev, nxt, d_taps)
    d_normed[...] += dot_cols(g_proj, w_in[...])
    d_mixer[...] = dot32(normed_t[...], g_proj).astype(jnp.bfloat16)

    @pl.when(step == pl.num_programs(0) - 1)
    def _():
        gain_sum = jnp.zeros((1, tok.shape[1]), jnp.float32)
        for first in range(0, rows, PIECE):
            at = slice(first, first + PIECE)
            scaled, scale = normalized(tok[at].astype(jnp.float32))
            grad = d_normed[at]
            gain_sum = gain_sum + jnp.sum(grad * scaled, axis=0, keepdims=True)
            tokens_grad[at] = (d_resid[at] + norm_back(grad, gain[...], scaled, scale)).astype(jnp.bfloat16)
        d_gain[...] = gain_sum


def project_back_late(begun, back, d_mixed, factors, projs, after, has_prev, has_next, skip, taps, w_in, normed, tok, d_resid, gain, start):
    rows, width = tok.shape
    size = 512
    per = width // size
    half = jnp.bfloat16
    lane = lambda j: j // 2
    part = lambda j: lax.rem(j, 2)
    place = lambda j: part(j) * per + lane(j)
    group = pl.BlockSpec((size // LANES, rows, LANES), lambda j: (lane(j), 0, 0))
    third = lambda n: pl.BlockSpec((n, size), lambda j: (0, place(j)))
    return pl.pallas_call(
        back_late_kernel,
        grid=(2 * per,),
        out_shape=[
            jax.ShapeDtypeStruct(begun.shape, half),
            jax.ShapeDtypeStruct((3, 2 * width), jnp.float32),
            jax.ShapeDtypeStruct((rows, width), half),
            jax.ShapeDtypeStruct((1, width), jnp.float32),
        ],
        in_specs=[pl.BlockSpec(memory_space=pl.ANY), group, group]
        + [pl.BlockSpec((None, rows, size), lambda j: (part(j), 0, lane(j)))]
        + [pl.BlockSpec((None, rows + HALO, size), lambda j: (part(j), 0, lane(j)))]
        + [third(HALO), SMEM_SPEC, SMEM_SPEC, pl.BlockSpec((1, size), lambda j: (0, lane(j))), third(3), third(width)]
        + block_specs([(rows, width)] * 3 + [(1, width), (rows, width)]),
        out_specs=[pl.BlockSpec((width, size), lambda j: (0, place(j))), third(3)] + block_specs([(rows, width), (1, width)]),
        scratch_shapes=[
            pltpu.VMEM((width, rows), half),
            pltpu.VMEM((rows, width), jnp.float32),
            pltpu.VMEM((rows + HALO, size), jnp.float32),
            pltpu.VMEM((rows + HALO, size), jnp.float32),
        ],
        input_output_aliases={0: 0},
        compiler_params=pltpu.CompilerParams(vmem_limit_bytes=60 * 2**20),
        cost_estimate=pl.CostEstimate(flops=8 * rows * width * width, bytes_accessed=30 * 10**6, transcendentals=0),
        name="project_back_late",
    )(begun, back, d_mixed, factors, projs, after, has_prev, has_next, skip, taps, w_in, normed, tok, d_resid, gain, start)


def adam_update(master, moment, square, grad, factor, rate, decay):
    clipped = grad * factor
    moment_new = beta_one * moment + (1.0 - beta_one) * clipped
    square_new = beta_two * square + (1.0 - beta_two) * clipped * clipped
    moment_hat = moment_new / (1.0 - beta_one**ADAM_STEP)
    square_hat = square_new / (1.0 - beta_two**ADAM_STEP)
    master_new = master - rate * (moment_hat / (jnp.sqrt(square_hat) + adam_eps) + decay * master)
    return (master_new, moment_new, square_new)


def on_device(
    tokens,
    cotangent,
    seq_first,
    decay_code,
    mixer_master,
    mixer_moment,
    mixer_square,
    mlp_master,
    mlp_moment,
    mlp_square,
    channel_master,
    channel_moment,
    channel_square,
    filter_in_master,
    filter_in_moment,
    filter_in_square,
    filter_out_master,
    filter_out_moment,
    filter_out_square,
):
    block_rows = tokens.shape[1]
    model_width = tokens.shape[2]
    lane_count = 3 * model_width
    per = block_rows // PIECE
    seq_count = lax.axis_size("seq")
    long_blocks = max(seq_count // 4, 4)
    length = long_blocks * block_rows
    own_width = model_width // seq_count
    seq_index = lax.axis_index("seq")
    w_in, out_own, up_own, down_own, before, first_tiles = open_gather(
        mixer_master, mlp_master, tokens[0], seq_first, seq_count
    )
    firsts = first_tiles[:, 0, 0]
    w_down = lax.all_gather(down_own, "dp", axis=0, tiled=True)
    blocks = jnp.arange(seq_count, dtype=jnp.int32)
    same = firsts[None, :] == firsts[:, None]
    lasts = jnp.max(jnp.where(same, blocks[None, :], 0), axis=1).astype(jnp.int32)
    own_first = firsts[seq_index]
    has_prev = (seq_index - own_first >= 1).astype(jnp.int32).reshape(1)
    has_next = (lasts[seq_index] > seq_index).astype(jnp.int32).reshape(1)
    conv_taps = channel_master[:, :lane_count]
    gain_one = channel_master[0:1, lane_count:]
    gain_two = channel_master[1:2, lane_count:]
    skip_gain = channel_master[2:3, lane_count:]
    own_codes = lax.dynamic_slice_in_dim(decay_code, seq_index * own_width, own_width, 0)
    own_last = lax.dynamic_slice_in_dim(filter_out_master, seq_index * own_width, own_width, 1)
    conv_input, factors, x_zero, projs, normed_b = project(tokens[0], before, has_prev, gain_one, w_in, conv_taps)
    swapped, w_out, filt = swap_with_filter(
        channel_order(conv_input, seq_count), out_own, filter_in_master, own_last, own_codes, length
    )
    pieces = swapped.reshape(seq_count * per, PIECE, own_width)
    conv_out = conv_forward(firsts, pieces, filt, per)
    conv, w_up = swap_with_rows(conv_out.reshape(seq_count, block_rows, own_width), up_own, 5)
    conv = lane_order(conv)
    (
        output, act_b, grad_up_b, gated_b, normed_two_b, d_resid, grad_branch_b, conv_grad, d_mixed, d_x_zero, d_gain_two, d_skip,
    ) = mlp_block(conv, conv_input, x_zero, tokens[0], cotangent[0], skip_gain, gain_two, w_out, w_up, w_down)
    swapped_grad, up_grad_b, down_grad_b, after_zero = swap_with_grads(
        channel_order(conv_grad, seq_count), cotangent[0], normed_two_b, act_b, grad_up_b, d_x_zero
    )
    grad_pieces = swapped_grad.reshape(seq_count * per, PIECE, own_width)
    mixer_begun, d_taps_high, d_normed_begun = project_back_early(
        d_x_zero, projs, after_zero, has_prev, has_next, conv_taps, w_in, normed_b, grad_branch_b, gated_b
    )
    conv_in_grad, filt_grad = conv_backward(firsts, lasts, pieces, grad_pieces, filt, per)
    back = to_tokens(conv_in_grad.reshape(seq_count, block_rows, own_width))
    _, filter_pull = jax.vjp(
        lambda first, last: make_filter(first, last, own_codes, length), filter_in_master, own_last
    )
    first_grad, own_last_grad = filter_pull(filt_grad)
    back, mixer_begun, d_taps_high, d_normed_begun, first_grad, own_last_grad = lax.optimization_barrier(
        (back, mixer_begun, d_taps_high, d_normed_begun, first_grad, own_last_grad)
    )
    head_grad = skip_gain.reshape(-1, 1, LANES) * d_mixed[:, :HALO] + back[:, :HALO].astype(jnp.float32)
    head_grad = head_grad.transpose(1, 0, 2).reshape(HALO, model_width)
    head = [head_grad * factors[0, :HALO], head_grad * factors[1, :HALO]]
    after = passed_along(jnp.concatenate(head, axis=1).astype(jnp.bfloat16), "seq", -1)
    last_grad = lax.dynamic_update_slice_in_dim(
        jnp.zeros_like(filter_out_master), own_last_grad, seq_index * own_width, 1
    )
    mixer_grad_b, d_taps_low, tokens_grad, d_gain_one = project_back_late(
        mixer_begun, back, d_mixed, factors, projs, after, has_prev, has_next, skip_gain, conv_taps, w_in,
        normed_b, tokens[0], d_resid, gain_one, d_normed_begun,
    )
    d_taps = jnp.concatenate([d_taps_low, d_taps_high], axis=1)
    vectors = jnp.concatenate([d_gain_one, d_gain_two, d_skip], axis=0)
    channel_grad = jnp.concatenate([d_taps, vectors], axis=1)
    small_parts = (channel_grad, first_grad, last_grad)
    large_grads, small_sum, total = grad_sum(
        up_grad_b, down_grad_b, mixer_grad_b, jnp.concatenate([part.reshape(-1) for part in small_parts])
    )
    mlp_grad = large_grads[:2].astype(jnp.float32)
    mixer_grad = large_grads[2].astype(jnp.float32)
    ends = np.cumsum([part.size for part in small_parts])
    channel_grad, first_grad, last_grad = (
        small_sum[end - part.size : end].reshape(part.shape) for part, end in zip(small_parts, ends)
    )
    grad_norm = jnp.sqrt(total)
    factor = jnp.minimum(1.0, clip_limit / (grad_norm + 1e-06))
    mixer_new, mixer_moment_new, mixer_square_new = adam_update(
        mixer_master, mixer_moment, mixer_square, mixer_grad, factor, rate_matrix, weight_decay
    )
    mlp_new, mlp_moment_new, mlp_square_new = adam_update(
        mlp_master, mlp_moment, mlp_square, mlp_grad, factor, rate_matrix, weight_decay
    )
    channel_new, channel_moment_new, channel_square_new = adam_update(
        channel_master, channel_moment, channel_square, channel_grad, factor, rate_small, 0.0
    )
    filter_in_new, filter_in_moment_new, filter_in_square_new = adam_update(
        filter_in_master,
        filter_in_moment,
        filter_in_square,
        first_grad,
        factor,
        rate_small,
        weight_decay,
    )
    filter_out_new, filter_out_moment_new, filter_out_square_new = adam_update(
        filter_out_master,
        filter_out_moment,
        filter_out_square,
        last_grad,
        factor,
        rate_small,
        weight_decay,
    )
    return (
        output[None],
        tokens_grad[None],
        grad_norm.reshape(1),
        channel_grad,
        first_grad,
        last_grad,
        mixer_new,
        mixer_moment_new,
        mixer_square_new,
        mlp_new,
        mlp_moment_new,
        mlp_square_new,
        channel_new,
        channel_moment_new,
        channel_square_new,
        filter_in_new,
        filter_in_moment_new,
        filter_in_square_new,
        filter_out_new,
        filter_out_moment_new,
        filter_out_square_new,
    )


def solution(mesh):
    in_specs = (
        P("dp", "seq", None),
        P("dp", "seq", None),
        P("dp", "seq"),
        P(),
        P("dp", None),
        P("dp", None),
        P("dp", None),
        P(None, "dp", None),
        P(None, "dp", None),
        P(None, "dp", None),
        P(),
        P(),
        P(),
        P(),
        P(),
        P(),
        P(),
        P(),
        P(),
    )
    out_specs = (
        P("dp", "seq", None),
        P("dp", "seq", None),
        P(),
        P(),
        P(),
        P(),
        P("dp", None),
        P("dp", None),
        P("dp", None),
        P(None, "dp", None),
        P(None, "dp", None),
        P(None, "dp", None),
        P(),
        P(),
        P(),
        P(),
        P(),
        P(),
        P(),
        P(),
        P(),
    )
    return jax.shard_map(
        on_device, mesh=mesh, in_specs=in_specs, out_specs=out_specs, check_vma=False
    )
```
